32 devices in a mesh: band: 16 (over z, y, x), head: 2 (over core).
Axes of the slice: x: 2, y: 2, z: 4, core: 2. Of those that a mesh axis runs over, the one named last changes fastest.
Arguments:
- pixels: bfloat16 [16, 16, 196, 256], P(None, 'band'), may hold values from -6 to 6
- band_mask: int32 [16, 16], replicated, may hold values 0 or 1
- wave_ids: int32 [16, 1], replicated, may hold values from 0 to 15
- pos_embed: bfloat16 [196, 768], replicated, may hold values from -3 to 3
- in_proj: bfloat16 [3, 768, 768], P(None, None, 'head'), may hold values from -0.21875 to 0.21875
- out_proj: bfloat16 [768, 768], P('head'), may hold values from -0.4375 to 0.4375
- up_proj: bfloat16 [768, 3072], P(None, 'head'), may hold values from -0.21875 to 0.21875
- down_proj: bfloat16 [3072, 768], P('head'), may hold values from -0.109375 to 0.109375
- gain_one: bfloat16 [768], replicated, may hold values from 0.5 to 1.5
- gain_two: bfloat16 [768], replicated, may hold values from 0.5 to 1.5
- kernel_gen: bfloat16 [128, 256, 768], P(None, 'band', 'head'), may hold values from -0.01171875 to 0.01171875
- bias_gen: bfloat16 [128, 768], P(None, 'head'), may hold values from -0.1875 to 0.1875
- wave_table: float32 [16, 128], replicated, may hold values from -6 to 6
- hyper_in: float32 [128, 384], replicated, may hold values from -0.5 to 0.5
- hyper_out: float32 [128, 128], replicated, may hold values from -0.5 to 0.5
- hyper_up: float32 [128, 2048], replicated, may hold values from -0.5 to 0.5
- hyper_down: float32 [2048, 128], replicated, may hold values from -0.125 to 0.125
- hyper_gain_one: float32 [128], replicated, may hold values from 0.5 to 1.5
- hyper_gain_two: float32 [128], replicated, may hold values from 0.5 to 1.5
- cotangent: bfloat16 [16, 196, 768], P('band'), may hold values from -6 to 6
Outputs:
- layer_out: bfloat16 [16, 196, 768], P('band')
- grad_pixels: bfloat16 [16, 16, 196, 256], P('head', 'band')
- grad_pos: float32 [196, 768], P(None, 'band')
- grad_in_proj: float32 [3, 768, 768], P(None, 'band', 'head')
- grad_out_proj: float32 [768, 768], P('head', 'band')
- grad_up_proj: float32 [768, 3072], P('band', 'head')
- grad_down_proj: float32 [3072, 768], P('head', 'band')
- grad_gain_one: float32 [768], P('band')
- grad_gain_two: float32 [768], P('band')
- grad_kernel_gen: float32 [128, 256, 768], P(None, 'band', 'head')
- grad_bias_gen: float32 [128, 768], P(None, 'head')
- grad_wave_table: float32 [16, 128], replicated
- grad_hyper_in: float32 [128, 384], replicated
- grad_hyper_out: float32 [128, 128], replicated
- grad_hyper_up: float32 [128, 2048], replicated
- grad_hyper_down: float32 [2048, 128], replicated
- grad_hyper_gain_one: float32 [128], replicated
- grad_hyper_gain_two: float32 [128], replicated
The draws below stay inside these ranges and needn't reach their ends.
Inputs may be any that keep to these rules, and one draw needn't show every extreme that they name: `wave_ids`: every wavelength from 0 to 15 is the wavelength of some band slot.
All inputs are finite; a program needn't handle non-finite values.
Results may differ from the reference program's by a relative error of at most 0.015.
Values may be sent and summed in bfloat16 or wider, within the bound.
No kernel may reach another device: no remote copies, remote signals or barrier semaphores. Data moves between devices by JAX's collectives and lax.ppermute only.
A program may use at most 256 MiB of HBM per device.

```python
import jax
import jax.numpy as jnp
from jax import lax

D = 768
HEADS = 12
HS = 64
FF = 3072
NP = 196
PIX = 256
HD = 128
HHEADS = 4
HFF = 2048
WL = 16
IMG = 16
SLOTS = 16


def with_ends(drawn, stream_key, low, largest):
    spot = [jax.random.randint(jax.random.fold_in(stream_key, axis), (), 0, length) for axis, length in enumerate(drawn.shape)]
    main_axis = drawn.shape.index(max(drawn.shape))
    beside = spot[:main_axis] + [(spot[main_axis] + 1) % drawn.shape[main_axis]] + spot[main_axis + 1:]
    return drawn.at[tuple(spot)].set(low).at[tuple(beside)].set(largest)


def spiked(values, stream_key, source, target, parts, factor):
    def block_of(position):
        return (jnp.arange(values.shape[position]) // (values.shape[position] // parts)).reshape((-1,) + (1,) * (values.ndim - 1 - position))

    near = jax.random.permutation(stream_key, parts)[block_of(target)]
    other_side = (block_of(target) + parts // 2) % parts
    return jnp.where((block_of(source) == near) | (block_of(source) == other_side), factor * values, values)


def steps_of(rng, shape, pieces, least, high):
    def one(position, shards_of):
        draws = jax.random.uniform(jax.random.fold_in(jax.random.fold_in(rng, 6), position), (shards_of,), jnp.float32, least / len(pieces), high / len(pieces))
        return jnp.repeat(jnp.exp(draws), shape[position] // shards_of).reshape((-1,) + (1,) * (len(shape) - position - 1))

    gain = one(*pieces[0])
    for cut in pieces[1:]:
        gain = gain * one(*cut)
    return gain


def choose_distinct(stream_key, rows, number_of, top, lift):
    ranking = jax.random.permutation(jax.random.fold_in(stream_key, 1), number_of)
    boost = ranking
    for power in range(3):
        boost = boost * boost // number_of
    boost = boost * lift // number_of
    tickets = jax.random.randint(jax.random.fold_in(stream_key, 2), (rows, number_of), 0, 4096) + boost
    fixed_rows = jax.random.permutation(jax.random.fold_in(stream_key, 3), rows)[jnp.arange(number_of) % rows]
    tickets = jnp.where(jnp.arange(rows)[:, None] == fixed_rows[None, :], 1 << 14, tickets)
    priority = tickets * number_of + jnp.arange(number_of)
    return lax.top_k(priority.astype(jnp.int32), top)[1].astype(jnp.int32)


def noise(own_key, dims, scale, reach, split=(), kind=jnp.bfloat16):
    values = jax.random.normal(own_key, dims, jnp.float32) * scale
    if len(split) > 0:
        values = steps_of(own_key, dims, split, -0.22, 0.18) * values
    return jnp.clip(values, min=-reach, max=reach).astype(kind)


def noise_with(rng, shape, deviation, limit, cuts, heavy, kind=jnp.bfloat16):
    values = deviation * jax.random.normal(rng, shape, jnp.float32)
    if cuts:
        values = values * steps_of(rng, shape, cuts, -0.22, 0.18)
    return jnp.clip(spiked(values, jax.random.fold_in(rng, 3), *heavy), -limit, limit).astype(kind)


def setup_inputs(seed: int = 0) -> dict:
    key_list = jax.random.split(jax.random.key(seed), 21)
    return {
        "pixels": noise_with(key_list[0], (IMG, SLOTS, NP, PIX), 1.0, 6.0, ((1, 16),), (1, 0, 16, 2.0)),
        "band_mask": with_ends((jax.random.randint(key_list[1], (IMG, SLOTS), 0, 2) < 1).astype(jnp.int32), jax.random.fold_in(key_list[1], 1), 0, 1),
        "wave_ids": choose_distinct(key_list[2], SLOTS, WL, 1, 512),
        "pos_embed": noise(key_list[3], (NP, D), 0.5, 3.0),
        "in_proj": noise(key_list[4], (3, D, D), D ** -0.5, 0.21875, ((2, 2),)),
        "out_proj": noise(key_list[5], (D, D), (D // 4) ** -0.5, 0.4375, ((0, 2),)),
        "up_proj": noise(key_list[6], (D, FF), D ** -0.5, 0.21875, ((1, 2),)),
        "down_proj": noise(key_list[7], (FF, D), FF ** -0.5, 0.109375, ((0, 2),)),
        "gain_one": jnp.clip(1.0 + 0.1 * jax.random.normal(key_list[8], (D,), jnp.float32), 0.5, 1.5).astype(jnp.bfloat16),
        "gain_two": jnp.clip(1.0 + 0.1 * jax.random.normal(key_list[9], (D,), jnp.float32), 0.5, 1.5).astype(jnp.bfloat16),
        "kernel_gen": noise(key_list[10], (HD, PIX, D), (HD * PIX * SLOTS // 2) ** -0.5, 0.01171875, ((1, 16), (2, 2))),
        "bias_gen": noise(key_list[11], (HD, D), (HD * SLOTS // 2) ** -0.5, 0.1875, ((1, 2),)),
        "wave_table": noise(key_list[12], (WL, HD), 1.0, 6.0, (), jnp.float32),
        "hyper_in": noise(key_list[13], (HD, 3 * HD), HD ** -0.5, 0.5, (), jnp.float32),
        "hyper_out": noise(key_list[14], (HD, HD), HD ** -0.5, 0.5, (), jnp.float32),
        "hyper_up": noise(key_list[15], (HD, HFF), HD ** -0.5, 0.5, (), jnp.float32),
        "hyper_down": noise(key_list[16], (HFF, HD), HFF ** -0.5, 0.125, (), jnp.float32),
        "hyper_gain_one": jnp.clip(1.0 + 0.1 * jax.random.normal(key_list[17], (HD,), jnp.float32), 0.5, 1.5),
        "hyper_gain_two": jnp.clip(1.0 + 0.1 * jax.random.normal(key_list[18], (HD,), jnp.float32), 0.5, 1.5),
        "cotangent": noise(key_list[19], (IMG, NP, D), 1.0, 6.0, ((0, 16),)),
    }


highest = lax.Precision.HIGHEST
norm_epsilon = 1e-06
score_scale = 0.125

@jax.custom_vjp
def low(v):
    return lax.optimization_barrier(v.astype(jnp.bfloat16)).astype(jnp.float32)

@jax.custom_vjp
def low_back(v):
    return v

def low_keep(v):
    return (low(v), None)

def low_pass(kept, grad):
    return (grad,)

def back_keep(v):
    return (v, None)

def back_low(kept, grad):
    return (low(grad),)
low.defvjp(low_keep, low_pass)
low_back.defvjp(back_keep, back_low)

def layer_norm(values, gain_vec):
    row_mean = lax.optimization_barrier(jnp.mean(values, axis=-1, keepdims=True))
    centered = values - row_mean
    variance = lax.optimization_barrier(jnp.mean(centered * centered, axis=-1, keepdims=True))
    return centered * lax.rsqrt(variance + norm_epsilon) * gain_vec

def gelu_exact(values):
    return jax.nn.gelu(values, approximate=False)

def hyper(wave_table, hyper_in, hyper_out, hyper_up, hyper_down, hyper_gain_one, hyper_gain_two):
    wave_count, hyper_width = wave_table.shape
    head_size = hyper_width // HHEADS
    projected = jnp.dot(wave_table, hyper_in, precision=highest).reshape(wave_count, 3, HHEADS, head_size)
    scores = jnp.einsum('qhe,khe->hqk', projected[:, 0], projected[:, 1], precision=highest) * head_size ** (-0.5)
    weights = jax.nn.softmax(scores, axis=-1)
    attended = jnp.einsum('hqk,khe->qhe', weights, projected[:, 2], precision=highest).reshape(wave_count, hyper_width)
    first_out = layer_norm(wave_table + jnp.dot(attended, hyper_out, precision=highest), hyper_gain_one)
    inner_act = gelu_exact(jnp.dot(first_out, hyper_up, precision=highest))
    return layer_norm(first_out + jnp.dot(inner_act, hyper_down, precision=highest), hyper_gain_two)

def forward(pixels, pos_embed, in_proj, out_proj, up_proj, down_proj, gain_one, gain_two, kernel_gen, bias_gen, wave_table, hyper_in, hyper_out, hyper_up, hyper_down, hyper_gain_one, hyper_gain_two, mask_float, onehot):
    mixture = hyper(wave_table, hyper_in, hyper_out, hyper_up, hyper_down, hyper_gain_one, hyper_gain_two)
    mix_low = low(mixture)
    kernels = low(low_back(jnp.einsum('wh,hpd->wpd', mix_low, kernel_gen, precision=highest)))
    wave_bias = jnp.dot(mix_low, bias_gen, precision=highest)
    slot_kernels = jnp.einsum('sw,wpd->spd', onehot, kernels, precision=highest)
    slot_bias = jnp.dot(onehot, wave_bias, precision=highest)
    masked = pixels * mask_float[:, :, None, None]
    embed = jnp.einsum('isnp,spd->ind', masked, slot_kernels, precision=highest)
    embed = embed + jnp.dot(mask_float, slot_bias, precision=highest)[:, None, :]
    embed = low_back(embed)
    tokens = (embed + pos_embed[None]).reshape(IMG * NP, D)
    normed_low = low(layer_norm(tokens, gain_one))
    projected = low_back(low(jnp.einsum('rd,jde->jre', normed_low, in_proj, precision=highest)))
    query_rows = projected[0].reshape(IMG, NP, HEADS, HS)
    key_rows = projected[1].reshape(IMG, NP, HEADS, HS)
    value_rows = projected[2].reshape(IMG, NP, HEADS, HS)
    scores = low_back(jnp.einsum('iqhe,ikhe->ihqk', query_rows, key_rows, precision=highest) * score_scale)
    probs_low = low(jax.nn.softmax(scores, axis=-1))
    attended = jnp.einsum('ihqk,ikhe->iqhe', probs_low, value_rows, precision=highest).reshape(IMG * NP, D)
    attended = low_back(low(attended))
    mid_stream = tokens + low_back(jnp.dot(attended, out_proj, precision=highest))
    second_low = low(layer_norm(mid_stream, gain_two))
    hidden = low_back(jnp.dot(second_low, up_proj, precision=highest))
    active_low = low(gelu_exact(hidden))
    return mid_stream + low_back(jnp.dot(active_low, down_proj, precision=highest))

def reference(pixels, band_mask, wave_ids, pos_embed, in_proj, out_proj, up_proj, down_proj, gain_one, gain_two, kernel_gen, bias_gen, wave_table, hyper_in, hyper_out, hyper_up, hyper_down, hyper_gain_one, hyper_gain_two, cotangent):
    mask_float = band_mask.astype(jnp.float32)
    onehot = (wave_ids[:, 0][:, None] == jnp.arange(WL, dtype=jnp.int32)[None, :]).astype(jnp.float32)
    params = tuple((argument.astype(jnp.float32) for argument in (pixels, pos_embed, in_proj, out_proj, up_proj, down_proj, gain_one, gain_two, kernel_gen, bias_gen, wave_table, hyper_in, hyper_out, hyper_up, hyper_down, hyper_gain_one, hyper_gain_two)))

    def whole_layer(*inputs):
        return forward(*inputs, mask_float, onehot)
    result, pullback = jax.vjp(whole_layer, *params)
    grads = pullback(cotangent.astype(jnp.float32).reshape(IMG * NP, D))
    return (result.reshape(IMG, NP, D).astype(jnp.bfloat16), grads[0].astype(jnp.bfloat16), grads[1], grads[2], grads[3], grads[4], grads[5], grads[6], grads[7], grads[8], grads[9], grads[10], grads[11], grads[12], grads[13], grads[14], grads[15], grads[16])
```

```python
import jax
import jax.numpy as jnp
import numpy as np
from jax import lax
from jax.experimental import pallas as pl
from jax.experimental.pallas import tpu as pltpu
from jax.sharding import PartitionSpec as P

HS = 64
HHEADS = 4
LANES = 128

highest = lax.Precision.HIGHEST
norm_epsilon = 1e-06
score_scale = 0.125
f32 = jnp.float32
bf16 = jnp.bfloat16


def layer_norm(values, gain_vec):
    row_mean = jnp.mean(values, axis=-1, keepdims=True)
    centered = values - row_mean
    variance = jnp.mean(centered * centered, axis=-1, keepdims=True)
    return centered * lax.rsqrt(variance + norm_epsilon) * gain_vec


def gelu_exact(values):
    return jax.nn.gelu(values, approximate=False)


def hyper(wave_table, hyper_in, hyper_out, hyper_up, hyper_down, hyper_gain_one, hyper_gain_two):
    wave_count, hyper_width = wave_table.shape
    head_size = hyper_width // HHEADS
    projected = jnp.dot(wave_table, hyper_in, precision=highest).reshape(
        wave_count, 3, HHEADS, head_size
    )
    scores = jnp.einsum(
        "qhe,khe->hqk", projected[:, 0], projected[:, 1], precision=highest
    ) * head_size ** (-0.5)
    weights = jax.nn.softmax(scores, axis=-1)
    attended = jnp.einsum("hqk,khe->qhe", weights, projected[:, 2], precision=highest).reshape(
        wave_count, hyper_width
    )
    first_out = layer_norm(
        wave_table + jnp.dot(attended, hyper_out, precision=highest), hyper_gain_one
    )
    inner_act = gelu_exact(jnp.dot(first_out, hyper_up, precision=highest))
    return layer_norm(first_out + jnp.dot(inner_act, hyper_down, precision=highest), hyper_gain_two)


def contract_first(left, right):
    return lax.dot_general(left, right, (((0,), (0,)), ((), ())), preferred_element_type=f32)


def contract_last(left, right):
    return lax.dot_general(left, right, (((1,), (1,)), ((), ())), preferred_element_type=f32)


def hop(values, step):
    count = lax.axis_size("band")
    return lax.ppermute(values, "band", [(i, i ^ step) for i in range(count)])


def swap(values):
    return lax.ppermute(values, "head", [(0, 1), (1, 0)])


def head_sum(part):
    low = part.astype(bf16)
    return low.astype(f32) + swap(low).astype(f32)


def gather_orders(count):
    steps = []
    step = count // 2
    while step:
        steps.append(step)
        step //= 2
    if len(steps) < 4:
        return [tuple(steps)] * 3
    head, (c, b, a) = tuple(steps[:-3]), steps[-3:]
    return [head + (c, b, a), head + (a, c, b), head + (b, a, c)]


def indices_of(order):
    found = [0]
    for step in order:
        found = found + [i ^ step for i in found]
    return found


def without(count, step, value):
    return [i for i in range(count) if bool(i & step) == bool(value)]


def scatter_steps(kept, arriving, done_steps, order, count):
    left = without(count, order[0], 0)
    for step in order[1:]:
        high = [p for p, i in enumerate(left) if i & step]
        low = [p for p, i in enumerate(left) if not i & step]
        run = step
        for other in order[: order.index(step)]:
            if other < step:
                run //= 2
        shape = (len(left) // (2 * run), 2, run) + kept.shape[1:]
        k, r = kept.reshape(shape), arriving.reshape(shape)
        half = (len(low),) + kept.shape[1:]
        send = (k[:, 1].astype(f32) + r[:, 1].astype(f32)).astype(bf16).reshape(half)
        kept = (k[:, 0].astype(f32) + r[:, 0].astype(f32)).reshape(half)
        arriving = hop(send, step)
        left = [left[p] for p in low]
    return (kept.astype(f32) + arriving.astype(f32))[0]


def scatter_rows(grad, band_index, order, count):
    bits = []
    step = count // 2
    while step:
        bits.append(step)
        step //= 2
    values = grad.reshape((2,) * len(bits) + grad.shape[1:])
    left = list(bits)
    for step in order:
        axis = left.index(step)
        left.remove(step)
        mine = jnp.where(band_index & step, 1, 0)
        send = lax.dynamic_index_in_dim(values, 1 - mine, axis, False).astype(bf16)
        keep = lax.dynamic_index_in_dim(values, mine, axis, False)
        values = keep.astype(f32) + hop(send, step).astype(f32)
    return values


def embed_kernel(images, mask, *refs):
    pixel_refs, kernel_ref, outs = refs[:3], refs[3], refs[4:]
    q = pl.program_id(0)
    for c in range(3):
        scale = mask[images[c, q]].astype(f32)
        product = jnp.dot(
            pixel_refs[c][0, 0],
            kernel_ref[:, c * LANES : (c + 1) * LANES],
            preferred_element_type=f32,
        )
        outs[c][0] = (product * scale).astype(bf16)


def embed_part(images, mask, pixels, kernels):
    _, _, patches, pixel_count = pixels.shape
    half = images.shape[1]

    def pixel_spec(c):
        return pl.BlockSpec(
            (1, 1, patches, pixel_count), lambda q, im, ma, c=c: (im[c, q], 0, 0, 0)
        )

    return pl.pallas_call(
        embed_kernel,
        grid_spec=pltpu.PrefetchScalarGridSpec(
            num_scalar_prefetch=2,
            grid=(half,),
            in_specs=[pixel_spec(c) for c in range(3)]
            + [pl.BlockSpec(kernels.shape, lambda q, im, ma: (0, 0))],
            out_specs=[pl.BlockSpec((1, patches, LANES), lambda q, im, ma: (q, 0, 0))] * 3,
        ),
        out_shape=[jax.ShapeDtypeStruct((half, patches, LANES), bf16)] * 3,
        name="embed_part",
    )(images, mask, pixels, pixels, pixels, kernels)


def kernel_grad_kernel(images, mask, *refs):
    pixel_refs, grad_refs, old_ref, old_bias, out_ref, out_bias = (
        refs[:3],
        refs[3:6],
        refs[6],
        refs[7],
        refs[8],
        refs[9],
    )
    q = pl.program_id(0)

    @pl.when(q == 0)
    def _():
        out_ref[...] = old_ref[...]
        out_bias[...] = old_bias[...]

    for c in range(3):

        @pl.when(mask[images[c, q]] != 0)
        def _(c=c):
            grad = grad_refs[c][0]
            span = slice(c * LANES, (c + 1) * LANES)
            out_ref[:, span] += contract_first(pixel_refs[c][0, 0], grad)
            out_bias[:, span] += jnp.sum(grad.astype(f32), axis=0, keepdims=True)


def kernel_grad(images, mask, pixels, grads, old, old_bias):
    _, _, patches, pixel_count = pixels.shape
    half = images.shape[1]

    def pixel_spec(c):
        return pl.BlockSpec(
            (1, 1, patches, pixel_count), lambda q, im, ma, c=c: (im[c, q], 0, 0, 0)
        )

    whole = [
        pl.BlockSpec(old.shape, lambda q, im, ma: (0, 0)),
        pl.BlockSpec(old_bias.shape, lambda q, im, ma: (0, 0)),
    ]
    return pl.pallas_call(
        kernel_grad_kernel,
        grid_spec=pltpu.PrefetchScalarGridSpec(
            num_scalar_prefetch=2,
            grid=(half,),
            in_specs=[pixel_spec(c) for c in range(3)]
            + [pl.BlockSpec((1, patches, LANES), lambda q, im, ma: (q, 0, 0))] * 3
            + whole,
            out_specs=whole,
        ),
        out_shape=[
            jax.ShapeDtypeStruct(old.shape, f32),
            jax.ShapeDtypeStruct(old_bias.shape, f32),
        ],
        name="kernel_grad",
    )(images, mask, pixels, pixels, pixels, *grads, old, old_bias)


def pixel_grad_kernel(places, mask, *refs):
    grad_refs, kernel_ref, outs = refs[:12], refs[12], refs[13:]
    q = pl.program_id(0)
    count = pl.num_programs(0)
    for side in range(2):
        total = None
        for c in range(3):
            early = grad_refs[(side * 3 + c) * 2][0]
            late = grad_refs[(side * 3 + c) * 2 + 1][0]
            grad = jnp.where(places[side * 3 + c, q] < count, early, late)
            part = contract_last(grad, kernel_ref[:, c * LANES : (c + 1) * LANES])
            total = part if total is None else total + part
        outs[side][0, 0] = (total * mask[side, q].astype(f32)).astype(bf16)


def pixel_grad(places, mask, early, late, kernels):
    count, patches, _ = early[0].shape
    pixel_count = kernels.shape[0]
    specs, args = [], []
    for side in range(2):
        for c in range(3):
            specs.append(
                pl.BlockSpec(
                    (1, patches, LANES),
                    lambda q, pc, ma, r=side * 3 + c: (jnp.minimum(pc[r, q], count - 1), 0, 0),
                )
            )
            specs.append(
                pl.BlockSpec(
                    (1, patches, LANES),
                    lambda q, pc, ma, r=side * 3 + c: (jnp.maximum(pc[r, q] - count, 0), 0, 0),
                )
            )
            args += [early[c], late[c]]
    specs.append(pl.BlockSpec(kernels.shape, lambda q, pc, ma: (0, 0)))
    return pl.pallas_call(
        pixel_grad_kernel,
        grid_spec=pltpu.PrefetchScalarGridSpec(
            num_scalar_prefetch=2,
            grid=(count,),
            in_specs=specs,
            out_specs=[pl.BlockSpec((1, 1, patches, pixel_count), lambda q, pc, ma: (q, 0, 0, 0))]
            * 2,
        ),
        out_shape=[jax.ShapeDtypeStruct((count, 1, patches, pixel_count), bf16)] * 2,
        name="pixel_grad",
    )(places, mask, *args, kernels)


def shards(
    pixels,
    band_mask,
    wave_ids,
    pos_embed,
    in_proj,
    out_proj,
    up_proj,
    down_proj,
    gain_one,
    gain_two,
    kernel_gen,
    bias_gen,
    wave_table,
    hyper_in,
    hyper_out,
    hyper_up,
    hyper_down,
    hyper_gain_one,
    hyper_gain_two,
    cotangent,
):
    band_index = lax.axis_index("band")
    head_index = lax.axis_index("head")
    count = lax.axis_size("band")
    images, slot_local, patches, pixel_count = pixels.shape
    model_width = in_proj.shape[1]
    half_width = in_proj.shape[2]
    wave_count, hyper_width = wave_table.shape
    assert images == count and slot_local == 1
    heads_local = half_width // HS
    orders = gather_orders(count)
    scatters = [tuple(reversed(order)) for order in orders]

    onehot = (
        wave_ids[:, 0][:, None] == jnp.arange(wave_count, dtype=jnp.int32)[None, :]
    ).astype(f32)
    onehot_low = onehot.astype(bf16)
    mask_column = lax.dynamic_slice_in_dim(band_mask, band_index, 1, 1)[:, 0]
    mask_row = lax.dynamic_slice_in_dim(band_mask, band_index, 1, 0).astype(f32)

    mixture, hyper_back = jax.vjp(
        hyper, wave_table, hyper_in, hyper_out, hyper_up, hyper_down, hyper_gain_one, hyper_gain_two
    )
    mix_low = mixture.astype(bf16)
    gen_flat = kernel_gen.reshape(hyper_width, -1)
    mix_slots = jnp.dot(onehot_low, mix_low, preferred_element_type=f32).astype(bf16)
    slot_piece = jnp.dot(mix_slots, gen_flat, preferred_element_type=f32).astype(bf16)
    slot_piece = slot_piece.reshape(count, -1, half_width)
    kernels = lax.all_to_all(slot_piece, "band", 0, 0, tiled=True).reshape(pixel_count, half_width)
    wave_bias = jnp.dot(mix_low, bias_gen, preferred_element_type=f32)
    image_bias = jnp.dot(jnp.dot(mask_row, onehot, precision=highest), wave_bias, precision=highest)

    def image_table(value):
        return jnp.stack(
            [
                band_index ^ jnp.asarray(without(count, order[0], value), jnp.int32)
                for order in scatters
            ]
        )

    sends = embed_part(image_table(1), mask_column, pixels, kernels)
    arriving = [hop(send, order[0]) for send, order in zip(sends, scatters)]
    keeps = embed_part(image_table(0), mask_column, pixels, kernels)
    embed_half = jnp.concatenate(
        [scatter_steps(k, a, 1, o, count) for k, a, o in zip(keeps, arriving, scatters)], axis=1
    )
    embed_half = embed_half + image_bias
    embed = lax.all_gather(embed_half.astype(bf16), "head", axis=1, tiled=True).astype(f32)

    tokens = embed + pos_embed.astype(f32)
    normed, norm_back_one = jax.vjp(layer_norm, tokens, gain_one.astype(f32))
    normed_low = normed.astype(bf16)
    projected = jnp.einsum("rd,jde->jre", normed_low, in_proj, preferred_element_type=f32)
    projected = projected.astype(bf16).reshape(3, patches, heads_local, HS)
    query_rows = projected[0]
    key_rows = projected[1]
    value_rows = projected[2]
    scores = (
        jnp.einsum("qhe,khe->hqk", query_rows, key_rows, preferred_element_type=f32) * score_scale
    )
    softmax_out = jax.nn.softmax(scores, axis=-1)
    probs_low = softmax_out.astype(bf16)
    attended = jnp.einsum("hqk,khe->qhe", probs_low, value_rows, preferred_element_type=f32)
    attended = attended.astype(bf16).reshape(patches, half_width)
    attn_part = jnp.dot(attended, out_proj, preferred_element_type=f32)
    mid_stream = tokens + head_sum(attn_part)
    second, norm_back_two = jax.vjp(layer_norm, mid_stream, gain_two.astype(f32))
    second_low = second.astype(bf16)
    hidden = jnp.dot(second_low, up_proj, preferred_element_type=f32)
    active, gelu_back = jax.vjp(gelu_exact, hidden)
    active_low = active.astype(bf16)
    down_part = jnp.dot(active_low, down_proj, preferred_element_type=f32)
    result = mid_stream + head_sum(down_part)
    layer_out = result.astype(bf16).reshape(1, patches, model_width)

    grad_low = cotangent.reshape(patches, model_width)
    grad_result = grad_low.astype(f32)
    grad_active = contract_last(grad_low, down_proj)
    grad_hidden = gelu_back(grad_active)[0].astype(bf16)
    grad_second = head_sum(contract_last(grad_hidden, up_proj))

    half_order = tuple(reversed(orders[0]))
    other_order = (half_order[1], half_order[0]) + half_order[2:]

    def row_blocks(grad):
        return grad.astype(bf16).reshape(count, model_width // count, -1)

    grad_down = scatter_rows(
        row_blocks(contract_first(grad_low, active_low)), band_index, other_order, count
    )
    grad_up = scatter_rows(
        row_blocks(contract_first(second_low, grad_hidden)), band_index, half_order, count
    )

    grad_mid_norm, grad_gain_two = norm_back_two(grad_second)
    grad_mid = grad_result + grad_mid_norm
    grad_mid_low = grad_mid.astype(bf16)
    grad_out = row_blocks(contract_first(grad_mid_low, attended))
    grad_attended = contract_last(grad_mid_low, out_proj).astype(bf16)
    grad_attended = grad_attended.reshape(patches, heads_local, HS)
    grad_probs = jnp.einsum("qhe,khe->hqk", grad_attended, value_rows, preferred_element_type=f32)
    grad_value = jnp.einsum("hqk,qhe->khe", probs_low, grad_attended, preferred_element_type=f32)
    grad_scores = softmax_out * (
        grad_probs - jnp.sum(grad_probs * softmax_out, axis=-1, keepdims=True)
    )
    grad_scores_low = grad_scores.astype(bf16)
    grad_query = (
        jnp.einsum("hqk,khe->qhe", grad_scores_low, key_rows, preferred_element_type=f32)
        * score_scale
    )
    grad_key = (
        jnp.einsum("hqk,qhe->khe", grad_scores_low, query_rows, preferred_element_type=f32)
        * score_scale
    )
    grad_projected = jnp.stack([grad_query, grad_key, grad_value]).astype(bf16)
    grad_projected = grad_projected.reshape(3, patches, half_width)
    grad_normed_part = jnp.einsum(
        "jre,jde->rd", grad_projected, in_proj, preferred_element_type=f32
    )
    grad_normed = head_sum(grad_normed_part)
    grad_tokens_norm, grad_gain_one = norm_back_one(grad_normed)
    grad_tokens = grad_mid + grad_tokens_norm
    grad_embed = grad_tokens.astype(bf16)
    grad_embed_half = lax.dynamic_slice_in_dim(grad_embed, head_index * half_width, half_width, 1)

    early, late = [], []
    for c, order in enumerate(orders):
        block = grad_embed_half[None, :, c * LANES : (c + 1) * LANES]
        for step in order[:-1]:
            block = jnp.concatenate([block, hop(block, step)], axis=0)
        early.append(block)
        late.append(hop(block, order[-1]))
    early_index = [indices_of(order[:-1]) for order in orders]
    late_index = [[i ^ order[-1] for i in e] for e, order in zip(early_index, orders)]

    def relative_table(lists):
        return band_index ^ jnp.asarray(lists, jnp.int32)

    zero = jnp.zeros((pixel_count, half_width), f32)
    zero_bias = jnp.zeros((1, half_width), f32)
    grad_kernels, grad_bias = kernel_grad(
        relative_table(early_index), mask_column, pixels, early, zero, zero_bias
    )
    grad_kernels, grad_bias = kernel_grad(
        relative_table(late_index), mask_column, pixels, late, grad_kernels, grad_bias
    )

    place = np.zeros((3, count), np.int32)
    for c in range(3):
        for position, index in enumerate(early_index[c] + late_index[c]):
            place[c, index] = position
    place = jnp.asarray(place)
    image_list = jnp.stack(
        [
            head_index * (count // 2) + jnp.arange(count // 2, dtype=jnp.int32),
            (1 - head_index) * (count // 2) + jnp.arange(count // 2, dtype=jnp.int32),
        ]
    )
    places = jnp.concatenate([jnp.take(place, image_list[s] ^ band_index, axis=1) for s in (0, 1)])
    side_mask = jnp.stack([jnp.take(mask_column, image_list[s]) for s in (0, 1)])
    own_pixels, other_pixels = pixel_grad(places, side_mask, early, late, kernels)
    grad_pixels = (own_pixels.astype(f32) + swap(other_pixels).astype(f32)).astype(bf16)

    bias_high = grad_bias.astype(bf16)
    bias_low = (grad_bias - bias_high.astype(f32)).astype(bf16)
    blocks = grad_kernels.astype(bf16).reshape(count, -1, half_width)
    piece = blocks.shape[1]
    blocks = jnp.concatenate(
        [
            blocks,
            jnp.broadcast_to(bias_high[None], (count, 1, half_width)),
            jnp.broadcast_to(bias_low[None], (count, 1, half_width)),
        ],
        axis=1,
    )
    blocks = lax.all_to_all(blocks, "band", 0, 0, tiled=True)
    grad_flat = (
        jnp.dot(
            onehot_low.T,
            blocks[:, :piece].reshape(count, -1),
            preferred_element_type=f32,
        )
        .astype(bf16)
    )
    slot_bias = blocks[:, piece].astype(f32) + blocks[:, piece + 1].astype(f32)
    grad_wave_bias = jnp.dot(onehot.T, slot_bias, precision=highest)
    grad_kernel_gen = contract_first(mix_low, grad_flat).reshape(kernel_gen.shape)
    grad_mix_part = contract_last(grad_flat, gen_flat)
    grad_mix_part = grad_mix_part + jnp.dot(
        grad_wave_bias, bias_gen.astype(f32).T, precision=highest
    ) * (1.0 / count)
    grad_bias_gen = jnp.dot(mix_low.astype(f32).T, grad_wave_bias, precision=highest)

    grad_mix = grad_mix_part + swap(grad_mix_part)
    step = 1
    while step < count:
        if step * 4 <= count:
            grad_mix = (grad_mix + hop(grad_mix, step)) + (
                hop(grad_mix, 2 * step) + hop(grad_mix, 3 * step)
            )
            step *= 4
        else:
            grad_mix = grad_mix + hop(grad_mix, step)
            step *= 2
    hyper_grads = hyper_back(grad_mix)

    grad_in = [
        row_blocks(contract_first(normed_low, grad_projected[j])) for j in range(3)
    ]
    small = jnp.concatenate(
        [
            grad_tokens,
            grad_gain_one[None],
            grad_gain_two[None],
        ],
        axis=0,
    )
    extra = row_blocks(small.T)
    first = scatter_rows(
        jnp.concatenate([grad_in[0], grad_in[1]], axis=2), band_index, half_order, count
    )
    second_part = scatter_rows(
        jnp.concatenate([grad_in[2], grad_out, extra], axis=2), band_index, other_order, count
    )
    grad_in_proj = jnp.stack(
        [first[:, :half_width], first[:, half_width:], second_part[:, :half_width]]
    )
    grad_out_proj = second_part[:, half_width : 2 * half_width].T
    tail = second_part[:, 2 * half_width :].T
    return (
        layer_out,
        grad_pixels,
        tail[:patches],
        grad_in_proj,
        grad_out_proj,
        grad_up,
        grad_down.T,
        tail[patches],
        tail[patches + 1],
        grad_kernel_gen,
        grad_bias_gen,
        *hyper_grads,
    )


def solution(mesh):
    in_specs = (
        P(None, "band", None, None),
        P(),
        P(),
        P(),
        P(None, None, "head"),
        P("head", None),
        P(None, "head"),
        P("head", None),
        P(),
        P(),
        P(None, "band", "head"),
        P(None, "head"),
        P(),
        P(),
        P(),
        P(),
        P(),
        P(),
        P(),
        P("band", None, None),
    )
    out_specs = (
        P("band", None, None),
        P("head", "band", None, None),
        P(None, "band"),
        P(None, "band", "head"),
        P("head", "band"),
        P("band", "head"),
        P("head", "band"),
        P("band"),
        P("band"),
        P(None, "band", "head"),
        P(None, "head"),
        P(),
        P(),
        P(),
        P(),
        P(),
        P(),
        P(),
    )
    return jax.shard_map(shards, mesh=mesh, in_specs=in_specs, out_specs=out_specs, check_vma=False)
```

```python
import jax
import jax.numpy as jnp
import numpy as np
from jax import lax
from jax.experimental import pallas as pl
from jax.experimental.pallas import tpu as pltpu
from jax.sharding import PartitionSpec as P

HS = 64
HHEADS = 4
LANES = 128
EXTRA = 256

highest = lax.Precision.HIGHEST
norm_epsilon = 1e-06
score_scale = 0.125
root_half = 0.7071067811865476
density_scale = 0.3989422804014327
f32 = jnp.float32
bf16 = jnp.bfloat16


def norm_parts(values):
    centered = values - jnp.mean(values, axis=-1, keepdims=True)
    variance = jnp.mean(centered * centered, axis=-1, keepdims=True)
    scale = lax.rsqrt(variance + norm_epsilon)
    return centered * scale, scale


def norm_grad(grad, normal, scale):
    inner = jnp.mean(grad, axis=-1, keepdims=True)
    along = jnp.mean(grad * normal, axis=-1, keepdims=True)
    return scale * (grad - inner - normal * along)


def gelu_parts(values):
    cumulative = 0.5 * (1.0 + lax.erf(values * root_half))
    density = jnp.exp(-0.5 * values * values) * density_scale
    return cumulative, cumulative + values * density


def contract_first(left, right):
    return lax.dot_general(left, right, (((0,), (0,)), ((), ())), preferred_element_type=f32)


def contract_last(left, right):
    return lax.dot_general(left, right, (((1,), (1,)), ((), ())), preferred_element_type=f32)


def exact(left, right, dims=((1,), (0,))):
    return lax.dot_general(
        left, right, (dims, ((), ())), precision=highest, preferred_element_type=f32
    )


FIRST = ((0,), (0,))
LAST = ((1,), (1,))


def low_dot(left, right):
    return jnp.dot(left, right, preferred_element_type=f32)


def equal_index(rows, columns, row_shift, column_shift, row_mask, column_mask):
    row = lax.broadcasted_iota(jnp.int32, (rows, columns), 0)
    column = lax.broadcasted_iota(jnp.int32, (rows, columns), 1)
    return ((row >> row_shift) & row_mask) == ((column >> column_shift) & column_mask)


def onehot_of(wave_column, wave_count):
    slots = wave_column.shape[0]
    return wave_column == lax.broadcasted_iota(jnp.int32, (slots, wave_count), 1)


def spread(mix, piece):
    rows, width = mix.shape
    shift = piece.bit_length() - 1
    all_bits = 2**30 - 1
    repeat_rows = equal_index(rows * piece, rows, shift, 0, all_bits, all_bits)
    repeat_columns = equal_index(width, width * piece, 0, shift, all_bits, all_bits)
    tall = low_dot(repeat_rows.astype(bf16), mix).astype(bf16)
    return low_dot(tall, repeat_columns.astype(bf16))


def kron_identity(mix, piece):
    rows, width = mix.shape
    same = equal_index(rows * piece, width * piece, 0, 0, piece - 1, piece - 1)
    return jnp.where(same, spread(mix, piece), 0.0).astype(bf16)


def head_lanes(width, head_size, head):
    lane = lax.broadcasted_iota(jnp.int32, (1, width), 1)
    return (lane >> (head_size.bit_length() - 1)) == head


def hop(values, step):
    count = lax.axis_size("band")
    return lax.ppermute(values, "band", [(i, i ^ step) for i in range(count)])


def swap(values):
    return lax.ppermute(values, "head", [(0, 1), (1, 0)])


def head_sum(part):
    low = part.astype(bf16)
    return low.astype(f32) + swap(low).astype(f32)


def gather_orders(count):
    steps = []
    step = count // 2
    while step:
        steps.append(step)
        step //= 2
    if len(steps) < 4:
        return [tuple(steps)] * 3
    head, (c, b, a) = tuple(steps[:-3]), steps[-3:]
    return [head + (c, b, a), head + (a, c, b), head + (b, a, c)]


def relative_index(position, order):
    index = 0
    for t, step in enumerate(order):
        index = index + ((position >> t) & 1) * step
    return index


def position_of(index, order):
    position = 0
    for t, step in enumerate(order):
        position = position + (((index >> (step.bit_length() - 1)) & 1) << t)
    return position


def scatter_sum(keeps, sends, orders, arriving=None):
    if arriving is None:
        arriving = [hop(send, order[-1]) for send, order in zip(sends, orders)]
    for t in range(len(orders[0]) - 2, -1, -1):
        sends, kept = [], []
        for k, a in zip(keeps, arriving):
            half = k.shape[0] // 2
            sends.append((k[half:].astype(f32) + a[half:].astype(f32)).astype(bf16))
            kept.append(k[:half].astype(f32) + a[:half].astype(f32))
        keeps = kept
        if t == 0 and len({order[0] for order in orders}) == 1:
            merged = hop(jnp.concatenate(sends, axis=-1), orders[0][0])
            arriving, start = [], 0
            for send in sends:
                arriving.append(merged[..., start : start + send.shape[-1]])
                start += send.shape[-1]
        else:
            arriving = [hop(send, order[t]) for send, order in zip(sends, orders)]
    return [k.astype(f32) + a.astype(f32) for k, a in zip(keeps, arriving)]


def loop(count, body):
    if count <= 16:
        for q in range(count):
            body(q)
    else:

        def step(q, carry):
            body(q)
            return carry

        lax.fori_loop(0, count, step, 0)


def span(c):
    return slice(c * LANES, (c + 1) * LANES)


def local_call(kernel, where, tables, args, out_shape, scratch=(), name=None, flops=0):
    vmem = pl.BlockSpec(memory_space=pltpu.VMEM)
    smem = pl.BlockSpec(memory_space=pltpu.SMEM)
    moved = sum(x.size * x.dtype.itemsize for x in args)
    moved += sum(int(np.prod(s.shape)) * s.dtype.itemsize for s in out_shape)
    return pl.pallas_call(
        kernel,
        in_specs=[smem] * (1 + len(tables)) + [vmem] * len(args),
        out_specs=[vmem] * len(out_shape),
        out_shape=list(out_shape),
        scratch_shapes=list(scratch),
        cost_estimate=pl.CostEstimate(flops=flops, bytes_accessed=moved, transcendentals=0),
        compiler_params=pltpu.CompilerParams(vmem_limit_bytes=56 * 2**20),
        name=name,
    )(where, *tables, *args)


def hyper_forward(where, wave_ids, band_mask, table, weights, gains, gen_rows, bias_gen, count):
    slots = wave_ids.shape[0]
    wave_count, width = table.shape
    piece = gen_rows.shape[0] // width
    half_width = gen_rows.shape[1]
    inner = weights[2].shape[1]
    head_size = width // HHEADS

    def kernel(
        where_ref, ids_ref, mask_ref, table_ref, in_ref, out_ref, up_ref, down_ref, one_ref,
        two_ref, gen_ref, bias_ref, piece_out, image_bias_out, mix_out, projected_out, probs_out,
        attended_out, normal_one_out, scale_one_out, hidden_out, normal_two_out, scale_two_out,
    ):
        values = table_ref[...]
        projected = exact(values, in_ref[...])
        projected_out[...] = projected
        query, key, value = (projected[:, i * width : (i + 1) * width] for i in range(3))
        attended = jnp.zeros((wave_count, width), f32)
        for head in range(HHEADS):
            lanes = head_lanes(width, head_size, head)
            scores = exact(jnp.where(lanes, query, 0.0), key, LAST) * head_size ** (-0.5)
            scores = jnp.exp(scores - jnp.max(scores, axis=-1, keepdims=True))
            probs = scores / jnp.sum(scores, axis=-1, keepdims=True)
            probs_out[head] = probs
            attended += exact(probs, jnp.where(lanes, value, 0.0))
        attended_out[...] = attended
        normal_one, scale_one = norm_parts(values + exact(attended, out_ref[...]))
        first = normal_one * one_ref[...]
        hidden = exact(first, up_ref[...])
        factor, _ = gelu_parts(hidden)
        normal_two, scale_two = norm_parts(first + exact(hidden * factor, down_ref[...]))
        mix = (normal_two * two_ref[...]).astype(bf16)
        normal_one_out[...] = normal_one
        scale_one_out[...] = scale_one
        hidden_out[...] = hidden
        normal_two_out[...] = normal_two
        scale_two_out[...] = scale_two
        mix_out[...] = mix
        onehot = onehot_of(ids_ref[...], wave_count)
        slot_mix = low_dot(onehot.astype(bf16), mix).astype(bf16)
        piece_out[...] = low_dot(kron_identity(slot_mix, piece), gen_ref[...]).astype(bf16)
        image = lax.broadcasted_iota(jnp.int32, mask_ref.shape, 0) == where_ref[0]
        bands = jnp.sum(jnp.where(image, mask_ref[...], 0).astype(f32), axis=0, keepdims=True)
        waves = exact(bands, onehot.astype(f32))
        image_bias_out[...] = exact(waves, low_dot(mix, bias_ref[...]))

    def shape(*dims):
        return jax.ShapeDtypeStruct(dims, f32)

    return local_call(
        kernel,
        where,
        [],
        [wave_ids, band_mask, table, *weights, *gains, gen_rows, bias_gen],
        [
            jax.ShapeDtypeStruct((slots * piece, half_width), bf16),
            shape(1, half_width),
            jax.ShapeDtypeStruct((wave_count, width), bf16),
            shape(wave_count, 3 * width),
            shape(HHEADS, wave_count, wave_count),
            shape(wave_count, width),
            shape(wave_count, width),
            shape(wave_count, 1),
            shape(wave_count, inner),
            shape(wave_count, width),
            shape(wave_count, 1),
        ],
        name="hyper_forward",
        flops=8 * slots * piece * gen_rows.size,
    )


def hyper_backward(where, grad_mix, table, weights, gains, kept):
    wave_count, width = table.shape
    head_size = width // HHEADS

    def kernel(
        where_ref, grad_ref, table_ref, in_ref, out_ref, up_ref, down_ref, one_ref, two_ref,
        projected_ref, probs_ref, attended_ref, normal_one_ref, scale_one_ref, hidden_ref,
        normal_two_ref, scale_two_ref, table_out, in_out, out_out, up_out, down_out, one_out,
        two_out,
    ):
        grad = grad_ref[...]
        normal_two = normal_two_ref[...]
        two_out[...] = jnp.sum(grad * normal_two, axis=0, keepdims=True)
        grad_two = norm_grad(grad * two_ref[...], normal_two, scale_two_ref[...])
        hidden = hidden_ref[...]
        factor, slope = gelu_parts(hidden)
        normal_one = normal_one_ref[...]
        first = normal_one * one_ref[...]
        grad_hidden = exact(grad_two, down_ref[...], LAST) * slope
        down_out[...] = exact(hidden * factor, grad_two, FIRST)
        up_out[...] = exact(first, grad_hidden, FIRST)
        grad_first = grad_two + exact(grad_hidden, up_ref[...], LAST)
        one_out[...] = jnp.sum(grad_first * normal_one, axis=0, keepdims=True)
        grad_one = norm_grad(grad_first * one_ref[...], normal_one, scale_one_ref[...])
        out_out[...] = exact(attended_ref[...], grad_one, FIRST)
        grad_attended = exact(grad_one, out_ref[...], LAST)
        projected = projected_ref[...]
        query, key, value = (projected[:, i * width : (i + 1) * width] for i in range(3))
        grads = [jnp.zeros((wave_count, width), f32) for _ in range(3)]
        for head in range(HHEADS):
            lanes = head_lanes(width, head_size, head)
            own = jnp.where(lanes, grad_attended, 0.0)
            probs = probs_ref[head]
            grad_probs = exact(own, value, LAST)
            grads[2] += exact(probs, own, FIRST)
            scores = probs * (grad_probs - jnp.sum(grad_probs * probs, axis=-1, keepdims=True))
            scores = scores * head_size ** (-0.5)
            grads[0] += exact(scores, jnp.where(lanes, key, 0.0))
            grads[1] += exact(scores, jnp.where(lanes, query, 0.0), FIRST)
        grad_projected = jnp.concatenate(grads, axis=1)
        in_out[...] = exact(table_ref[...], grad_projected, FIRST)
        table_out[...] = grad_one + exact(grad_projected, in_ref[...], LAST)

    arrays = [table, *weights, *gains]
    return local_call(
        kernel,
        where,
        [],
        [grad_mix, *arrays, *kept],
        [jax.ShapeDtypeStruct(a.shape, f32) for a in arrays],
        name="hyper_backward",
        flops=80 * wave_count * weights[2].size,
    )


def attention_forward(where, own, other, pos, gain, in_proj, out_proj):
    patches, half_width = own.shape
    width = 2 * half_width
    heads = half_width // HS

    def kernel(
        where_ref, own_ref, other_ref, pos_ref, gain_ref, in_ref, out_ref, tokens_out, normed_out,
        query_out, key_out, value_out, probs_out, attended_out, part_out,
    ):
        own_half, other_half = own_ref[...].astype(f32), other_ref[...].astype(f32)
        first = where_ref[1] == 0
        embed = jnp.concatenate(
            [jnp.where(first, own_half, other_half), jnp.where(first, other_half, own_half)], axis=1
        )
        tokens = embed + pos_ref[...].astype(f32)
        tokens_out[...] = tokens
        normal, _ = norm_parts(tokens)
        normed = (normal * gain_ref[...].astype(f32)).astype(bf16)
        normed_out[...] = normed
        projected = [low_dot(normed, in_ref[j]).astype(bf16) for j in range(3)]
        query_out[...], key_out[...], value_out[...] = projected
        for pair in range(heads // 2):
            lanes = slice(pair * 2 * HS, (pair + 1) * 2 * HS)
            query, key, value = (p[:, lanes] for p in projected)
            total = None
            for side in range(2):
                mine = head_lanes(2 * HS, HS, side)
                scores = contract_last(jnp.where(mine, query, 0), key) * score_scale
                scores = jnp.exp(scores - jnp.max(scores, axis=-1, keepdims=True))
                probs = scores / jnp.sum(scores, axis=-1, keepdims=True)
                probs_out[2 * pair + side] = probs
                part = low_dot(probs.astype(bf16), jnp.where(mine, value, 0))
                total = part if total is None else total + part
            attended_out[:, lanes] = total.astype(bf16)
        part_out[...] = low_dot(attended_out[...], out_ref[...]).astype(bf16)

    def low(*dims):
        return jax.ShapeDtypeStruct(dims, bf16)

    return local_call(
        kernel,
        where,
        [],
        [own, other, pos, gain, in_proj, out_proj],
        [
            jax.ShapeDtypeStruct((patches, width), f32),
            low(patches, width),
            low(patches, half_width),
            low(patches, half_width),
            low(patches, half_width),
            jax.ShapeDtypeStruct((heads, patches, patches), f32),
            low(patches, half_width),
            low(patches, width),
        ],
        name="attention_forward",
        flops=2 * patches * (in_proj.size + out_proj.size + 4 * patches * half_width),
    )


def feed_forward(where, tokens, own, other, gain, up, down, cotangent):
    patches, width = tokens.shape
    local = up.shape[1]
    tile = local // 3

    def kernel(
        where_ref, tokens_ref, own_ref, other_ref, gain_ref, up_ref, down_ref, cotangent_ref,
        mid_out, second_out, active_out, grad_hidden_out, parts_out,
    ):
        mid = tokens_ref[...] + (own_ref[...].astype(f32) + other_ref[...].astype(f32))
        mid_out[...] = mid
        normal, _ = norm_parts(mid)
        second = (normal * gain_ref[...].astype(f32)).astype(bf16)
        second_out[...] = second
        for t in range(3):
            columns = slice(t * tile, (t + 1) * tile)
            hidden = low_dot(second, up_ref[:, columns])
            factor, slope = gelu_parts(hidden)
            active_out[:, columns] = (hidden * factor).astype(bf16)
            grad_active = contract_last(cotangent_ref[...], down_ref[columns, :])
            grad_hidden_out[:, columns] = (grad_active * slope).astype(bf16)
        parts_out[0] = low_dot(active_out[...], down_ref[...]).astype(bf16)
        parts_out[1] = contract_last(grad_hidden_out[...], up_ref[...]).astype(bf16)

    return local_call(
        kernel,
        where,
        [],
        [tokens, own, other, gain, up, down, cotangent],
        [
            jax.ShapeDtypeStruct((patches, width), f32),
            jax.ShapeDtypeStruct((patches, width), bf16),
            jax.ShapeDtypeStruct((patches, local), bf16),
            jax.ShapeDtypeStruct((patches, local), bf16),
            jax.ShapeDtypeStruct((2, patches, width), bf16),
        ],
        name="feed_forward",
        flops=8 * patches * up.size,
    )


def attention_backward(
    where, mid, own, other, cotangent, gain, in_proj, out_proj, query, key, value, probs
):
    patches, width = mid.shape
    half_width = width // 2
    heads = half_width // HS

    def kernel(
        where_ref, mid_ref, own_ref, other_ref, cotangent_ref, gain_ref, in_ref, out_ref,
        query_ref, key_ref, value_ref, probs_ref, layer_out, gain_out, grad_mid_out, low_out,
        query_out, key_out, value_out, part_out,
    ):
        mid_values = mid_ref[...]
        down = own_ref[0].astype(f32) + other_ref[0].astype(f32)
        layer_out[...] = (mid_values + down).astype(bf16)
        grad_second = own_ref[1].astype(f32) + other_ref[1].astype(f32)
        normal, scale = norm_parts(mid_values)
        gain_out[...] = jnp.sum(grad_second * normal, axis=0, keepdims=True)
        grad_mid = cotangent_ref[...].astype(f32) + norm_grad(
            grad_second * gain_ref[...].astype(f32), normal, scale
        )
        grad_mid_out[...] = grad_mid
        grad_low = grad_mid.astype(bf16)
        low_out[...] = grad_low
        grad_attended = contract_last(grad_low, out_ref[...]).astype(bf16)
        for pair in range(heads // 2):
            lanes = slice(pair * 2 * HS, (pair + 1) * 2 * HS)
            query, key, value = query_ref[:, lanes], key_ref[:, lanes], value_ref[:, lanes]
            totals = [None] * 3
            for side in range(2):
                mine = head_lanes(2 * HS, HS, side)
                own_grad = jnp.where(mine, grad_attended[:, lanes], 0)
                probs = probs_ref[2 * pair + side]
                grad_probs = contract_last(own_grad, value)
                inner = jnp.sum(grad_probs * probs, axis=-1, keepdims=True)
                scores = (probs * (grad_probs - inner)).astype(bf16)
                parts = (
                    low_dot(scores, jnp.where(mine, key, 0)),
                    contract_first(scores, jnp.where(mine, query, 0)),
                    contract_first(probs.astype(bf16), own_grad),
                )
                totals = [p if t is None else t + p for t, p in zip(totals, parts)]
            query_out[:, lanes] = (totals[0] * score_scale).astype(bf16)
            key_out[:, lanes] = (totals[1] * score_scale).astype(bf16)
            value_out[:, lanes] = totals[2].astype(bf16)
        part = contract_last(query_out[...], in_ref[0])
        part += contract_last(key_out[...], in_ref[1])
        part += contract_last(value_out[...], in_ref[2])
        part_out[...] = part.astype(bf16)

    def low(*dims):
        return jax.ShapeDtypeStruct(dims, bf16)

    return local_call(
        kernel,
        where,
        [],
        [mid, own, other, cotangent, gain, in_proj, out_proj, query, key, value, probs],
        [
            low(patches, width),
            jax.ShapeDtypeStruct((1, width), f32),
            jax.ShapeDtypeStruct((patches, width), f32),
            low(patches, width),
            low(patches, half_width),
            low(patches, half_width),
            low(patches, half_width),
            low(patches, width),
        ],
        name="attention_backward",
        flops=2 * patches * (in_proj.size + out_proj.size + 8 * patches * half_width),
    )


def token_grad(where, tokens, grad_mid, own, other, gain, gain_two_grad):
    patches, width = tokens.shape
    half_width = width // 2

    def kernel(
        where_ref, tokens_ref, grad_mid_ref, own_ref, other_ref, gain_ref, two_ref, half_out,
        small_out,
    ):
        grad_normed = own_ref[...].astype(f32) + other_ref[...].astype(f32)
        normal, scale = norm_parts(tokens_ref[...])
        grad_one = jnp.sum(grad_normed * normal, axis=0, keepdims=True)
        grad = grad_mid_ref[...] + norm_grad(
            grad_normed * gain_ref[...].astype(f32), normal, scale
        )
        low = grad.astype(bf16)
        half_out[...] = jnp.where(where_ref[1] == 0, low[:, :half_width], low[:, half_width:])
        small_out[...] = jnp.zeros_like(small_out)
        small_out[:patches, :] = low
        small_out[patches : patches + 1, :] = grad_one.astype(bf16)
        small_out[patches + 1 : patches + 2, :] = two_ref[...].astype(bf16)

    return local_call(
        kernel,
        where,
        [],
        [tokens, grad_mid, own, other, gain, gain_two_grad],
        [
            jax.ShapeDtypeStruct((patches, half_width), bf16),
            jax.ShapeDtypeStruct((EXTRA, width), bf16),
        ],
        name="token_grad",
    )


def wave_grads(wave_column, blocks_ref, rows_ref, wave_count, piece):
    slots = wave_column.shape[0]
    for s in range(slots):
        rows_ref[s * piece : (s + 1) * piece, :] = blocks_ref[s, :piece, :]
    onehot = onehot_of(wave_column, wave_count)
    bits = 2**30 - 1
    shift = piece.bit_length() - 1
    tall = low_dot(
        equal_index(slots * piece, slots, shift, 0, bits, bits).astype(bf16), onehot.astype(bf16)
    ).astype(bf16)
    wide = low_dot(
        tall, equal_index(wave_count, wave_count * piece, 0, shift, bits, bits).astype(bf16)
    )
    same = equal_index(slots * piece, wave_count * piece, 0, 0, piece - 1, piece - 1)
    select = jnp.where(same, wide, 0.0).astype(bf16)
    kernels = contract_first(select, rows_ref[...]).astype(bf16)
    biases = jnp.concatenate(
        [
            blocks_ref[s, piece : piece + 1, :].astype(f32)
            + blocks_ref[s, piece + 1 : piece + 2, :].astype(f32)
            for s in range(slots)
        ],
        axis=0,
    )
    return kernels, exact(onehot.astype(f32), biases, FIRST)


def mix_grad(where, wave_ids, blocks, gen_rows, bias_gen, wave_count, count):
    width, half_width = bias_gen.shape
    piece = gen_rows.shape[0] // width

    def kernel(
        where_ref, ids_ref, blocks_ref, gen_ref, bias_ref, mix_out, kernels_out, biases_out, rows_ref
    ):
        kernels, biases = wave_grads(ids_ref[...], blocks_ref, rows_ref, wave_count, piece)
        kernels_out[...] = kernels
        biases_out[...] = biases
        products = contract_last(kernels, gen_ref[...])
        same = equal_index(*products.shape, 0, 0, piece - 1, piece - 1)
        products = jnp.where(same, products, 0.0)
        rows = jnp.sum(products.reshape(wave_count, piece, -1), axis=1)
        bits = 2**30 - 1
        gather = equal_index(
            width * piece, width, piece.bit_length() - 1, 0, bits, bits
        ).astype(f32)
        mix = exact(rows, gather)
        mix_out[...] = mix + exact(biases, bias_ref[...].astype(f32), LAST) * (1.0 / count)

    return local_call(
        kernel,
        where,
        [],
        [wave_ids, blocks, gen_rows, bias_gen],
        [
            jax.ShapeDtypeStruct((wave_count, width), f32),
            jax.ShapeDtypeStruct((wave_count * piece, half_width), bf16),
            jax.ShapeDtypeStruct((wave_count, half_width), f32),
        ],
        scratch=[pltpu.VMEM((wave_ids.shape[0] * piece, half_width), bf16)],
        name="mix_grad",
        flops=2 * wave_count * piece * gen_rows.size,
    )


def generator_grads(where, mix_low, kernels, biases):
    wave_count, width = mix_low.shape
    piece = kernels.shape[0] // wave_count
    half_width = kernels.shape[1]

    def kernel(where_ref, mix_ref, kernels_ref, biases_ref, gen_out, bias_out):
        mix = mix_ref[...]
        gen_out[...] = contract_first(kron_identity(mix, piece), kernels_ref[...])
        bias_out[...] = exact(mix.astype(f32), biases_ref[...], FIRST)

    return local_call(
        kernel,
        where,
        [],
        [mix_low, kernels, biases],
        [
            jax.ShapeDtypeStruct((width * piece, half_width), f32),
            jax.ShapeDtypeStruct((width, half_width), f32),
        ],
        name="generator_grads",
        flops=2 * wave_count * piece * width * piece * half_width,
    )


def embed_part(upper, orders, where, mask, pixels, kernels):
    images, patches, pixel_count = pixels.shape
    half = images // 2

    def kernel(where_ref, mask_ref, pixel_ref, kernel_ref, *outs):
        band = where_ref[0]

        def body(q):
            for c, order in enumerate(orders):
                image = band ^ relative_index(q + half * upper, order)
                scale = mask_ref[image, band].astype(f32)
                product = jnp.dot(
                    pixel_ref[image], kernel_ref[:, span(c)], preferred_element_type=f32
                )
                outs[c][q] = (product * scale).astype(bf16)

        loop(half, body)

    return local_call(
        kernel,
        where,
        [mask],
        [pixels, kernels],
        [jax.ShapeDtypeStruct((half, patches, LANES), bf16)] * 3,
        name="embed_part",
        flops=images * patches * pixel_count * 3 * LANES,
    )


def kernel_grad(upper, orders, where, mask, pixels, grads, total, bias):
    images, patches, pixel_count = pixels.shape
    half = images // 2
    piece = pixel_count // images
    width = 3 * LANES

    def kernel(where_ref, mask_ref, pixel_ref, *refs):
        band = where_ref[0]
        grad_refs = refs[:3]
        if upper:
            old_total, old_bias, out_ref, total_ref, bias_ref = refs[3:]
            total_ref[...] = old_total[...]
            bias_ref[...] = old_bias[...]
        else:
            total_ref, bias_ref = refs[3:]
            total_ref[...] = jnp.zeros_like(total_ref)
            bias_ref[...] = jnp.zeros_like(bias_ref)

        def body(q):
            for c, order in enumerate(orders):
                image = band ^ relative_index(q + half * upper, order)

                @pl.when(mask_ref[image, band] != 0)
                def _(c=c, image=image):
                    grad = grad_refs[c][q]
                    total_ref[span(c), :] += contract_first(grad, pixel_ref[image])
                    bias_ref[:, span(c)] += jnp.sum(grad.astype(f32), axis=0, keepdims=True)

        loop(half, body)
        if upper:
            high = bias_ref[...].astype(bf16)
            low = (bias_ref[...] - high.astype(f32)).astype(bf16)
            whole = total_ref[...].T.astype(bf16)
            for k in range(images):
                out_ref[k, :piece, :] = whole[k * piece : (k + 1) * piece]
                out_ref[k, piece : piece + 1, :] = high
                out_ref[k, piece + 1 : piece + 2, :] = low

    accumulators = [
        jax.ShapeDtypeStruct((width, pixel_count), f32),
        jax.ShapeDtypeStruct((1, width), f32),
    ]
    flops = images * patches * pixel_count * width
    if not upper:
        return local_call(
            kernel, where, [mask], [pixels, *grads], accumulators, name="kernel_grad", flops=flops
        )
    return local_call(
        kernel,
        where,
        [mask],
        [pixels, *grads, total, bias],
        [jax.ShapeDtypeStruct((images, piece + 2, width), bf16)],
        scratch=[pltpu.VMEM(s.shape, f32) for s in accumulators],
        name="kernel_grad_end",
        flops=flops,
    )[0]


def pixel_grad(orders, where, mask, early, late, kernels):
    half, patches, _ = early[0].shape
    pixel_count = kernels.shape[0]

    def kernel(where_ref, mask_ref, *refs):
        early_refs, late_refs, kernel_ref, outs = refs[:3], refs[3:6], refs[6], refs[7:]
        band, head = where_ref[0], where_ref[1]

        def body(q):
            for side in range(2):
                first = head if side == 0 else 1 - head
                image = first * half + q
                parts = []
                for c, order in enumerate(orders):
                    position = position_of(image ^ band, order)
                    low = jnp.minimum(position, half - 1)
                    high = jnp.maximum(position - half, 0)
                    parts.append(
                        jnp.where(position < half, early_refs[c][low], late_refs[c][high])
                    )
                total = contract_last(jnp.concatenate(parts, axis=1), kernel_ref[...])
                outs[side][q] = (total * mask_ref[image, band].astype(f32)).astype(bf16)

        loop(half, body)

    return local_call(
        kernel,
        where,
        [mask],
        [*early, *late, kernels],
        [jax.ShapeDtypeStruct((half, patches, pixel_count), bf16)] * 2,
        name="pixel_grad",
        flops=4 * half * patches * pixel_count * 3 * LANES,
    )


def row_products(orders, count, where, lefts, rights, portions, name):
    rows = lefts[0].shape[1] // count
    half = count // 2 * rows
    widths = [sum(piece[3] for piece in portion) for portion in portions]
    if rows % 16:
        keeps, sends = [], []
        for portion, order in zip(portions, orders):
            places = jnp.asarray([relative_index(p, order) for p in range(count)], jnp.int32)
            columns = ((where[0] ^ places) * rows)[:, None] + jnp.arange(rows, dtype=jnp.int32)
            select = jnp.arange(count * rows, dtype=jnp.int32)[:, None] == columns.reshape(1, -1)
            turned = [jnp.dot(left, select.astype(bf16)) for left in lefts]
            whole = jnp.concatenate(
                [contract_first(turned[i], rights[j][:, s : s + w]) for i, j, s, w in portion],
                axis=1,
            ).astype(bf16)
            keeps.append(whole[:half])
            sends.append(whole[half:])
        return keeps, sends
    uses = sorted({(piece[0], c) for c, portion in enumerate(portions) for piece in portion})

    def kernel(where_ref, *refs):
        left_refs = refs[: len(lefts)]
        right_refs = refs[len(lefts) : len(lefts) + len(rights)]
        outs = refs[len(lefts) + len(rights) : len(lefts) + len(rights) + 2 * len(portions)]
        turned_refs = refs[-len(uses) - len(lefts) : -len(uses)]
        ordered = dict(zip(uses, refs[-len(uses) :]))
        band = where_ref[0]
        for left_ref, turned_ref in zip(left_refs, turned_refs):
            turned_ref[...] = left_ref[...].T
        for (i, c), ordered_ref in ordered.items():
            for p in range(count):
                block = (band ^ relative_index(p, orders[c])) * rows
                ordered_ref[p * rows : (p + 1) * rows, :] = turned_refs[i][
                    pl.ds(pl.multiple_of(block, 16), rows), :
                ]
        for side in (1, 0):
            for c, portion in enumerate(portions):
                place = 0
                for i, j, start, width in portion:
                    left = ordered[i, c][side * half : (side + 1) * half, :]
                    for column in range(0, width, 256):
                        wide = min(256, width - column)
                        outs[2 * c + side][:, place : place + wide] = jnp.dot(
                            left,
                            right_refs[j][:, start + column : start + column + wide],
                            preferred_element_type=f32,
                        ).astype(bf16)
                        place += wide

    shapes = []
    for width in widths:
        shapes += [jax.ShapeDtypeStruct((half, width), bf16)] * 2
    turned = [pltpu.VMEM((left.shape[1], left.shape[0]), bf16) for left in lefts]
    ordered = [pltpu.VMEM((lefts[i].shape[1], lefts[i].shape[0]), bf16) for i, _ in uses]
    outs = local_call(
        kernel,
        where,
        [],
        [*lefts, *rights],
        shapes,
        scratch=turned + ordered,
        name=name,
        flops=2 * lefts[0].size * sum(widths),
    )
    return outs[0::2], outs[1::2]


def shards(
    pixels,
    band_mask,
    wave_ids,
    pos_embed,
    in_proj,
    out_proj,
    up_proj,
    down_proj,
    gain_one,
    gain_two,
    kernel_gen,
    bias_gen,
    wave_table,
    hyper_in,
    hyper_out,
    hyper_up,
    hyper_down,
    hyper_gain_one,
    hyper_gain_two,
    cotangent,
):
    band_index = lax.axis_index("band")
    head_index = lax.axis_index("head")
    count = lax.axis_size("band")
    images, slot_local, patches, pixel_count = pixels.shape
    model_width = in_proj.shape[1]
    half_width = in_proj.shape[2]
    wave_count, hyper_width = wave_table.shape
    assert images == count and slot_local == 1
    orders = gather_orders(count)
    where = jnp.stack([band_index, head_index]).astype(jnp.int32)
    pixels = pixels.reshape(images, patches, pixel_count)

    gen_rows = kernel_gen.reshape(-1, half_width)
    hyper_weights = [hyper_in, hyper_out, hyper_up, hyper_down]
    hyper_gains = [hyper_gain_one[None], hyper_gain_two[None]]
    slot_piece, image_bias, mix_low, *hyper_kept = hyper_forward(
        where,
        wave_ids,
        band_mask,
        wave_table,
        hyper_weights,
        hyper_gains,
        gen_rows,
        bias_gen,
        count,
    )
    slot_piece = slot_piece.reshape(count, -1, half_width)
    kernels = lax.all_to_all(slot_piece, "band", 0, 0, tiled=True).reshape(pixel_count, half_width)

    sends = embed_part(1, orders, where, band_mask, pixels, kernels)
    arriving = [hop(send, order[-1]) for send, order in zip(sends, orders)]
    keeps = embed_part(0, orders, where, band_mask, pixels, kernels)
    embed_half = jnp.concatenate(
        [part[0] for part in scatter_sum(keeps, None, orders, arriving)], axis=1
    )
    embed_low = (embed_half + image_bias).astype(bf16)
    gain_one = gain_one[None]
    gain_two = gain_two[None]
    tokens, normed_low, query, key, value, probs, attended, attn_part = attention_forward(
        where, embed_low, swap(embed_low), pos_embed, gain_one, in_proj, out_proj
    )
    grad_low = cotangent[0]
    mid_stream, second_low, active_low, grad_hidden, ff_parts = feed_forward(
        where, tokens, attn_part, swap(attn_part), gain_two, up_proj, down_proj, grad_low
    )
    ff_other = swap(ff_parts)

    ff_local = up_proj.shape[1]
    third = ff_local * 2 // 3
    ff_keeps, ff_sends = row_products(
        orders,
        count,
        where,
        [second_low, grad_low],
        [grad_hidden, active_low],
        [
            [(0, 0, 0, third)],
            [(0, 0, third, ff_local - third), (1, 1, 0, 2 * third - ff_local)],
            [(1, 1, 2 * third - ff_local, third)],
        ],
        "ff_grads",
    )
    ff_sends, ff_other = lax.optimization_barrier((ff_sends, ff_other))
    ff_arriving = [hop(send, order[-1]) for send, order in zip(ff_sends, orders)]

    layer_out, gain_two_grad, grad_mid, grad_mid_low, *grad_projected, normed_part = (
        attention_backward(
            where,
            mid_stream,
            ff_parts,
            ff_other,
            grad_low,
            gain_two,
            in_proj,
            out_proj,
            query,
            key,
            value,
            probs,
        )
    )
    grad_embed_half, small = token_grad(
        where, tokens, grad_mid, normed_part, swap(normed_part), gain_one, gain_two_grad
    )

    first = hop(grad_embed_half, orders[0][0])
    early, late = [], []
    for c, order in enumerate(orders):
        block = jnp.stack([grad_embed_half[:, span(c)], first[:, span(c)]])
        for step in order[1:-1]:
            block = jnp.concatenate([block, hop(block, step)], axis=0)
        early.append(block)
        late.append(hop(block, order[-1]))
    total, bias = kernel_grad(0, orders, where, band_mask, pixels, early, None, None)
    blocks = kernel_grad(1, orders, where, band_mask, pixels, late, total, bias)
    own_pixels, other_pixels = pixel_grad(orders, where, band_mask, early, late, kernels)
    grad_pixels = (own_pixels.astype(f32) + swap(other_pixels).astype(f32)).astype(bf16)
    grad_pixels = grad_pixels[:, None]

    blocks = lax.all_to_all(blocks, "band", 0, 0, tiled=True)
    grad_mix, wave_kernels, wave_biases = mix_grad(
        where, wave_ids, blocks, gen_rows, bias_gen, wave_count, count
    )
    grad_kernel_gen, grad_bias_gen = generator_grads(where, mix_low, wave_kernels, wave_biases)
    grad_mix = grad_mix + swap(grad_mix)
    step = 1
    while step < count:
        if step * 4 <= count:
            grad_mix = (grad_mix + hop(grad_mix, step)) + (
                hop(grad_mix, 2 * step) + hop(grad_mix, 3 * step)
            )
            step *= 4
        else:
            grad_mix = grad_mix + hop(grad_mix, step)
            step *= 2
    hyper_grads = hyper_backward(
        where, grad_mix, wave_table, hyper_weights, hyper_gains, hyper_kept
    )

    at_keeps, at_sends = row_products(
        orders,
        count,
        where,
        [normed_low, grad_mid_low, small],
        [*grad_projected, attended, jnp.eye(EXTRA, dtype=bf16)],
        [
            [(0, 0, 0, half_width), (0, 1, 0, 256)],
            [(0, 1, 256, half_width - 256), (0, 2, 0, half_width), (1, 3, 0, 128)],
            [(1, 3, 128, half_width - 128), (2, 4, 0, EXTRA)],
        ],
        "attention_grads",
    )
    ff_keeps, ff_arriving, at_sends, _ = lax.optimization_barrier(
        (ff_keeps, ff_arriving, at_sends, late)
    )
    ff_sums = jnp.concatenate(scatter_sum(ff_keeps, None, orders, ff_arriving), axis=1)
    at_sums = jnp.concatenate(scatter_sum(at_keeps, at_sends, orders), axis=1)
    grad_up, grad_down = ff_sums[:, :ff_local], ff_sums[:, ff_local:]
    grad_in_proj = jnp.stack(
        [at_sums[:, i * half_width : (i + 1) * half_width] for i in range(3)]
    )
    grad_out_proj = at_sums[:, 3 * half_width : 4 * half_width].T
    tail = at_sums[:, 4 * half_width :].T
    return (
        layer_out[None],
        grad_pixels,
        tail[:patches],
        grad_in_proj,
        grad_out_proj,
        grad_up,
        grad_down.T,
        tail[patches],
        tail[patches + 1],
        grad_kernel_gen.reshape(kernel_gen.shape),
        grad_bias_gen,
        *hyper_grads[:5],
        hyper_grads[5][0],
        hyper_grads[6][0],
    )


def solution(mesh):
    in_specs = (
        P(None, "band", None, None),
        P(),
        P(),
        P(),
        P(None, None, "head"),
        P("head", None),
        P(None, "head"),
        P("head", None),
        P(),
        P(),
        P(None, "band", "head"),
        P(None, "head"),
        P(),
        P(),
        P(),
        P(),
        P(),
        P(),
        P(),
        P("band", None, None),
    )
    out_specs = (
        P("band", None, None),
        P("head", "band", None, None),
        P(None, "band"),
        P(None, "band", "head"),
        P("head", "band"),
        P("band", "head"),
        P("head", "band"),
        P("band"),
        P("band"),
        P(None, "band", "head"),
        P(None, "head"),
        P(),
        P(),
        P(),
        P(),
        P(),
        P(),
        P(),
    )
    return jax.shard_map(shards, mesh=mesh, in_specs=in_specs, out_specs=out_specs, check_vma=False)
```

```python
import jax
import jax.numpy as jnp
import numpy as np
from jax import lax
from jax.experimental import pallas as pl
from jax.experimental.pallas import tpu as pltpu
from jax.sharding import PartitionSpec as P

HS = 64
HHEADS = 4
LANES = 128
EXTRA = 256
PART = 208

highest = lax.Precision.HIGHEST
norm_epsilon = 1e-06
score_scale = 0.125
root_half = 0.7071067811865476
density_scale = 0.3989422804014327
f32 = jnp.float32
bf16 = jnp.bfloat16


def norm_parts(values):
    centered = values - jnp.mean(values, axis=-1, keepdims=True)
    variance = jnp.mean(centered * centered, axis=-1, keepdims=True)
    scale = lax.rsqrt(variance + norm_epsilon)
    return centered * scale, scale


def norm_grad(grad, normal, scale):
    inner = jnp.mean(grad, axis=-1, keepdims=True)
    along = jnp.mean(grad * normal, axis=-1, keepdims=True)
    return scale * (grad - inner - normal * along)


def gelu_parts(values):
    cumulative = 0.5 * (1.0 + lax.erf(values * root_half))
    density = jnp.exp(-0.5 * values * values) * density_scale
    return cumulative, cumulative + values * density


def contract_first(left, right):
    return lax.dot_general(left, right, (((0,), (0,)), ((), ())), preferred_element_type=f32)


def contract_last(left, right):
    return lax.dot_general(left, right, (((1,), (1,)), ((), ())), preferred_element_type=f32)


def exact(left, right, dims=((1,), (0,))):
    return lax.dot_general(
        left, right, (dims, ((), ())), precision=highest, preferred_element_type=f32
    )


FIRST = ((0,), (0,))
LAST = ((1,), (1,))


def low_dot(left, right):
    return jnp.dot(left, right, preferred_element_type=f32)


def equal_index(rows, columns, row_shift, column_shift, row_mask, column_mask):
    row = lax.broadcasted_iota(jnp.int32, (rows, columns), 0)
    column = lax.broadcasted_iota(jnp.int32, (rows, columns), 1)
    return ((row >> row_shift) & row_mask) == ((column >> column_shift) & column_mask)


def onehot_of(wave_column, wave_count):
    slots = wave_column.shape[0]
    return wave_column == lax.broadcasted_iota(jnp.int32, (slots, wave_count), 1)


def spread(mix, piece):
    rows, width = mix.shape
    shift = piece.bit_length() - 1
    all_bits = 2**30 - 1
    repeat_rows = equal_index(rows * piece, rows, shift, 0, all_bits, all_bits)
    repeat_columns = equal_index(width, width * piece, 0, shift, all_bits, all_bits)
    tall = low_dot(repeat_rows.astype(bf16), mix).astype(bf16)
    return low_dot(tall, repeat_columns.astype(bf16))


def kron_identity(mix, piece):
    rows, width = mix.shape
    same = equal_index(rows * piece, width * piece, 0, 0, piece - 1, piece - 1)
    return jnp.where(same, spread(mix, piece), 0.0).astype(bf16)


def head_lanes(width, head_size, head):
    lane = lax.broadcasted_iota(jnp.int32, (1, width), 1)
    return (lane >> (head_size.bit_length() - 1)) == head


def hop(values, step):
    count = lax.axis_size("band")
    return lax.ppermute(values, "band", [(i, i ^ step) for i in range(count)])


def swap(values):
    return lax.ppermute(values, "head", [(0, 1), (1, 0)])


def head_sum(part):
    low = part.astype(bf16)
    return low.astype(f32) + swap(low).astype(f32)


def gather_orders(count):
    steps = []
    step = count // 2
    while step:
        steps.append(step)
        step //= 2
    if len(steps) < 4:
        return [tuple(steps)] * 3
    head, (c, b, a) = tuple(steps[:-3]), steps[-3:]
    return [head + (c, b, a), head + (a, c, b), head + (b, a, c)]


def relative_index(position, order):
    index = 0
    for t, step in enumerate(order):
        index = index + ((position >> t) & 1) * step
    return index


def position_of(index, order):
    position = 0
    for t, step in enumerate(order):
        position = position + (((index >> (step.bit_length() - 1)) & 1) << t)
    return position


def scatter_sum(keeps, sends, orders, arriving=None):
    if arriving is None:
        arriving = [hop(send, order[-1]) for send, order in zip(sends, orders)]
    for t in range(len(orders[0]) - 2, -1, -1):
        sends, kept = [], []
        for k, a in zip(keeps, arriving):
            half = k.shape[0] // 2
            sends.append((k[half:].astype(f32) + a[half:].astype(f32)).astype(bf16))
            kept.append(k[:half].astype(f32) + a[:half].astype(f32))
        keeps = kept
        if t == 0 and len({order[0] for order in orders}) == 1:
            merged = hop(jnp.concatenate(sends, axis=-1), orders[0][0])
            arriving, start = [], 0
            for send in sends:
                arriving.append(merged[..., start : start + send.shape[-1]])
                start += send.shape[-1]
        else:
            arriving = [hop(send, order[t]) for send, order in zip(sends, orders)]
    return [k.astype(f32) + a.astype(f32) for k, a in zip(keeps, arriving)]


def loop(count, body):
    if count <= 16:
        for q in range(count):
            body(q)
    else:

        def step(q, carry):
            body(q)
            return carry

        lax.fori_loop(0, count, step, 0)


def span(c):
    return slice(c * LANES, (c + 1) * LANES)


def local_call(
    kernel, where, tables, args, out_shape, scratch=(), name=None, flops=0, mebibytes=24
):
    vmem = pl.BlockSpec(memory_space=pltpu.VMEM)
    smem = pl.BlockSpec(memory_space=pltpu.SMEM)
    moved = sum(x.size * x.dtype.itemsize for x in args)
    moved += sum(int(np.prod(s.shape)) * s.dtype.itemsize for s in out_shape)
    return pl.pallas_call(
        kernel,
        in_specs=[smem] * (1 + len(tables)) + [vmem] * len(args),
        out_specs=[vmem] * len(out_shape),
        out_shape=list(out_shape),
        scratch_shapes=list(scratch),
        cost_estimate=pl.CostEstimate(flops=flops, bytes_accessed=moved, transcendentals=0),
        compiler_params=pltpu.CompilerParams(vmem_limit_bytes=mebibytes * 2**20),
        name=name,
    )(where, *tables, *args)


def hyper_forward(where, wave_ids, band_mask, table, weights, gains, gen_rows, bias_gen, count):
    slots = wave_ids.shape[0]
    wave_count, width = table.shape
    piece = gen_rows.shape[0] // width
    half_width = gen_rows.shape[1]
    inner = weights[2].shape[1]
    head_size = width // HHEADS

    def kernel(
        where_ref, ids_ref, mask_ref, table_ref, in_ref, out_ref, up_ref, down_ref, one_ref,
        two_ref, gen_ref, bias_ref, piece_out, image_bias_out, mix_out, projected_out, probs_out,
        attended_out, normal_one_out, scale_one_out, hidden_out, normal_two_out, scale_two_out,
    ):
        values = table_ref[...]
        projected = exact(values, in_ref[...])
        projected_out[...] = projected
        query, key, value = (projected[:, i * width : (i + 1) * width] for i in range(3))
        attended = jnp.zeros((wave_count, width), f32)
        for head in range(HHEADS):
            lanes = head_lanes(width, head_size, head)
            scores = exact(jnp.where(lanes, query, 0.0), key, LAST) * head_size ** (-0.5)
            scores = jnp.exp(scores - jnp.max(scores, axis=-1, keepdims=True))
            probs = scores / jnp.sum(scores, axis=-1, keepdims=True)
            probs_out[head] = probs
            attended += exact(probs, jnp.where(lanes, value, 0.0))
        attended_out[...] = attended
        normal_one, scale_one = norm_parts(values + exact(attended, out_ref[...]))
        first = normal_one * one_ref[...]
        hidden = exact(first, up_ref[...])
        factor, _ = gelu_parts(hidden)
        normal_two, scale_two = norm_parts(first + exact(hidden * factor, down_ref[...]))
        mix = (normal_two * two_ref[...]).astype(bf16)
        normal_one_out[...] = normal_one
        scale_one_out[...] = scale_one
        hidden_out[...] = hidden
        normal_two_out[...] = normal_two
        scale_two_out[...] = scale_two
        mix_out[...] = mix
        onehot = onehot_of(ids_ref[...], wave_count)
        slot_mix = low_dot(onehot.astype(bf16), mix).astype(bf16)
        piece_out[...] = low_dot(kron_identity(slot_mix, piece), gen_ref[...]).astype(bf16)
        image = lax.broadcasted_iota(jnp.int32, mask_ref.shape, 0) == where_ref[0]
        bands = jnp.sum(jnp.where(image, mask_ref[...], 0).astype(f32), axis=0, keepdims=True)
        waves = exact(bands, onehot.astype(f32))
        image_bias_out[...] = exact(waves, low_dot(mix, bias_ref[...]))

    def shape(*dims):
        return jax.ShapeDtypeStruct(dims, f32)

    return local_call(
        kernel,
        where,
        [],
        [wave_ids, band_mask, table, *weights, *gains, gen_rows, bias_gen],
        [
            jax.ShapeDtypeStruct((slots * piece, half_width), bf16),
            shape(1, half_width),
            jax.ShapeDtypeStruct((wave_count, width), bf16),
            shape(wave_count, 3 * width),
            shape(HHEADS, wave_count, wave_count),
            shape(wave_count, width),
            shape(wave_count, width),
            shape(wave_count, 1),
            shape(wave_count, inner),
            shape(wave_count, width),
            shape(wave_count, 1),
        ],
        name="hyper_forward",
        mebibytes=56,
        flops=8 * slots * piece * gen_rows.size,
    )


def hyper_backward(where, grad_mix, table, weights, gains, kept):
    wave_count, width = table.shape
    head_size = width // HHEADS

    def kernel(
        where_ref, grad_ref, table_ref, in_ref, out_ref, up_ref, down_ref, one_ref, two_ref,
        projected_ref, probs_ref, attended_ref, normal_one_ref, scale_one_ref, hidden_ref,
        normal_two_ref, scale_two_ref, table_out, in_out, out_out, up_out, down_out, one_out,
        two_out,
    ):
        grad = jnp.sum(grad_ref[...], axis=0)
        normal_two = normal_two_ref[...]
        two_out[...] = jnp.sum(grad * normal_two, axis=0, keepdims=True)
        grad_two = norm_grad(grad * two_ref[...], normal_two, scale_two_ref[...])
        hidden = hidden_ref[...]
        factor, slope = gelu_parts(hidden)
        normal_one = normal_one_ref[...]
        first = normal_one * one_ref[...]
        grad_hidden = exact(grad_two, down_ref[...], LAST) * slope
        down_out[...] = exact(hidden * factor, grad_two, FIRST)
        up_out[...] = exact(first, grad_hidden, FIRST)
        grad_first = grad_two + exact(grad_hidden, up_ref[...], LAST)
        one_out[...] = jnp.sum(grad_first * normal_one, axis=0, keepdims=True)
        grad_one = norm_grad(grad_first * one_ref[...], normal_one, scale_one_ref[...])
        out_out[...] = exact(attended_ref[...], grad_one, FIRST)
        grad_attended = exact(grad_one, out_ref[...], LAST)
        projected = projected_ref[...]
        query, key, value = (projected[:, i * width : (i + 1) * width] for i in range(3))
        grads = [jnp.zeros((wave_count, width), f32) for _ in range(3)]
        for head in range(HHEADS):
            lanes = head_lanes(width, head_size, head)
            own = jnp.where(lanes, grad_attended, 0.0)
            probs = probs_ref[head]
            grad_probs = exact(own, value, LAST)
            grads[2] += exact(probs, own, FIRST)
            scores = probs * (grad_probs - jnp.sum(grad_probs * probs, axis=-1, keepdims=True))
            scores = scores * head_size ** (-0.5)
            grads[0] += exact(scores, jnp.where(lanes, key, 0.0))
            grads[1] += exact(scores, jnp.where(lanes, query, 0.0), FIRST)
        grad_projected = jnp.concatenate(grads, axis=1)
        in_out[...] = exact(table_ref[...], grad_projected, FIRST)
        table_out[...] = grad_one + exact(grad_projected, in_ref[...], LAST)

    arrays = [table, *weights, *gains]
    return local_call(
        kernel,
        where,
        [],
        [grad_mix, *arrays, *kept],
        [jax.ShapeDtypeStruct(a.shape, f32) for a in arrays],
        name="hyper_backward",
        flops=80 * wave_count * weights[2].size,
    )


def attention_forward(where, own, other, pos, gain, in_proj, out_proj):
    patches, half_width = own.shape
    width = 2 * half_width
    heads = half_width // HS

    def kernel(
        where_ref, own_ref, other_ref, pos_ref, gain_ref, in_ref, out_ref, tokens_out, normed_out,
        query_out, key_out, value_out, probs_out, attended_out, part_out,
    ):
        own_half, other_half = own_ref[...].astype(f32), other_ref[...].astype(f32)
        first = where_ref[1] == 0
        embed = jnp.concatenate(
            [jnp.where(first, own_half, other_half), jnp.where(first, other_half, own_half)], axis=1
        )
        tokens = embed + pos_ref[...].astype(f32)
        tokens_out[...] = tokens
        normal, _ = norm_parts(tokens)
        normed = (normal * gain_ref[...].astype(f32)).astype(bf16)
        normed_out[...] = normed
        projected = [low_dot(normed, in_ref[j]).astype(bf16) for j in range(3)]
        query_out[...], key_out[...], value_out[...] = projected
        for pair in range(heads // 2):
            lanes = slice(pair * 2 * HS, (pair + 1) * 2 * HS)
            query, key, value = (p[:, lanes] for p in projected)
            total = None
            for side in range(2):
                mine = head_lanes(2 * HS, HS, side)
                scores = contract_last(jnp.where(mine, query, 0), key) * score_scale
                scores = jnp.exp(scores - jnp.max(scores, axis=-1, keepdims=True))
                probs = scores / jnp.sum(scores, axis=-1, keepdims=True)
                probs_out[2 * pair + side] = probs
                part = low_dot(probs.astype(bf16), jnp.where(mine, value, 0))
                total = part if total is None else total + part
            attended_out[:, lanes] = total.astype(bf16)
        part_out[...] = low_dot(attended_out[...], out_ref[...]).astype(bf16)

    def low(*dims):
        return jax.ShapeDtypeStruct(dims, bf16)

    return local_call(
        kernel,
        where,
        [],
        [own, other, pos, gain, in_proj, out_proj],
        [
            jax.ShapeDtypeStruct((patches, width), f32),
            low(patches, width),
            low(patches, half_width),
            low(patches, half_width),
            low(patches, half_width),
            jax.ShapeDtypeStruct((heads, patches, patches), f32),
            low(patches, half_width),
            low(patches, width),
        ],
        name="attention_forward",
        flops=2 * patches * (in_proj.size + out_proj.size + 4 * patches * half_width),
    )


def feed_forward(where, tokens, own, other, gain, up, down, cotangent):
    patches, width = tokens.shape
    local = up.shape[1]
    tile = local // 3

    def kernel(
        where_ref, tokens_ref, own_ref, other_ref, gain_ref, up_ref, down_ref, cotangent_ref,
        mid_out, second_out, active_out, grad_hidden_out, parts_out,
    ):
        mid = tokens_ref[...] + (own_ref[...].astype(f32) + other_ref[...].astype(f32))
        mid_out[...] = mid
        normal, _ = norm_parts(mid)
        second = (normal * gain_ref[...].astype(f32)).astype(bf16)
        second_out[...] = second
        for t in range(3):
            columns = slice(t * tile, (t + 1) * tile)
            hidden = low_dot(second, up_ref[:, columns])
            factor, slope = gelu_parts(hidden)
            active_out[:, columns] = (hidden * factor).astype(bf16)
            grad_active = contract_last(cotangent_ref[...], down_ref[columns, :])
            grad_hidden_out[:, columns] = (grad_active * slope).astype(bf16)
        parts_out[:patches, :] = low_dot(active_out[...], down_ref[...]).astype(bf16)
        parts_out[PART : PART + patches, :] = contract_last(
            grad_hidden_out[...], up_ref[...]
        ).astype(bf16)

    return local_call(
        kernel,
        where,
        [],
        [tokens, own, other, gain, up, down, cotangent],
        [
            jax.ShapeDtypeStruct((patches, width), f32),
            jax.ShapeDtypeStruct((patches, width), bf16),
            jax.ShapeDtypeStruct((patches, local), bf16),
            jax.ShapeDtypeStruct((patches, local), bf16),
            jax.ShapeDtypeStruct((PART + patches, width), bf16),
        ],
        name="feed_forward",
        flops=8 * patches * up.size,
    )


def attention_backward(
    where, mid, own, other, cotangent, gain, in_proj, out_proj, query, key, value, probs
):
    patches, width = mid.shape
    half_width = width // 2
    heads = half_width // HS

    def kernel(
        where_ref, mid_ref, own_ref, other_ref, cotangent_ref, gain_ref, in_ref, out_ref,
        query_ref, key_ref, value_ref, probs_ref, layer_out, gain_out, grad_mid_out, low_out,
        query_out, key_out, value_out, part_out,
    ):
        mid_values = mid_ref[...]
        down = own_ref[:patches, :].astype(f32) + other_ref[:patches, :].astype(f32)
        layer_out[...] = (mid_values + down).astype(bf16)
        back = slice(PART, PART + patches)
        grad_second = own_ref[back, :].astype(f32) + other_ref[back, :].astype(f32)
        normal, scale = norm_parts(mid_values)
        gain_out[...] = jnp.sum(grad_second * normal, axis=0, keepdims=True)
        grad_mid = cotangent_ref[...].astype(f32) + norm_grad(
            grad_second * gain_ref[...].astype(f32), normal, scale
        )
        grad_mid_out[...] = grad_mid
        grad_low = grad_mid.astype(bf16)
        low_out[...] = grad_low
        grad_attended = contract_last(grad_low, out_ref[...]).astype(bf16)
        for pair in range(heads // 2):
            lanes = slice(pair * 2 * HS, (pair + 1) * 2 * HS)
            query, key, value = query_ref[:, lanes], key_ref[:, lanes], value_ref[:, lanes]
            totals = [None] * 3
            for side in range(2):
                mine = head_lanes(2 * HS, HS, side)
                own_grad = jnp.where(mine, grad_attended[:, lanes], 0)
                probs = probs_ref[2 * pair + side]
                grad_probs = contract_last(own_grad, value)
                inner = jnp.sum(grad_probs * probs, axis=-1, keepdims=True)
                scores = (probs * (grad_probs - inner)).astype(bf16)
                parts = (
                    low_dot(scores, jnp.where(mine, key, 0)),
                    contract_first(scores, jnp.where(mine, query, 0)),
                    contract_first(probs.astype(bf16), own_grad),
                )
                totals = [p if t is None else t + p for t, p in zip(totals, parts)]
            query_out[:, lanes] = (totals[0] * score_scale).astype(bf16)
            key_out[:, lanes] = (totals[1] * score_scale).astype(bf16)
            value_out[:, lanes] = totals[2].astype(bf16)
        part = contract_last(query_out[...], in_ref[0])
        part += contract_last(key_out[...], in_ref[1])
        part += contract_last(value_out[...], in_ref[2])
        part_out[...] = part.astype(bf16)

    def low(*dims):
        return jax.ShapeDtypeStruct(dims, bf16)

    return local_call(
        kernel,
        where,
        [],
        [mid, own, other, cotangent, gain, in_proj, out_proj, query, key, value, probs],
        [
            low(patches, width),
            jax.ShapeDtypeStruct((1, width), f32),
            jax.ShapeDtypeStruct((patches, width), f32),
            low(patches, width),
            low(patches, half_width),
            low(patches, half_width),
            low(patches, half_width),
            low(patches, width),
        ],
        name="attention_backward",
        flops=2 * patches * (in_proj.size + out_proj.size + 8 * patches * half_width),
    )


def token_grad(where, tokens, grad_mid, own, other, gain, gain_two_grad):
    patches, width = tokens.shape
    half_width = width // 2

    def kernel(
        where_ref, tokens_ref, grad_mid_ref, own_ref, other_ref, gain_ref, two_ref, half_out,
        small_out,
    ):
        grad_normed = own_ref[...].astype(f32) + other_ref[...].astype(f32)
        normal, scale = norm_parts(tokens_ref[...])
        grad_one = jnp.sum(grad_normed * normal, axis=0, keepdims=True)
        grad = grad_mid_ref[...] + norm_grad(
            grad_normed * gain_ref[...].astype(f32), normal, scale
        )
        low = grad.astype(bf16)
        half_out[...] = jnp.where(where_ref[1] == 0, low[:, :half_width], low[:, half_width:])
        small_out[...] = jnp.zeros_like(small_out)
        small_out[:patches, :] = low
        small_out[patches : patches + 1, :] = grad_one.astype(bf16)
        small_out[patches + 1 : patches + 2, :] = two_ref[...].astype(bf16)

    return local_call(
        kernel,
        where,
        [],
        [tokens, grad_mid, own, other, gain, gain_two_grad],
        [
            jax.ShapeDtypeStruct((patches, half_width), bf16),
            jax.ShapeDtypeStruct((EXTRA, width), bf16),
        ],
        name="token_grad",
    )


def wave_grads(wave_column, blocks_ref, rows_ref, wave_count, piece):
    slots = wave_column.shape[0]
    for s in range(slots):
        rows_ref[s * piece : (s + 1) * piece, :] = blocks_ref[s, :piece, :]
    onehot = onehot_of(wave_column, wave_count)
    bits = 2**30 - 1
    shift = piece.bit_length() - 1
    tall = low_dot(
        equal_index(slots * piece, slots, shift, 0, bits, bits).astype(bf16), onehot.astype(bf16)
    ).astype(bf16)
    wide = low_dot(
        tall, equal_index(wave_count, wave_count * piece, 0, shift, bits, bits).astype(bf16)
    )
    same = equal_index(slots * piece, wave_count * piece, 0, 0, piece - 1, piece - 1)
    select = jnp.where(same, wide, 0.0).astype(bf16)
    kernels = contract_first(select, rows_ref[...]).astype(bf16)
    biases = jnp.concatenate(
        [
            blocks_ref[s, piece : piece + 1, :].astype(f32)
            + blocks_ref[s, piece + 1 : piece + 2, :].astype(f32)
            for s in range(slots)
        ],
        axis=0,
    )
    return kernels, exact(onehot.astype(f32), biases, FIRST)


def mix_grad(where, wave_ids, blocks, gen_rows, bias_gen, wave_count, count):
    width, half_width = bias_gen.shape
    piece = gen_rows.shape[0] // width

    def kernel(
        where_ref, ids_ref, blocks_ref, gen_ref, bias_ref, mix_out, kernels_out, biases_out, rows_ref
    ):
        kernels, biases = wave_grads(ids_ref[...], blocks_ref, rows_ref, wave_count, piece)
        kernels_out[...] = kernels
        biases_out[...] = biases
        products = contract_last(kernels, gen_ref[...])
        same = equal_index(*products.shape, 0, 0, piece - 1, piece - 1)
        products = jnp.where(same, products, 0.0)
        rows = jnp.sum(products.reshape(wave_count, piece, -1), axis=1)
        bits = 2**30 - 1
        gather = equal_index(
            width * piece, width, piece.bit_length() - 1, 0, bits, bits
        ).astype(f32)
        mix = exact(rows, gather)
        mix_out[...] = mix + exact(biases, bias_ref[...].astype(f32), LAST) * (1.0 / count)

    return local_call(
        kernel,
        where,
        [],
        [wave_ids, blocks, gen_rows, bias_gen],
        [
            jax.ShapeDtypeStruct((wave_count, width), f32),
            jax.ShapeDtypeStruct((wave_count * piece, half_width), bf16),
            jax.ShapeDtypeStruct((wave_count, half_width), f32),
        ],
        scratch=[pltpu.VMEM((wave_ids.shape[0] * piece, half_width), bf16)],
        name="mix_grad",
        flops=2 * wave_count * piece * gen_rows.size,
    )


def generator_grads(where, mix_low, kernels, biases):
    wave_count, width = mix_low.shape
    piece = kernels.shape[0] // wave_count
    half_width = kernels.shape[1]

    def kernel(where_ref, mix_ref, kernels_ref, biases_ref, gen_out, bias_out):
        mix = mix_ref[...]
        gen_out[...] = contract_first(kron_identity(mix, piece), kernels_ref[...])
        bias_out[...] = exact(mix.astype(f32), biases_ref[...], FIRST)

    return local_call(
        kernel,
        where,
        [],
        [mix_low, kernels, biases],
        [
            jax.ShapeDtypeStruct((width * piece, half_width), f32),
            jax.ShapeDtypeStruct((width, half_width), f32),
        ],
        name="generator_grads",
        flops=2 * wave_count * piece * width * piece * half_width,
    )


def embed_part(upper, orders, where, mask, pixels, kernels):
    images, patches, pixel_count = pixels.shape
    half = images // 2

    def kernel(where_ref, mask_ref, pixel_ref, kernel_ref, *outs):
        band = where_ref[0]

        def body(q):
            for c, order in enumerate(orders):
                image = band ^ relative_index(q + half * upper, order)
                scale = mask_ref[image, band].astype(f32)
                product = jnp.dot(
                    pixel_ref[image], kernel_ref[:, span(c)], preferred_element_type=f32
                )
                outs[c][q] = (product * scale).astype(bf16)

        loop(half, body)

    return local_call(
        kernel,
        where,
        [mask],
        [pixels, kernels],
        [jax.ShapeDtypeStruct((half, patches, LANES), bf16)] * 3,
        name="embed_part",
        flops=images * patches * pixel_count * 3 * LANES,
    )


def kernel_grad(upper, orders, where, mask, pixels, grads, total, bias):
    images, patches, pixel_count = pixels.shape
    half = images // 2
    piece = pixel_count // images
    width = 3 * LANES

    def kernel(where_ref, mask_ref, pixel_ref, *refs):
        band = where_ref[0]
        grad_refs = refs[:3]
        if upper:
            old_total, old_bias, out_ref, total_ref, bias_ref = refs[3:]
            total_ref[...] = old_total[...]
            bias_ref[...] = old_bias[...]
        else:
            total_ref, bias_ref = refs[3:]
            total_ref[...] = jnp.zeros_like(total_ref)
            bias_ref[...] = jnp.zeros_like(bias_ref)

        def body(q):
            for c, order in enumerate(orders):
                image = band ^ relative_index(q + half * upper, order)

                @pl.when(mask_ref[image, band] != 0)
                def _(c=c, image=image):
                    grad = grad_refs[c][q]
                    total_ref[span(c), :] += contract_first(grad, pixel_ref[image])
                    bias_ref[:, span(c)] += jnp.sum(grad.astype(f32), axis=0, keepdims=True)

        loop(half, body)
        if upper:
            high = bias_ref[...].astype(bf16)
            low = (bias_ref[...] - high.astype(f32)).astype(bf16)
            whole = total_ref[...].T.astype(bf16)
            for k in range(images):
                out_ref[k, :piece, :] = whole[k * piece : (k + 1) * piece]
                out_ref[k, piece : piece + 1, :] = high
                out_ref[k, piece + 1 : piece + 2, :] = low

    accumulators = [
        jax.ShapeDtypeStruct((width, pixel_count), f32),
        jax.ShapeDtypeStruct((1, width), f32),
    ]
    flops = images * patches * pixel_count * width
    if not upper:
        return local_call(
            kernel, where, [mask], [pixels, *grads], accumulators, name="kernel_grad", flops=flops
        )
    return local_call(
        kernel,
        where,
        [mask],
        [pixels, *grads, total, bias],
        [jax.ShapeDtypeStruct((images, piece + 2, width), bf16)],
        scratch=[pltpu.VMEM(s.shape, f32) for s in accumulators],
        name="kernel_grad_end",
        flops=flops,
    )[0]


def pixel_grad(orders, where, mask, early, late, kernels):
    half, patches, _ = early[0].shape
    pixel_count = kernels.shape[0]

    def kernel(where_ref, mask_ref, *refs):
        early_refs, late_refs, kernel_ref, outs = refs[:3], refs[3:6], refs[6], refs[7:]
        band, head = where_ref[0], where_ref[1]

        def body(q):
            for side in range(2):
                first = head if side == 0 else 1 - head
                image = first * half + q
                parts = []
                for c, order in enumerate(orders):
                    position = position_of(image ^ band, order)
                    low = jnp.minimum(position, half - 1)
                    high = jnp.maximum(position - half, 0)
                    parts.append(
                        jnp.where(position < half, early_refs[c][low], late_refs[c][high])
                    )
                total = contract_last(jnp.concatenate(parts, axis=1), kernel_ref[...])
                outs[side][q] = (total * mask_ref[image, band].astype(f32)).astype(bf16)

        loop(half, body)

    return local_call(
        kernel,
        where,
        [mask],
        [*early, *late, kernels],
        [jax.ShapeDtypeStruct((half, patches, pixel_count), bf16)] * 2,
        name="pixel_grad",
        flops=4 * half * patches * pixel_count * 3 * LANES,
    )


def row_products(orders, count, where, lefts, rights, portions, name, sides=(1, 0)):
    rows = lefts[0].shape[1] // count
    half = count // 2 * rows
    widths = [sum(piece[3] for piece in portion) for portion in portions]
    if rows % 16:
        keeps, sends = [], []
        for portion, order in zip(portions, orders):
            places = jnp.asarray([relative_index(p, order) for p in range(count)], jnp.int32)
            columns = ((where[0] ^ places) * rows)[:, None] + jnp.arange(rows, dtype=jnp.int32)
            select = jnp.arange(count * rows, dtype=jnp.int32)[:, None] == columns.reshape(1, -1)
            turned = [jnp.dot(left, select.astype(bf16)) for left in lefts]
            whole = jnp.concatenate(
                [contract_first(turned[i], rights[j][:, s : s + w]) for i, j, s, w in portion],
                axis=1,
            ).astype(bf16)
            keeps.append(whole[:half])
            sends.append(whole[half:])
        return [keeps, sends]
    uses = sorted({(piece[0], c) for c, portion in enumerate(portions) for piece in portion})

    def kernel(where_ref, *refs):
        left_refs = refs[: len(lefts)]
        right_refs = refs[len(lefts) : len(lefts) + len(rights)]
        outs = refs[len(lefts) + len(rights) :]
        turned_refs = refs[-len(uses) - len(lefts) : -len(uses)]
        ordered = dict(zip(uses, refs[-len(uses) :]))
        band = where_ref[0]
        for left_ref, turned_ref in zip(left_refs, turned_refs):
            turned_ref[...] = left_ref[...].T
        for (i, c), ordered_ref in ordered.items():
            for p in range(count):
                if p // (count // 2) not in sides:
                    continue
                block = (band ^ relative_index(p, orders[c])) * rows
                ordered_ref[p * rows : (p + 1) * rows, :] = turned_refs[i][
                    pl.ds(pl.multiple_of(block, 16), rows), :
                ]
        for side in sides:
            for c, portion in enumerate(portions):
                place = 0
                for i, j, start, width in portion:
                    left = ordered[i, c][side * half : (side + 1) * half, :]
                    for column in range(0, width, 256):
                        wide = min(256, width - column)
                        outs[sides.index(side) * len(portions) + c][:, place : place + wide] = jnp.dot(
                            left,
                            right_refs[j][:, start + column : start + column + wide],
                            preferred_element_type=f32,
                        ).astype(bf16)
                        place += wide

    shapes = [jax.ShapeDtypeStruct((half, width), bf16) for width in widths] * len(sides)
    turned = [pltpu.VMEM((left.shape[1], left.shape[0]), bf16) for left in lefts]
    ordered = [pltpu.VMEM((lefts[i].shape[1], lefts[i].shape[0]), bf16) for i, _ in uses]
    outs = local_call(
        kernel,
        where,
        [],
        [*lefts, *rights],
        shapes,
        scratch=turned + ordered,
        name=name,
        flops=len(sides) * lefts[0].size * sum(widths),
    )
    return [outs[i * len(portions) : (i + 1) * len(portions)] for i in range(len(sides))]


def merged_products(orders, where, lefts, rights, portions, ff_keeps, ff_arriving):
    count = 16
    rows = lefts[0].shape[1] // count
    quarter = 4 * rows
    widths = [sum(piece[3] for piece in portion) for portion in portions]
    ff_widths = [keep.shape[1] for keep in ff_keeps]
    turns = [orders[(c + 1) % 3] for c in range(3)]
    uses = sorted({(piece[0], c) for c, portion in enumerate(portions) for piece in portion})
    inputs = len(lefts) + len(rights)

    def kernel(where_ref, *refs):
        left_refs, right_refs = refs[: len(lefts)], refs[len(lefts) : inputs]
        keep_refs, arriving_refs = refs[inputs : inputs + 3], refs[inputs + 3 : inputs + 6]
        sends, keeps = refs[inputs + 6 : inputs + 9], refs[inputs + 9 : inputs + 12]
        turned_refs = refs[inputs + 12 : inputs + 12 + len(lefts)]
        ordered = dict(zip(uses, refs[inputs + 12 + len(lefts) :]))
        band = where_ref[0]
        for c in range(3):
            total = keep_refs[c][...].astype(f32) + arriving_refs[c][...].astype(f32)
            keeps[c][:, : ff_widths[c]] = total[:quarter].astype(bf16)
            sends[c][:, : ff_widths[c]] = total[quarter:].astype(bf16)
        for left_ref, turned_ref in zip(left_refs, turned_refs):
            turned_ref[...] = left_ref[...].T
        for (i, c), ordered_ref in ordered.items():
            for p in range(count):
                block = (band ^ relative_index(p, turns[c])) * rows
                ordered_ref[p * rows : (p + 1) * rows, :] = turned_refs[i][
                    pl.ds(pl.multiple_of(block, 16), rows), :
                ]
        for c, portion in enumerate(portions):
            place = 0
            for i, j, start, width in portion:
                for column in range(0, width, 256):
                    wide = min(256, width - column)
                    product = jnp.dot(
                        ordered[i, c][...],
                        right_refs[j][:, start + column : start + column + wide],
                        preferred_element_type=f32,
                    ).astype(bf16)
                    for k in range(4):
                        out = keeps[c] if k < 2 else sends[c]
                        at = ff_widths[c] + (k % 2) * widths[c] + place
                        out[:, at : at + wide] = product[k * quarter : (k + 1) * quarter]
                    place += wide

    shapes = [
        jax.ShapeDtypeStruct((quarter, f + 2 * w), bf16) for f, w in zip(ff_widths, widths)
    ] * 2
    outs = local_call(
        kernel,
        where,
        [],
        [*lefts, *rights, *ff_keeps, *ff_arriving],
        shapes,
        scratch=[pltpu.VMEM((left.shape[1], left.shape[0]), bf16) for left in lefts]
        + [pltpu.VMEM((lefts[i].shape[1], lefts[i].shape[0]), bf16) for i, _ in uses],
        name="attention_grads",
        flops=2 * lefts[0].size * sum(widths),
    )
    return outs[:3], outs[3:]


def second_sum(where, keeps, arriving, ff_widths, widths):
    quarter = keeps[0].shape[0]
    pair = quarter // 2

    def kernel(where_ref, *refs):
        keep_refs, arriving_refs, sends, kept = refs[:3], refs[3:6], refs[6:9], refs[9:12]
        for c in range(3):
            total = keep_refs[c][...].astype(f32) + arriving_refs[c][...].astype(f32)
            f, w = ff_widths[c], widths[c]
            kept[c][:, :f] = total[:pair, :f]
            sends[c][:, :f] = total[pair:, :f].astype(bf16)
            for k in range(2):
                rows = slice(k * pair, (k + 1) * pair)
                at = slice(f + k * w, f + (k + 1) * w)
                kept[c][:, at] = total[rows, f : f + w]
                sends[c][:, at] = total[rows, f + w : f + 2 * w].astype(bf16)

    shapes = [(pair, f + 2 * w) for f, w in zip(ff_widths, widths)]
    outs = local_call(
        kernel,
        where,
        [],
        [*keeps, *arriving],
        [jax.ShapeDtypeStruct(s, bf16) for s in shapes]
        + [jax.ShapeDtypeStruct(s, f32) for s in shapes],
        name="second_sum",
    )
    return outs[:3], outs[3:]


def third_sum(where, keeps, arriving, ff_widths, widths):
    pair = keeps[0].shape[0]
    rows = pair // 2
    ff_total = sum(ff_widths)

    def kernel(where_ref, *refs):
        keep_refs, arriving_refs = refs[:3], refs[3:6]
        ff_send, ff_kept, sends, kept = refs[6], refs[7], refs[8:11], refs[11:14]
        place = 0
        for c in range(3):
            total = keep_refs[c][...] + arriving_refs[c][...].astype(f32)
            f, w = ff_widths[c], widths[c]
            ff_kept[:, place : place + f] = total[:rows, :f]
            ff_send[:, place : place + f] = total[rows:, :f].astype(bf16)
            kept[c][...] = total[:, f : f + w]
            sends[c][...] = total[:, f + w :].astype(bf16)
            place += f

    outs = local_call(
        kernel,
        where,
        [],
        [*keeps, *arriving],
        [jax.ShapeDtypeStruct((rows, ff_total), bf16), jax.ShapeDtypeStruct((rows, ff_total), f32)]
        + [jax.ShapeDtypeStruct((pair, w), bf16) for w in widths]
        + [jax.ShapeDtypeStruct((pair, w), f32) for w in widths],
        name="third_sum",
    )
    return outs[0], outs[1], outs[2:5], outs[5:]


def fourth_sum(where, ff_kept, ff_arriving, keeps, arriving, large):
    rows = ff_kept.shape[0]
    widths = [keep.shape[1] for keep in keeps]
    half = ff_kept.shape[1] // 2
    rest = half - large

    def kernel(where_ref, *refs):
        ff_ref, ff_arriving_ref, keep_refs, arriving_refs = refs[0], refs[1], refs[2:5], refs[5:8]
        up_out, down_out, send, kept = refs[8:12]
        for k, out in enumerate((up_out, down_out)):
            for source, place, wide in ((k * large, 0, large), (2 * large + k * rest, large, rest)):
                at = slice(source, source + wide)
                out[:, place : place + wide] = ff_ref[:, at] + ff_arriving_ref[:, at].astype(f32)
        place = 0
        for c in range(3):
            total = keep_refs[c][...] + arriving_refs[c][...].astype(f32)
            at = slice(place, place + widths[c])
            kept[:, at] = total[:rows]
            send[:, at] = total[rows:].astype(bf16)
            place += widths[c]

    return local_call(
        kernel,
        where,
        [],
        [ff_kept, ff_arriving, *keeps, *arriving],
        [
            jax.ShapeDtypeStruct((rows, half), f32),
            jax.ShapeDtypeStruct((rows, half), f32),
            jax.ShapeDtypeStruct((rows, sum(widths)), bf16),
            jax.ShapeDtypeStruct((rows, sum(widths)), f32),
        ],
        name="fourth_sum",
    )


def after(values, *others):
    return lax.optimization_barrier((values, others))[0]


def shards(
    pixels,
    band_mask,
    wave_ids,
    pos_embed,
    in_proj,
    out_proj,
    up_proj,
    down_proj,
    gain_one,
    gain_two,
    kernel_gen,
    bias_gen,
    wave_table,
    hyper_in,
    hyper_out,
    hyper_up,
    hyper_down,
    hyper_gain_one,
    hyper_gain_two,
    cotangent,
):
    band_index = lax.axis_index("band")
    head_index = lax.axis_index("head")
    count = lax.axis_size("band")
    images, slot_local, patches, pixel_count = pixels.shape
    model_width = in_proj.shape[1]
    half_width = in_proj.shape[2]
    wave_count, hyper_width = wave_table.shape
    assert images == count and slot_local == 1
    orders = gather_orders(count)
    where = jnp.stack([band_index, head_index]).astype(jnp.int32)
    pixels = pixels.reshape(images, patches, pixel_count)

    gen_rows = kernel_gen.reshape(-1, half_width)
    hyper_weights = [hyper_in, hyper_out, hyper_up, hyper_down]
    hyper_gains = [hyper_gain_one[None], hyper_gain_two[None]]
    slot_piece, image_bias, mix_low, *hyper_kept = hyper_forward(
        where,
        wave_ids,
        band_mask,
        wave_table,
        hyper_weights,
        hyper_gains,
        gen_rows,
        bias_gen,
        count,
    )
    slot_piece = slot_piece.reshape(count, -1, half_width)
    kernels = lax.all_to_all(slot_piece, "band", 0, 0, tiled=True).reshape(pixel_count, half_width)

    sends = embed_part(1, orders, where, band_mask, pixels, kernels)
    arriving = [hop(send, order[-1]) for send, order in zip(sends, orders)]
    keeps = embed_part(0, orders, where, band_mask, pixels, kernels)
    embed_half = jnp.concatenate(
        [part[0] for part in scatter_sum(keeps, None, orders, arriving)], axis=1
    )
    embed_low = (embed_half + image_bias).astype(bf16)
    gain_one = gain_one[None]
    gain_two = gain_two[None]
    tokens, normed_low, query, key, value, probs, attended, attn_part = attention_forward(
        where, embed_low, swap(embed_low), pos_embed, gain_one, in_proj, out_proj
    )
    grad_low = cotangent[0]
    mid_stream, second_low, active_low, grad_hidden, ff_parts = feed_forward(
        where, tokens, attn_part, swap(attn_part), gain_two, up_proj, down_proj, grad_low
    )
    ff_other = swap(ff_parts)

    staged = count == 16
    ff_local = up_proj.shape[1]
    large = ff_local * 5 // 6
    small_part = ff_local - large
    ff_portions = [
        [(0, 0, 0, large)],
        [(1, 1, 0, large)],
        [(0, 0, large, small_part), (1, 1, large, small_part)],
    ]
    ff_lefts, ff_rights = [second_low, grad_low], [grad_hidden, active_low]
    ff_args = (orders, count, where)
    if staged:
        (ff_sends,) = row_products(
            *ff_args, ff_lefts, ff_rights, ff_portions, "ff_grads_send", (1,)
        )
        ff_other = after(ff_other, ff_sends)
    else:
        ff_keeps, ff_sends = row_products(*ff_args, ff_lefts, ff_rights, ff_portions, "ff_grads")
    ff_arriving = [hop(send, order[-1]) for send, order in zip(ff_sends, orders)]

    layer_out, gain_two_grad, grad_mid, grad_mid_low, *grad_projected, normed_part = (
        attention_backward(
            where,
            mid_stream,
            ff_parts,
            ff_other,
            grad_low,
            gain_two,
            in_proj,
            out_proj,
            query,
            key,
            value,
            probs,
        )
    )
    grad_embed_half, small = token_grad(
        where, tokens, grad_mid, normed_part, swap(normed_part), gain_one, gain_two_grad
    )

    if staged:
        ff_lefts = after(ff_lefts, grad_embed_half)
        (ff_keeps,) = row_products(
            *ff_args, ff_lefts, ff_rights, ff_portions, "ff_grads_keep", (0,)
        )
        grad_embed_half = after(grad_embed_half, ff_arriving[2])
    first = hop(grad_embed_half, orders[0][0])
    if staged:
        first = after(first, (ff_keeps, ff_arriving))
    at_portions = [
        [(0, 0, 0, half_width)],
        [(0, 1, 0, half_width)],
        [(0, 2, 0, half_width), (1, 3, 0, half_width), (2, 4, 0, EXTRA)],
    ]
    at_lefts = [normed_low, grad_mid_low, small]
    at_rights = [*grad_projected, attended, jnp.eye(EXTRA, dtype=bf16)]
    at_widths = [sum(piece[3] for piece in portion) for portion in at_portions]
    ff_widths = [sum(piece[3] for piece in portion) for portion in ff_portions]
    early, late = [], []
    for c, order in enumerate(orders):
        block = jnp.stack([grad_embed_half[:, span(c)], first[:, span(c)]])
        for step in order[1:-1]:
            block = jnp.concatenate([block, hop(block, step)], axis=0)
        early.append(block)
        late.append(hop(block, order[-1]))
    total, bias = kernel_grad(0, orders, where, band_mask, pixels, early, None, None)
    if staged:
        sends, keeps = merged_products(
            orders, where, after(at_lefts, early), at_rights, at_portions, ff_keeps, ff_arriving
        )
        sends, late, total = lax.optimization_barrier((sends, late, total))
        arriving = [hop(send, order[-2]) for send, order in zip(sends, orders)]
    blocks = kernel_grad(1, orders, where, band_mask, pixels, late, total, bias)
    spread_blocks = lax.all_to_all(blocks, "band", 0, 0, tiled=True)
    own_pixels, other_pixels = pixel_grad(orders, where, band_mask, early, late, kernels)
    if staged:
        arriving = after(arriving, (blocks, own_pixels))
        sends, keeps = second_sum(where, keeps, arriving, ff_widths, at_widths)
        arriving = [hop(send, order[-3]) for send, order in zip(sends, orders)]
        spread_blocks = after(spread_blocks, sends)
    grad_mix, wave_kernels, wave_biases = mix_grad(
        where, wave_ids, spread_blocks, gen_rows, bias_gen, wave_count, count
    )
    grad_mix = grad_mix + swap(grad_mix)
    grad_mix = jnp.broadcast_to(grad_mix[None], (count, *grad_mix.shape))
    grad_mix = lax.all_to_all(grad_mix, "band", 0, 0, tiled=True)
    if staged:
        arriving = after(arriving, grad_mix)
        ff_send, ff_kept, sends, keeps = third_sum(where, keeps, arriving, ff_widths, at_widths)
        ff_last = hop(ff_send, orders[0][0])
        arriving = [hop(send, orders[(c + 1) % 3][-3]) for c, send in enumerate(sends)]
        grad_mix = after(grad_mix, ff_send)
    hyper_grads = hyper_backward(
        where, grad_mix, wave_table, hyper_weights, hyper_gains, hyper_kept
    )
    grad_kernel_gen, grad_bias_gen = generator_grads(where, mix_low, wave_kernels, wave_biases)
    grad_pixels = (own_pixels.astype(f32) + swap(other_pixels).astype(f32)).astype(bf16)
    grad_pixels = grad_pixels[:, None]
    if staged:
        arriving = after(arriving, (hyper_grads[0], grad_bias_gen))
        grad_up, grad_down, send, kept = fourth_sum(
            where, ff_kept, ff_last, keeps, arriving, large
        )
        at_sums = kept + hop(send, orders[0][0]).astype(f32)
    else:
        at_keeps, at_sends = row_products(
            orders, count, where, at_lefts, at_rights, at_portions, "attention_grads"
        )
        up_sum, down_sum, both = scatter_sum(ff_keeps, None, orders, ff_arriving)
        grad_up = jnp.concatenate([up_sum, both[:, :small_part]], axis=1)
        grad_down = jnp.concatenate([down_sum, both[:, small_part:]], axis=1)
        at_sums = jnp.concatenate(scatter_sum(at_keeps, at_sends, orders), axis=1)
    grad_in_proj = jnp.stack(
        [at_sums[:, i * half_width : (i + 1) * half_width] for i in range(3)]
    )
    grad_out_proj = at_sums[:, 3 * half_width : 4 * half_width].T
    tail = at_sums[:, 4 * half_width :].T
    return (
        layer_out[None],
        grad_pixels,
        tail[:patches],
        grad_in_proj,
        grad_out_proj,
        grad_up,
        grad_down.T,
        tail[patches],
        tail[patches + 1],
        grad_kernel_gen.reshape(kernel_gen.shape),
        grad_bias_gen,
        *hyper_grads[:5],
        hyper_grads[5][0],
        hyper_grads[6][0],
    )


def solution(mesh):
    in_specs = (
        P(None, "band", None, None),
        P(),
        P(),
        P(),
        P(None, None, "head"),
        P("head", None),
        P(None, "head"),
        P("head", None),
        P(),
        P(),
        P(None, "band", "head"),
        P(None, "head"),
        P(),
        P(),
        P(),
        P(),
        P(),
        P(),
        P(),
        P("band", None, None),
    )
    out_specs = (
        P("band", None, None),
        P("head", "band", None, None),
        P(None, "band"),
        P(None, "band", "head"),
        P("head", "band"),
        P("band", "head"),
        P("head", "band"),
        P("band"),
        P("band"),
        P(None, "band", "head"),
        P(None, "head"),
        P(),
        P(),
        P(),
        P(),
        P(),
        P(),
        P(),
    )
    return jax.shard_map(shards, mesh=mesh, in_specs=in_specs, out_specs=out_specs, check_vma=False)
```

```python
import jax
import jax.numpy as jnp
import numpy as np
from jax import lax
from jax.experimental import pallas as pl
from jax.experimental.pallas import tpu as pltpu
from jax.sharding import PartitionSpec as P

HS = 64
HHEADS = 4
LANES = 128
EXTRA = 256
EARLY = 1024
HBM = pltpu.HBM
PART = 208

highest = lax.Precision.HIGHEST
norm_epsilon = 1e-06
score_scale = 0.125
root_half = 0.7071067811865476
density_scale = 0.3989422804014327
f32 = jnp.float32
bf16 = jnp.bfloat16


def norm_parts(values):
    centered = values - jnp.mean(values, axis=-1, keepdims=True)
    variance = jnp.mean(centered * centered, axis=-1, keepdims=True)
    scale = lax.rsqrt(variance + norm_epsilon)
    return centered * scale, scale


def norm_grad(grad, normal, scale):
    inner = jnp.mean(grad, axis=-1, keepdims=True)
    along = jnp.mean(grad * normal, axis=-1, keepdims=True)
    return scale * (grad - inner - normal * along)


def gelu_parts(values):
    cumulative = 0.5 * (1.0 + lax.erf(values * root_half))
    density = jnp.exp(-0.5 * values * values) * density_scale
    return cumulative, cumulative + values * density


def contract_first(left, right):
    return lax.dot_general(left, right, (((0,), (0,)), ((), ())), preferred_element_type=f32)


def contract_last(left, right):
    return lax.dot_general(left, right, (((1,), (1,)), ((), ())), preferred_element_type=f32)


def exact(left, right, dims=((1,), (0,))):
    def product(a, b):
        return lax.dot_general(a, b, (dims, ((), ())), preferred_element_type=f32)

    left_high, right_high = left.astype(bf16), right.astype(bf16)
    left_low = (left - left_high.astype(f32)).astype(bf16)
    right_low = (right - right_high.astype(f32)).astype(bf16)
    return product(left_high, right_high) + (
        product(left_high, right_low) + product(left_low, right_high)
    )


FIRST = ((0,), (0,))
LAST = ((1,), (1,))


def low_dot(left, right):
    return jnp.dot(left, right, preferred_element_type=f32)


def equal_index(rows, columns, row_shift, column_shift, row_mask, column_mask):
    row = lax.broadcasted_iota(jnp.int32, (rows, columns), 0)
    column = lax.broadcasted_iota(jnp.int32, (rows, columns), 1)
    return ((row >> row_shift) & row_mask) == ((column >> column_shift) & column_mask)


def onehot_of(ids_ref, wave_count):
    slots = ids_ref.shape[1]
    row = lax.broadcasted_iota(jnp.int32, (slots, wave_count), 0)
    waves = jnp.zeros((slots, wave_count), jnp.int32)
    for s in range(slots):
        waves = jnp.where(row == s, ids_ref[0, s], waves)
    return waves == lax.broadcasted_iota(jnp.int32, (slots, wave_count), 1)


def spread(mix, piece):
    rows, width = mix.shape
    shift = piece.bit_length() - 1
    all_bits = 2**30 - 1
    repeat_rows = equal_index(rows * piece, rows, shift, 0, all_bits, all_bits)
    repeat_columns = equal_index(width, width * piece, 0, shift, all_bits, all_bits)
    tall = low_dot(repeat_rows.astype(bf16), mix).astype(bf16)
    return low_dot(tall, repeat_columns.astype(bf16))


def kron_identity(mix, piece):
    rows, width = mix.shape
    same = equal_index(rows * piece, width * piece, 0, 0, piece - 1, piece - 1)
    return jnp.where(same, spread(mix, piece), 0.0).astype(bf16)


def head_lanes(width, head_size, head):
    lane = lax.broadcasted_iota(jnp.int32, (1, width), 1)
    return (lane >> (head_size.bit_length() - 1)) == head


def hop(values, step):
    count = lax.axis_size("band")
    return lax.ppermute(values, "band", [(i, i ^ step) for i in range(count)])


def swap(values):
    return lax.ppermute(values, "head", [(0, 1), (1, 0)])


def head_sum(part):
    low = part.astype(bf16)
    return low.astype(f32) + swap(low).astype(f32)


def gather_orders(count):
    steps = []
    step = count // 2
    while step:
        steps.append(step)
        step //= 2
    if len(steps) < 4:
        return [tuple(steps)] * 3
    head, (c, b, a) = tuple(steps[:-3]), steps[-3:]
    return [head + (c, b, a), head + (a, c, b), head + (b, a, c)]


def relative_index(position, order):
    index = 0
    for t, step in enumerate(order):
        index = index + ((position >> t) & 1) * step
    return index


def position_of(index, order):
    position = 0
    for t, step in enumerate(order):
        position = position + (((index >> (step.bit_length() - 1)) & 1) << t)
    return position


def scatter_sum(keeps, sends, orders, arriving=None):
    if arriving is None:
        arriving = [hop(send, order[-1]) for send, order in zip(sends, orders)]
    for t in range(len(orders[0]) - 2, -1, -1):
        sends, kept = [], []
        for k, a in zip(keeps, arriving):
            half = k.shape[0] // 2
            sends.append((k[half:].astype(f32) + a[half:].astype(f32)).astype(bf16))
            kept.append(k[:half].astype(f32) + a[:half].astype(f32))
        keeps = kept
        if t == 0 and len({order[0] for order in orders}) == 1:
            merged = hop(jnp.concatenate(sends, axis=-1), orders[0][0])
            arriving, start = [], 0
            for send in sends:
                arriving.append(merged[..., start : start + send.shape[-1]])
                start += send.shape[-1]
        else:
            arriving = [hop(send, order[t]) for send, order in zip(sends, orders)]
    return [k.astype(f32) + a.astype(f32) for k, a in zip(keeps, arriving)]


def loop(count, body):
    if count <= 16:
        for q in range(count):
            body(q)
    else:

        def step(q, carry):
            body(q)
            return carry

        lax.fori_loop(0, count, step, 0)


def span(c):
    return slice(c * LANES, (c + 1) * LANES)


def local_call(
    kernel, where, tables, args, out_shape, scratch=(), name=None, flops=0, mebibytes=24,
    spaces=None,
):
    vmem = pl.BlockSpec(memory_space=pltpu.VMEM)
    smem = pl.BlockSpec(memory_space=pltpu.SMEM)
    moved = sum(x.size * x.dtype.itemsize for x in args)
    moved += sum(int(np.prod(s.shape)) * s.dtype.itemsize for s in out_shape)
    return pl.pallas_call(
        kernel,
        in_specs=[smem] * (1 + len(tables)) + [vmem] * len(args),
        out_specs=[
            pl.BlockSpec(memory_space=space or pltpu.VMEM)
            for space in spaces or [None] * len(out_shape)
        ],
        out_shape=list(out_shape),
        scratch_shapes=list(scratch),
        cost_estimate=pl.CostEstimate(flops=flops, bytes_accessed=moved, transcendentals=0),
        compiler_params=pltpu.CompilerParams(vmem_limit_bytes=mebibytes * 2**20),
        name=name,
    )(where, *tables, *args)


def hyper_forward(where, wave_ids, band_mask, table, weights, gains, gen_rows, bias_gen, count):
    slots = wave_ids.shape[1]
    wave_count, width = table.shape
    piece = gen_rows.shape[0] // width
    half_width = gen_rows.shape[1]
    inner = weights[2].shape[1]
    head_size = width // HHEADS

    def kernel(
        where_ref, ids_ref, mask_ref, table_ref, in_ref, out_ref, up_ref, down_ref, one_ref,
        two_ref, gen_ref, bias_ref, piece_out, image_bias_out, mix_out, projected_out, probs_out,
        attended_out, normal_one_out, scale_one_out, hidden_out, normal_two_out, scale_two_out,
    ):
        values = table_ref[...]
        projected = exact(values, in_ref[...])
        projected_out[...] = projected
        query, key, value = (projected[:, i * width : (i + 1) * width] for i in range(3))
        attended = jnp.zeros((wave_count, width), f32)
        for head in range(HHEADS):
            lanes = head_lanes(width, head_size, head)
            scores = exact(jnp.where(lanes, query, 0.0), key, LAST) * head_size ** (-0.5)
            scores = jnp.exp(scores - jnp.max(scores, axis=-1, keepdims=True))
            probs = scores / jnp.sum(scores, axis=-1, keepdims=True)
            probs_out[head] = probs
            attended += exact(probs, jnp.where(lanes, value, 0.0))
        attended_out[...] = attended
        normal_one, scale_one = norm_parts(values + exact(attended, out_ref[...]))
        first = normal_one * one_ref[...]
        hidden = exact(first, up_ref[...])
        factor, _ = gelu_parts(hidden)
        normal_two, scale_two = norm_parts(first + exact(hidden * factor, down_ref[...]))
        mix = (normal_two * two_ref[...]).astype(bf16)
        normal_one_out[...] = normal_one
        scale_one_out[...] = scale_one
        hidden_out[...] = hidden
        normal_two_out[...] = normal_two
        scale_two_out[...] = scale_two
        mix_out[...] = mix
        onehot = onehot_of(ids_ref, wave_count)
        slot_mix = low_dot(onehot.astype(bf16), mix).astype(bf16)
        piece_out[...] = low_dot(kron_identity(slot_mix, piece), gen_ref[...]).astype(bf16)
        image = lax.broadcasted_iota(jnp.int32, mask_ref.shape, 0) == where_ref[0]
        bands = jnp.sum(jnp.where(image, mask_ref[...], 0).astype(f32), axis=0, keepdims=True)
        waves = exact(bands, onehot.astype(f32))
        image_bias_out[...] = exact(waves, low_dot(mix, bias_ref[...]))

    def shape(*dims):
        return jax.ShapeDtypeStruct(dims, f32)

    return local_call(
        kernel,
        where,
        [wave_ids],
        [band_mask, table, *weights, *gains, gen_rows, bias_gen],
        [
            jax.ShapeDtypeStruct((slots * piece, half_width), bf16),
            shape(1, half_width),
            jax.ShapeDtypeStruct((wave_count, width), bf16),
            shape(wave_count, 3 * width),
            shape(HHEADS, wave_count, wave_count),
            shape(wave_count, width),
            shape(wave_count, width),
            shape(wave_count, 1),
            shape(wave_count, inner),
            shape(wave_count, width),
            shape(wave_count, 1),
        ],
        name="hyper_forward",
        mebibytes=56,
        flops=8 * slots * piece * gen_rows.size,
    )


def hyper_backward(where, grad_mix, table, weights, gains, kept):
    wave_count, width = table.shape
    head_size = width // HHEADS

    def kernel(
        where_ref, grad_ref, table_ref, in_ref, out_ref, up_ref, down_ref, one_ref, two_ref,
        projected_ref, probs_ref, attended_ref, normal_one_ref, scale_one_ref, hidden_ref,
        normal_two_ref, scale_two_ref, table_out, in_out, out_out, up_out, down_out, one_out,
        two_out,
    ):
        grad = grad_ref[...]
        normal_two = normal_two_ref[...]
        two_out[...] = jnp.sum(grad * normal_two, axis=0, keepdims=True)
        grad_two = norm_grad(grad * two_ref[...], normal_two, scale_two_ref[...])
        hidden = hidden_ref[...]
        factor, slope = gelu_parts(hidden)
        normal_one = normal_one_ref[...]
        first = normal_one * one_ref[...]
        grad_hidden = exact(grad_two, down_ref[...], LAST) * slope
        down_out[...] = exact(hidden * factor, grad_two, FIRST)
        up_out[...] = exact(first, grad_hidden, FIRST)
        grad_first = grad_two + exact(grad_hidden, up_ref[...], LAST)
        one_out[...] = jnp.sum(grad_first * normal_one, axis=0, keepdims=True)
        grad_one = norm_grad(grad_first * one_ref[...], normal_one, scale_one_ref[...])
        out_out[...] = exact(attended_ref[...], grad_one, FIRST)
        grad_attended = exact(grad_one, out_ref[...], LAST)
        projected = projected_ref[...]
        query, key, value = (projected[:, i * width : (i + 1) * width] for i in range(3))
        grads = [jnp.zeros((wave_count, width), f32) for _ in range(3)]
        for head in range(HHEADS):
            lanes = head_lanes(width, head_size, head)
            own = jnp.where(lanes, grad_attended, 0.0)
            probs = probs_ref[head]
            grad_probs = exact(own, value, LAST)
            grads[2] += exact(probs, own, FIRST)
            scores = probs * (grad_probs - jnp.sum(grad_probs * probs, axis=-1, keepdims=True))
            scores = scores * head_size ** (-0.5)
            grads[0] += exact(scores, jnp.where(lanes, key, 0.0))
            grads[1] += exact(scores, jnp.where(lanes, query, 0.0), FIRST)
        grad_projected = jnp.concatenate(grads, axis=1)
        in_out[...] = exact(table_ref[...], grad_projected, FIRST)
        table_out[...] = grad_one + exact(grad_projected, in_ref[...], LAST)

    arrays = [table, *weights, *gains]
    return local_call(
        kernel,
        where,
        [],
        [grad_mix, *arrays, *kept],
        [jax.ShapeDtypeStruct(a.shape, f32) for a in arrays],
        name="hyper_backward",
        flops=80 * wave_count * weights[2].size,
    )


def attention_forward(where, own, other, pos, gain, in_proj, out_proj):
    patches, half_width = own.shape
    width = 2 * half_width
    heads = half_width // HS

    def kernel(
        where_ref, own_ref, other_ref, pos_ref, gain_ref, in_ref, out_ref, tokens_out, normed_out,
        query_out, key_out, value_out, probs_out, attended_out, part_out,
    ):
        own_half, other_half = own_ref[...].astype(f32), other_ref[...].astype(f32)
        first = where_ref[1] == 0
        embed = jnp.concatenate(
            [jnp.where(first, own_half, other_half), jnp.where(first, other_half, own_half)], axis=1
        )
        tokens = embed + pos_ref[...].astype(f32)
        tokens_out[...] = tokens
        normal, _ = norm_parts(tokens)
        normed = (normal * gain_ref[...].astype(f32)).astype(bf16)
        normed_out[...] = normed
        projected = [low_dot(normed, in_ref[j]).astype(bf16) for j in range(3)]
        query_out[...], key_out[...], value_out[...] = projected
        for pair in range(heads // 2):
            lanes = slice(pair * 2 * HS, (pair + 1) * 2 * HS)
            query, key, value = (p[:, lanes] for p in projected)
            total = None
            for side in range(2):
                mine = head_lanes(2 * HS, HS, side)
                scores = contract_last(jnp.where(mine, query, 0), key) * score_scale
                scores = jnp.exp(scores - jnp.max(scores, axis=-1, keepdims=True))
                probs = scores / jnp.sum(scores, axis=-1, keepdims=True)
                probs_out[2 * pair + side] = probs
                part = low_dot(probs.astype(bf16), jnp.where(mine, value, 0))
                total = part if total is None else total + part
            attended_out[:, lanes] = total.astype(bf16)
        part_out[...] = low_dot(attended_out[...], out_ref[...]).astype(bf16)

    def low(*dims):
        return jax.ShapeDtypeStruct(dims, bf16)

    return local_call(
        kernel,
        where,
        [],
        [own, other, pos, gain, in_proj, out_proj],
        [
            jax.ShapeDtypeStruct((patches, width), f32),
            low(patches, width),
            low(patches, half_width),
            low(patches, half_width),
            low(patches, half_width),
            jax.ShapeDtypeStruct((heads, patches, patches), f32),
            low(patches, half_width),
            low(patches, width),
        ],
        name="attention_forward",
        flops=2 * patches * (in_proj.size + out_proj.size + 4 * patches * half_width),
    )


def feed_forward(where, tokens, own, other, gain, up, down, cotangent):
    patches, width = tokens.shape
    local = up.shape[1]
    tile = local // 3

    def kernel(
        where_ref, tokens_ref, own_ref, other_ref, gain_ref, up_ref, down_ref, cotangent_ref,
        mid_out, second_out, active_out, grad_hidden_out, parts_out,
    ):
        mid = tokens_ref[...] + (own_ref[...].astype(f32) + other_ref[...].astype(f32))
        mid_out[...] = mid
        normal, _ = norm_parts(mid)
        second = (normal * gain_ref[...].astype(f32)).astype(bf16)
        second_out[...] = second
        for t in range(3):
            columns = slice(t * tile, (t + 1) * tile)
            hidden = low_dot(second, up_ref[:, columns])
            factor, slope = gelu_parts(hidden)
            active_out[:, columns] = (hidden * factor).astype(bf16)
            grad_active = contract_last(cotangent_ref[...], down_ref[columns, :])
            grad_hidden_out[:, columns] = (grad_active * slope).astype(bf16)
        parts_out[:patches, :] = low_dot(active_out[...], down_ref[...]).astype(bf16)
        parts_out[PART : PART + patches, :] = contract_last(
            grad_hidden_out[...], up_ref[...]
        ).astype(bf16)

    return local_call(
        kernel,
        where,
        [],
        [tokens, own, other, gain, up, down, cotangent],
        [
            jax.ShapeDtypeStruct((patches, width), f32),
            jax.ShapeDtypeStruct((patches, width), bf16),
            jax.ShapeDtypeStruct((patches, local), bf16),
            jax.ShapeDtypeStruct((patches, local), bf16),
            jax.ShapeDtypeStruct((PART + patches, width), bf16),
        ],
        name="feed_forward",
        flops=8 * patches * up.size,
    )


def attention_backward(
    where, mid, own, other, cotangent, gain, in_proj, out_proj, query, key, value, probs
):
    patches, width = mid.shape
    half_width = width // 2
    heads = half_width // HS

    def kernel(
        where_ref, mid_ref, own_ref, other_ref, cotangent_ref, gain_ref, in_ref, out_ref,
        query_ref, key_ref, value_ref, probs_ref, layer_out, gain_out, grad_mid_out, low_out,
        query_out, key_out, value_out, part_out,
    ):
        mid_values = mid_ref[...]
        down = own_ref[:patches, :].astype(f32) + other_ref[:patches, :].astype(f32)
        layer_out[...] = (mid_values + down).astype(bf16)
        back = slice(PART, PART + patches)
        grad_second = own_ref[back, :].astype(f32) + other_ref[back, :].astype(f32)
        normal, scale = norm_parts(mid_values)
        gain_out[...] = jnp.sum(grad_second * normal, axis=0, keepdims=True)
        grad_mid = cotangent_ref[...].astype(f32) + norm_grad(
            grad_second * gain_ref[...].astype(f32), normal, scale
        )
        grad_mid_out[...] = grad_mid
        grad_low = grad_mid.astype(bf16)
        low_out[...] = grad_low
        grad_attended = contract_last(grad_low, out_ref[...]).astype(bf16)
        for pair in range(heads // 2):
            lanes = slice(pair * 2 * HS, (pair + 1) * 2 * HS)
            query, key, value = query_ref[:, lanes], key_ref[:, lanes], value_ref[:, lanes]
            totals = [None] * 3
            for side in range(2):
                mine = head_lanes(2 * HS, HS, side)
                own_grad = jnp.where(mine, grad_attended[:, lanes], 0)
                probs = probs_ref[2 * pair + side]
                grad_probs = contract_last(own_grad, value)
                inner = jnp.sum(grad_probs * probs, axis=-1, keepdims=True)
                scores = (probs * (grad_probs - inner)).astype(bf16)
                parts = (
                    low_dot(scores, jnp.where(mine, key, 0)),
                    contract_first(scores, jnp.where(mine, query, 0)),
                    contract_first(probs.astype(bf16), own_grad),
                )
                totals = [p if t is None else t + p for t, p in zip(totals, parts)]
            query_out[:, lanes] = (totals[0] * score_scale).astype(bf16)
            key_out[:, lanes] = (totals[1] * score_scale).astype(bf16)
            value_out[:, lanes] = totals[2].astype(bf16)
        part = contract_last(query_out[...], in_ref[0])
        part += contract_last(key_out[...], in_ref[1])
        part += contract_last(value_out[...], in_ref[2])
        part_out[...] = part.astype(bf16)

    def low(*dims):
        return jax.ShapeDtypeStruct(dims, bf16)

    return local_call(
        kernel,
        where,
        [],
        [mid, own, other, cotangent, gain, in_proj, out_proj, query, key, value, probs],
        [
            low(patches, width),
            jax.ShapeDtypeStruct((1, width), f32),
            jax.ShapeDtypeStruct((patches, width), f32),
            low(patches, width),
            low(patches, half_width),
            low(patches, half_width),
            low(patches, half_width),
            low(patches, width),
        ],
        name="attention_backward",
        flops=2 * patches * (in_proj.size + out_proj.size + 8 * patches * half_width),
    )


def token_grad(where, tokens, grad_mid, own, other, gain, gain_two_grad):
    patches, width = tokens.shape
    half_width = width // 2

    def kernel(
        where_ref, tokens_ref, grad_mid_ref, own_ref, other_ref, gain_ref, two_ref, half_out,
        small_out,
    ):
        grad_normed = own_ref[...].astype(f32) + other_ref[...].astype(f32)
        normal, scale = norm_parts(tokens_ref[...])
        grad_one = jnp.sum(grad_normed * normal, axis=0, keepdims=True)
        grad = grad_mid_ref[...] + norm_grad(
            grad_normed * gain_ref[...].astype(f32), normal, scale
        )
        low = grad.astype(bf16)
        half_out[...] = jnp.where(where_ref[1] == 0, low[:, :half_width], low[:, half_width:])
        small_out[...] = jnp.zeros_like(small_out)
        small_out[:patches, :] = low
        small_out[patches : patches + 1, :] = grad_one.astype(bf16)
        small_out[patches + 1 : patches + 2, :] = two_ref[...].astype(bf16)

    return local_call(
        kernel,
        where,
        [],
        [tokens, grad_mid, own, other, gain, gain_two_grad],
        [
            jax.ShapeDtypeStruct((patches, half_width), bf16),
            jax.ShapeDtypeStruct((EXTRA, width), bf16),
        ],
        name="token_grad",
    )


def wave_grads(ids_ref, blocks_ref, rows_ref, wave_count, piece):
    slots = ids_ref.shape[1]
    for s in range(slots):
        rows_ref[s * piece : (s + 1) * piece, :] = blocks_ref[s, :piece, :]
    onehot = onehot_of(ids_ref, wave_count)
    bits = 2**30 - 1
    shift = piece.bit_length() - 1
    tall = low_dot(
        equal_index(slots * piece, slots, shift, 0, bits, bits).astype(bf16), onehot.astype(bf16)
    ).astype(bf16)
    wide = low_dot(
        tall, equal_index(wave_count, wave_count * piece, 0, shift, bits, bits).astype(bf16)
    )
    same = equal_index(slots * piece, wave_count * piece, 0, 0, piece - 1, piece - 1)
    select = jnp.where(same, wide, 0.0).astype(bf16)
    kernels = contract_first(select, rows_ref[...]).astype(bf16)
    biases = jnp.concatenate(
        [
            blocks_ref[s, piece : piece + 1, :].astype(f32)
            + blocks_ref[s, piece + 1 : piece + 2, :].astype(f32)
            for s in range(slots)
        ],
        axis=0,
    )
    return kernels, exact(onehot.astype(f32), biases, FIRST)


def mix_grad(where, wave_ids, blocks, gen_rows, bias_gen, wave_count, count):
    width, half_width = bias_gen.shape
    piece = gen_rows.shape[0] // width

    def kernel(
        where_ref, ids_ref, blocks_ref, gen_ref, bias_ref, mix_out, kernels_out, biases_out, rows_ref
    ):
        kernels, biases = wave_grads(ids_ref, blocks_ref, rows_ref, wave_count, piece)
        kernels_out[...] = kernels
        biases_out[...] = biases
        products = contract_last(kernels, gen_ref[...])
        same = equal_index(*products.shape, 0, 0, piece - 1, piece - 1)
        products = jnp.where(same, products, 0.0)
        rows = jnp.sum(products.reshape(wave_count, piece, -1), axis=1)
        bits = 2**30 - 1
        gather = equal_index(
            width * piece, width, piece.bit_length() - 1, 0, bits, bits
        ).astype(f32)
        mix = exact(rows, gather)
        mix_out[...] = mix + exact(biases, bias_ref[...].astype(f32), LAST) * (1.0 / count)

    return local_call(
        kernel,
        where,
        [wave_ids],
        [blocks, gen_rows, bias_gen],
        [
            jax.ShapeDtypeStruct((wave_count, width), f32),
            jax.ShapeDtypeStruct((wave_count * piece, half_width), bf16),
            jax.ShapeDtypeStruct((wave_count, half_width), f32),
        ],
        scratch=[pltpu.VMEM((wave_ids.shape[1] * piece, half_width), bf16)],
        name="mix_grad",
        flops=2 * wave_count * piece * gen_rows.size,
    )


def generator_grads(where, mix_low, kernels, biases):
    wave_count, width = mix_low.shape
    piece = kernels.shape[0] // wave_count
    half_width = kernels.shape[1]

    def kernel(where_ref, mix_ref, kernels_ref, biases_ref, gen_out, bias_out):
        mix = mix_ref[...]
        gen_out[...] = contract_first(kron_identity(mix, piece), kernels_ref[...])
        bias_out[...] = exact(mix.astype(f32), biases_ref[...], FIRST)

    return local_call(
        kernel,
        where,
        [],
        [mix_low, kernels, biases],
        [
            jax.ShapeDtypeStruct((width * piece, half_width), f32),
            jax.ShapeDtypeStruct((width, half_width), f32),
        ],
        name="generator_grads",
        flops=2 * wave_count * piece * width * piece * half_width,
    )


def embed_part(upper, orders, where, mask, pixels, kernels):
    images, patches, pixel_count = pixels.shape
    half = images // 2

    def kernel(where_ref, mask_ref, pixel_ref, kernel_ref, *outs):
        band = where_ref[0]

        def body(q):
            for c, order in enumerate(orders):
                image = band ^ relative_index(q + half * upper, order)
                scale = mask_ref[image, band].astype(f32)
                product = jnp.dot(
                    pixel_ref[image], kernel_ref[:, span(c)], preferred_element_type=f32
                )
                outs[c][q] = (product * scale).astype(bf16)

        loop(half, body)

    return local_call(
        kernel,
        where,
        [mask],
        [pixels, kernels],
        [jax.ShapeDtypeStruct((half, patches, LANES), bf16)] * 3,
        name="embed_part",
        flops=images * patches * pixel_count * 3 * LANES,
    )


def kernel_grad(upper, orders, where, mask, pixels, grads, total, bias):
    images, patches, pixel_count = pixels.shape
    half = images // 2
    piece = pixel_count // images
    width = 3 * LANES

    def kernel(where_ref, mask_ref, pixel_ref, *refs):
        band = where_ref[0]
        grad_refs = refs[:3]
        if upper:
            old_total, old_bias, out_ref, total_ref, bias_ref = refs[3:]
            total_ref[...] = old_total[...]
            bias_ref[...] = old_bias[...]
        else:
            total_ref, bias_ref = refs[3:]
            total_ref[...] = jnp.zeros_like(total_ref)
            bias_ref[...] = jnp.zeros_like(bias_ref)

        def body(q):
            for c, order in enumerate(orders):
                image = band ^ relative_index(q + half * upper, order)

                @pl.when(mask_ref[image, band] != 0)
                def _(c=c, image=image):
                    grad = grad_refs[c][q]
                    total_ref[span(c), :] += contract_first(grad, pixel_ref[image])
                    bias_ref[:, span(c)] += jnp.sum(grad.astype(f32), axis=0, keepdims=True)

        loop(half, body)
        if upper:
            high = bias_ref[...].astype(bf16)
            low = (bias_ref[...] - high.astype(f32)).astype(bf16)
            whole = total_ref[...].T.astype(bf16)
            for k in range(images):
                out_ref[k, :piece, :] = whole[k * piece : (k + 1) * piece]
                out_ref[k, piece : piece + 1, :] = high
                out_ref[k, piece + 1 : piece + 2, :] = low

    accumulators = [
        jax.ShapeDtypeStruct((width, pixel_count), f32),
        jax.ShapeDtypeStruct((1, width), f32),
    ]
    flops = images * patches * pixel_count * width
    if not upper:
        return local_call(
            kernel, where, [mask], [pixels, *grads], accumulators, name="kernel_grad", flops=flops
        )
    return local_call(
        kernel,
        where,
        [mask],
        [pixels, *grads, total, bias],
        [jax.ShapeDtypeStruct((images, piece + 2, width), bf16)],
        scratch=[pltpu.VMEM(s.shape, f32) for s in accumulators],
        name="kernel_grad_end",
        flops=flops,
    )[0]


def pixel_grad(orders, where, mask, early, late, kernels):
    half, patches, _ = early[0].shape
    pixel_count = kernels.shape[0]

    def kernel(where_ref, mask_ref, *refs):
        early_refs, late_refs, kernel_ref, outs = refs[:3], refs[3:6], refs[6], refs[7:]
        band, head = where_ref[0], where_ref[1]

        def body(q):
            for side in range(2):
                first = head if side == 0 else 1 - head
                image = first * half + q
                parts = []
                for c, order in enumerate(orders):
                    position = position_of(image ^ band, order)
                    low = jnp.minimum(position, half - 1)
                    high = jnp.maximum(position - half, 0)
                    parts.append(
                        jnp.where(position < half, early_refs[c][low], late_refs[c][high])
                    )
                total = contract_last(jnp.concatenate(parts, axis=1), kernel_ref[...])
                outs[side][q] = (total * mask_ref[image, band].astype(f32)).astype(bf16)

        loop(half, body)

    return local_call(
        kernel,
        where,
        [mask],
        [*early, *late, kernels],
        [jax.ShapeDtypeStruct((half, patches, pixel_count), bf16)] * 2,
        name="pixel_grad",
        flops=4 * half * patches * pixel_count * 3 * LANES,
    )


def row_products(orders, count, where, lefts, rights, portions, name):
    rows = lefts[0].shape[1] // count
    half = count // 2 * rows
    widths = [sum(piece[3] for piece in portion) for portion in portions]
    if rows % 16:
        keeps, sends = [], []
        for portion, order in zip(portions, orders):
            places = jnp.asarray([relative_index(p, order) for p in range(count)], jnp.int32)
            columns = ((where[0] ^ places) * rows)[:, None] + jnp.arange(rows, dtype=jnp.int32)
            select = jnp.arange(count * rows, dtype=jnp.int32)[:, None] == columns.reshape(1, -1)
            turned = [jnp.dot(left, select.astype(bf16)) for left in lefts]
            whole = jnp.concatenate(
                [contract_first(turned[i], rights[j][:, s : s + w]) for i, j, s, w in portion],
                axis=1,
            ).astype(bf16)
            keeps.append(whole[:half])
            sends.append(whole[half:])
        return keeps, sends
    uses = sorted({(piece[0], c) for c, portion in enumerate(portions) for piece in portion})

    def kernel(where_ref, *refs):
        left_refs = refs[: len(lefts)]
        right_refs = refs[len(lefts) : len(lefts) + len(rights)]
        outs = refs[len(lefts) + len(rights) : len(lefts) + len(rights) + 6]
        turned_refs = refs[len(lefts) + len(rights) + 6 : -len(uses) - 7]
        ordered = dict(zip(uses, refs[-len(uses) - 7 : -7]))
        made, sems = refs[-7:-1], refs[-1]
        band = where_ref[0]
        for left_ref, turned_ref in zip(left_refs, turned_refs):
            turned_ref[...] = left_ref[...].T
        for (i, c), ordered_ref in ordered.items():
            for p in range(count):
                block = (band ^ relative_index(p, orders[c])) * rows
                ordered_ref[p * rows : (p + 1) * rows, :] = turned_refs[i][
                    pl.ds(pl.multiple_of(block, 16), rows), :
                ]
        copies = []
        for side in (1, 0):
            for c, portion in enumerate(portions):
                place = 0
                slot = 3 - 3 * side + c
                for i, j, start, width in portion:
                    left = ordered[i, c][side * half : (side + 1) * half, :]
                    for column in range(0, width, 256):
                        wide = min(256, width - column)
                        made[slot][:, place : place + wide] = jnp.dot(
                            left,
                            right_refs[j][:, start + column : start + column + wide],
                            preferred_element_type=f32,
                        ).astype(bf16)
                        place += wide
                copies.append(pltpu.make_async_copy(made[slot], outs[slot], sems.at[slot]))
                copies[-1].start()
        for copy in copies:
            copy.wait()

    shapes = [jax.ShapeDtypeStruct((half, width), bf16) for width in widths] * 2
    turned = [pltpu.VMEM((left.shape[1], left.shape[0]), bf16) for left in lefts]
    ordered = [pltpu.VMEM((lefts[i].shape[1], lefts[i].shape[0]), bf16) for i, _ in uses]
    outs = local_call(
        kernel,
        where,
        [],
        [*lefts, *rights],
        shapes,
        scratch=turned
        + ordered
        + [pltpu.VMEM(shape.shape, bf16) for shape in shapes]
        + [pltpu.SemaphoreType.DMA((6,))],
        spaces=[HBM] * 6,
        name=name,
        flops=2 * lefts[0].size * sum(widths),
        mebibytes=32,
    )
    return outs[3:], outs[:3]


def half_sum(where, keeps, arriving, last):
    half = keeps[0].shape[0] // 2
    widths = [keep.shape[1] for keep in keeps]

    def kernel(where_ref, *refs):
        keep_refs, arriving_refs = refs[:3], refs[3:6]
        sends, kept = (refs[6:7], refs[7:8]) if last else (refs[6:9], refs[9:12])
        place = 0
        for c in range(3):
            total = keep_refs[c][...].astype(f32) + arriving_refs[c][...].astype(f32)
            at = slice(place, place + widths[c]) if last else slice(None)
            out = 0 if last else c
            kept[out][:, at] = total[:half]
            sends[out][:, at] = total[half:].astype(bf16)
            place += widths[c]

    shapes = [(half, sum(widths))] if last else [(half, width) for width in widths]
    outs = local_call(
        kernel,
        where,
        [],
        [*keeps, *arriving],
        [jax.ShapeDtypeStruct(shape, bf16) for shape in shapes]
        + [jax.ShapeDtypeStruct(shape, f32) for shape in shapes],
        name="half_sum",
    )
    return outs[: len(shapes)], outs[len(shapes) :]


def final_sum(where, kept, arriving, ff_local, half_width, patches):
    rows = kept.shape[0]

    def kernel(
        where_ref, kept_ref, arriving_ref, up_out, down_out, in_out, out_out, pos_out, one_out,
        two_out,
    ):
        total = kept_ref[...] + arriving_ref[...].astype(f32)
        side = ff_local + EXTRA // 2
        up_out[...] = total[:, :ff_local]
        down_out[...] = total[:, side : side + ff_local]
        for k in range(3):
            in_out[k] = total[:, 2 * side + k * half_width : 2 * side + (k + 1) * half_width]
        out_out[...] = total[:, 2 * side + 3 * half_width :]
        extra = jnp.concatenate(
            [total[:, ff_local:side], total[:, side + ff_local : 2 * side]], axis=1
        )
        pos_out[...] = extra[:, :patches]
        extra = extra.T
        one_out[...] = extra[patches : patches + 1]
        two_out[...] = extra[patches + 1 : patches + 2]

    def shape(*dims):
        return jax.ShapeDtypeStruct(dims, f32)

    return local_call(
        kernel,
        where,
        [],
        [kept, arriving],
        [
            shape(rows, ff_local),
            shape(rows, ff_local),
            shape(3, rows, half_width),
            shape(rows, half_width),
            shape(rows, patches),
            shape(1, rows),
            shape(1, rows),
        ],
        name="final_sum",
    )


STEPS = (1, 2, 4, 8)
XY, YX, ZX, ZY = (8, 4, 2, 1), (8, 4, 1, 2), (8, 2, 1, 4), (8, 1, 2, 4)


def product_scratch(lefts, uses):
    return [pltpu.VMEM((left.shape[1], left.shape[0]), bf16) for left in lefts] + [
        pltpu.VMEM((lefts[i].shape[1], lefts[i].shape[0]), bf16) for i, _ in uses
    ]


def order_rows(band, left_refs, turned_refs, ordered, positions):
    rows = left_refs[0].shape[1] // 16
    for left_ref, turned_ref in zip(left_refs, turned_refs):
        turned_ref[...] = left_ref[...].T
    for (i, order), ordered_ref in ordered.items():
        for p in positions:
            block = (band ^ relative_index(p, order)) * rows
            ordered_ref[p * rows : (p + 1) * rows, :] = turned_refs[i][
                pl.ds(pl.multiple_of(block, 16), rows), :
            ]


def product_tiles(left, right_refs, portion, ordered, order, rows):
    place = 0
    for i, j, start, width in portion:
        for column in range(0, width, 256):
            wide = min(256, width - column)
            yield (
                place,
                wide,
                jnp.dot(
                    ordered[i, order][rows, :],
                    right_refs[j][:, start + column : start + column + wide],
                    preferred_element_type=f32,
                ).astype(bf16),
            )
            place += wide


def early_products(where, lefts, rights, portions, orders):
    uses = sorted({(piece[0], order) for portion, order in zip(portions, orders) for piece in portion})
    half = lefts[0].shape[1] // 2
    widths = [sum(piece[3] for piece in portion) for portion in portions]
    n = len(lefts) + len(rights)

    def kernel(where_ref, *refs):
        left_refs, right_refs = refs[: len(lefts)], refs[len(lefts) : n]
        outs, scratch = refs[n : n + len(portions)], refs[n + len(portions) :]
        ordered = dict(zip(uses, scratch[len(lefts) :]))
        order_rows(where_ref[0], left_refs, scratch[: len(lefts)], ordered, range(8, 16))
        for out, portion, order in zip(outs, portions, orders):
            tiles = product_tiles(
                None, right_refs, portion, ordered, order, slice(half, 2 * half)
            )
            for place, wide, product in tiles:
                out[:, place : place + wide] = product

    return local_call(
        kernel,
        where,
        [],
        [*lefts, *rights],
        [jax.ShapeDtypeStruct((half, width), bf16) for width in widths],
        scratch=product_scratch(lefts, uses),
        name="early_products",
        flops=lefts[0].size * sum(widths),
    )


def round_products(where, lefts, rights, early, early_orders, portions, orders):
    early_of = {0: 1, 1: 0}
    groups = [(0,), (1,), (2, 3)]
    uses = sorted(
        {
            (piece[0], order)
            for portion, order in zip([*early, *portions], [*early_orders, *orders])
            for piece in portion
        }
    )
    quarter = lefts[0].shape[1] // 4
    early_width = sum(piece[3] for piece in early[0])
    widths = [sum(piece[3] for piece in portion) for portion in portions]
    shapes = []
    for g, group in enumerate(groups):
        width = 2 * sum(widths[c] for c in group) + (early_width if g in early_of else 0)
        shapes.append(jax.ShapeDtypeStruct((quarter, width), bf16))
    n = len(lefts) + len(rights)

    def kernel(where_ref, *refs):
        left_refs, right_refs = refs[: len(lefts)], refs[len(lefts) : n]
        outs, made, sems = refs[n : n + 6], refs[-7:-1], refs[-1]
        scratch = refs[n + 6 : -7]
        ordered = dict(zip(uses, scratch[len(lefts) :]))
        order_rows(where_ref[0], left_refs, scratch[: len(lefts)], ordered, range(16))
        copies = []
        for side in (1, 0):
            for g, group in enumerate(groups):
                slot = 3 * (1 - side) + g
                base = 0
                if g in early_of:
                    e = early_of[g]
                    rows = slice(side * quarter, (side + 1) * quarter)
                    tiles = product_tiles(
                        None, right_refs, early[e], ordered, early_orders[e], rows
                    )
                    for place, wide, product in tiles:
                        made[slot][:, place : place + wide] = product
                    base = early_width
                for c in group:
                    rows = slice(side * 2 * quarter, (side + 1) * 2 * quarter)
                    tiles = product_tiles(None, right_refs, portions[c], ordered, orders[c], rows)
                    for place, wide, product in tiles:
                        for k in range(2):
                            at = base + k * widths[c] + place
                            made[slot][:, at : at + wide] = product[k * quarter : (k + 1) * quarter]
                    base += 2 * widths[c]
                copies.append(pltpu.make_async_copy(made[slot], outs[slot], sems.at[slot]))
                copies[-1].start()
        for copy in copies:
            copy.wait()

    outs = local_call(
        kernel,
        where,
        [],
        [*lefts, *rights],
        shapes * 2,
        scratch=product_scratch(lefts, uses)
        + [pltpu.VMEM(shape.shape, bf16) for shape in shapes * 2]
        + [pltpu.SemaphoreType.DMA((6,))],
        spaces=[HBM] * 6,
        name="round_products",
        flops=2 * lefts[0].size * sum(widths) + lefts[0].size * early_width,
        mebibytes=32,
    )
    return outs[:3], outs[3:]


def early_sum(where, sends, keeps, arriving):
    quarter = sends[0].shape[0]
    width = arriving[0].shape[1]
    buffers = [sends[0], keeps[0], sends[1], keeps[1]]

    def kernel(where_ref, *refs):
        arriving_refs, outs, parts, sems = refs[4:6], refs[6:10], refs[10], refs[11]
        loads = []
        for k in range(4):
            loads.append(
                pltpu.make_async_copy(refs[k].at[:, pl.ds(0, width)], parts.at[k], sems.at[k])
            )
            loads[-1].start()
        stores = []
        for k in range(4):
            loads[k].wait()
            rows = slice(quarter, 2 * quarter) if k % 2 == 0 else slice(0, quarter)
            added = arriving_refs[1 - k // 2][rows, :].astype(f32)
            parts[k] = (parts[k].astype(f32) + added).astype(bf16)
            stores.append(
                pltpu.make_async_copy(parts.at[k], outs[k].at[:, pl.ds(0, width)], sems.at[4 + k])
            )
            stores[-1].start()
        for store in stores:
            store.wait()

    smem = pl.BlockSpec(memory_space=pltpu.SMEM)
    outs = pl.pallas_call(
        kernel,
        in_specs=[smem]
        + [pl.BlockSpec(memory_space=HBM)] * 4
        + [pl.BlockSpec(memory_space=pltpu.VMEM)] * 2,
        out_specs=[pl.BlockSpec(memory_space=HBM)] * 4,
        out_shape=[jax.ShapeDtypeStruct(b.shape, bf16) for b in buffers],
        input_output_aliases={1: 0, 2: 1, 3: 2, 4: 3},
        scratch_shapes=[
            pltpu.VMEM((4, quarter, width), bf16),
            pltpu.SemaphoreType.DMA((8,)),
        ],
        compiler_params=pltpu.CompilerParams(vmem_limit_bytes=24 * 2**20),
        name="early_sum",
    )(where, *buffers, *arriving)
    return [outs[0], outs[2], sends[2]], [outs[1], outs[3], keeps[2]]


def second_sum(where, keeps, arriving, early_width, widths):
    quarter = keeps[0].shape[0]
    pair = quarter // 2
    wa, wb, wc, wd = widths

    def kernel(where_ref, *refs):
        keep_refs, arriving_refs = refs[:3], refs[3:6]
        send_y, send_x, send_z, keep_y, keep_x, keep_z = refs[6:]
        totals = [k[...].astype(f32) + a[...].astype(f32) for k, a in zip(keep_refs, arriving_refs)]
        for e, g in ((0, 1), (1, 0)):
            at = slice(e * early_width, (e + 1) * early_width)
            keep_z[:, at] = totals[g][:pair, :early_width]
            send_z[:, at] = totals[g][pair:, :early_width].astype(bf16)
        for total, start, width, keep, send, place in (
            (totals[0], early_width, wa, keep_y, send_y, 0),
            (totals[2], 2 * wc, wd, keep_y, send_y, 2 * wa),
            (totals[1], early_width, wb, keep_x, send_x, 0),
            (totals[2], 0, wc, keep_x, send_x, 2 * wb),
        ):
            for k in range(2):
                rows = slice(k * pair, (k + 1) * pair)
                at = slice(place + k * width, place + (k + 1) * width)
                keep[:, at] = total[rows, start : start + width]
                send[:, at] = total[rows, start + width : start + 2 * width].astype(bf16)

    shapes = [(pair, 2 * (wa + wd)), (pair, 2 * (wb + wc)), (pair, 2 * early_width)]
    outs = local_call(
        kernel,
        where,
        [],
        [*keeps, *arriving],
        [jax.ShapeDtypeStruct(shape, bf16) for shape in shapes]
        + [jax.ShapeDtypeStruct(shape, f32) for shape in shapes],
        name="second_sum",
    )
    return outs[:3], outs[3:]


def third_sum(where, keeps, arriving, early_width, widths):
    pair = keeps[0].shape[0]
    rows = pair // 2
    wa, wb, wc, wd = widths

    def kernel(where_ref, *refs):
        keep_refs, arriving_refs = refs[:3], refs[3:6]
        send_e, send_ab, send_c, send_d, keep_e, keep_ab, keep_c, keep_d = refs[6:]
        y, x, z = (k[...] + a[...].astype(f32) for k, a in zip(keep_refs, arriving_refs))
        keep_e[...] = z[:rows]
        send_e[...] = z[rows:].astype(bf16)
        for total, start, width, keep, send, place in (
            (y, 0, wa, keep_ab, send_ab, 0),
            (x, 0, wb, keep_ab, send_ab, wa),
            (x, 2 * wb, wc, keep_c, send_c, 0),
            (y, 2 * wa, wd, keep_d, send_d, 0),
        ):
            keep[:, place : place + width] = total[:, start : start + width]
            send[:, place : place + width] = total[:, start + width : start + 2 * width].astype(bf16)

    shapes = [(rows, 2 * early_width), (pair, wa + wb), (pair, wc), (pair, wd)]
    outs = local_call(
        kernel,
        where,
        [],
        [*keeps, *arriving],
        [jax.ShapeDtypeStruct(shape, bf16) for shape in shapes]
        + [jax.ShapeDtypeStruct(shape, f32) for shape in shapes],
        name="third_sum",
    )
    return outs[:4], outs[4:]


def fourth_sum(where, keeps, arriving):
    rows = keeps[0].shape[0] // 2
    widths = [keep.shape[1] for keep in keeps]

    def kernel(where_ref, *refs):
        send, kept = refs[6:]
        place = 0
        for keep, arrived, width in zip(refs[:3], refs[3:6], widths):
            total = keep[...] + arrived[...].astype(f32)
            kept[:, place : place + width] = total[:rows]
            send[:, place : place + width] = total[rows:].astype(bf16)
            place += width

    return local_call(
        kernel,
        where,
        [],
        [*keeps, *arriving],
        [
            jax.ShapeDtypeStruct((rows, sum(widths)), bf16),
            jax.ShapeDtypeStruct((rows, sum(widths)), f32),
        ],
        name="fourth_sum",
    )


def last_sum(where, early, early_arriving, kept, arriving, ff_local, half_width, patches):
    rows = kept.shape[0]
    early_width = early.shape[1] // 2
    rest = ff_local - early_width

    def kernel(
        where_ref, early_ref, early_arriving_ref, kept_ref, arriving_ref, up_out, down_out, in_out,
        out_out, pos_out, one_out, two_out,
    ):
        first = early_ref[...] + early_arriving_ref[...].astype(f32)
        total = kept_ref[...] + arriving_ref[...].astype(f32)
        up_out[:, :early_width] = first[:, :early_width]
        down_out[:, :early_width] = first[:, early_width:]
        up_out[:, early_width:] = total[:, :rest]
        b = rest + 256
        down_out[:, early_width:] = total[:, b : b + rest]
        in_out[0, :, :256] = total[:, rest:b]
        at = b + rest
        in_out[0, :, 256:] = total[:, at : at + half_width - 256]
        at += half_width - 256
        in_out[1] = total[:, at : at + half_width]
        in_out[2] = total[:, at + half_width : at + 2 * half_width]
        at += 2 * half_width
        out_out[...] = total[:, at : at + half_width]
        extra = total[:, at + half_width :].T
        pos_out[...] = total[:, at + half_width : at + half_width + patches]
        one_out[...] = extra[patches : patches + 1]
        two_out[...] = extra[patches + 1 : patches + 2]

    def shape(*dims):
        return jax.ShapeDtypeStruct(dims, f32)

    return local_call(
        kernel,
        where,
        [],
        [early, early_arriving, kept, arriving],
        [
            shape(rows, ff_local),
            shape(rows, ff_local),
            shape(3, rows, half_width),
            shape(rows, half_width),
            shape(rows, patches),
            shape(1, rows),
            shape(1, rows),
        ],
        name="last_sum",
    )


def after(values, *others):
    return lax.optimization_barrier((values, others))[0]


def shards(
    pixels,
    band_mask,
    wave_ids,
    pos_embed,
    in_proj,
    out_proj,
    up_proj,
    down_proj,
    gain_one,
    gain_two,
    kernel_gen,
    bias_gen,
    wave_table,
    hyper_in,
    hyper_out,
    hyper_up,
    hyper_down,
    hyper_gain_one,
    hyper_gain_two,
    cotangent,
):
    band_index = lax.axis_index("band")
    head_index = lax.axis_index("head")
    count = lax.axis_size("band")
    images, slot_local, patches, pixel_count = pixels.shape
    model_width = in_proj.shape[1]
    half_width = in_proj.shape[2]
    wave_count, hyper_width = wave_table.shape
    assert images == count and slot_local == 1
    orders = gather_orders(count)
    where = jnp.stack([band_index, head_index]).astype(jnp.int32)
    pixels = pixels.reshape(images, patches, pixel_count)
    wave_ids = wave_ids.reshape(1, -1)

    gen_rows = kernel_gen.reshape(-1, half_width)
    hyper_weights = [hyper_in, hyper_out, hyper_up, hyper_down]
    hyper_gains = [hyper_gain_one[None], hyper_gain_two[None]]
    slot_piece, image_bias, mix_low, *hyper_kept = hyper_forward(
        where,
        wave_ids,
        band_mask,
        wave_table,
        hyper_weights,
        hyper_gains,
        gen_rows,
        bias_gen,
        count,
    )
    slot_piece = slot_piece.reshape(count, -1, half_width)
    kernels = lax.all_to_all(slot_piece, "band", 0, 0, tiled=True).reshape(pixel_count, half_width)

    sends = embed_part(1, orders, where, band_mask, pixels, kernels)
    arriving = [hop(send, order[-1]) for send, order in zip(sends, orders)]
    keeps = embed_part(0, orders, where, band_mask, pixels, kernels)
    embed_half = jnp.concatenate(
        [part[0] for part in scatter_sum(keeps, None, orders, arriving)], axis=1
    )
    embed_low = (embed_half + image_bias).astype(bf16)
    gain_one = gain_one[None]
    gain_two = gain_two[None]
    tokens, normed_low, query, key, value, probs, attended, attn_part = attention_forward(
        where, embed_low, swap(embed_low), pos_embed, gain_one, in_proj, out_proj
    )
    grad_low = cotangent[0]
    mid_stream, second_low, active_low, grad_hidden, ff_parts = feed_forward(
        where, tokens, attn_part, swap(attn_part), gain_two, up_proj, down_proj, grad_low
    )
    ff_other = swap(ff_parts)

    ff_local = up_proj.shape[1]
    staged = count == 16
    if staged:
        early_width = EARLY
        ff_early = [[(0, 0, 0, early_width)], [(1, 1, 0, early_width)]]
        early_sends = early_products(
            where, [second_low, grad_low], [grad_hidden, active_low], ff_early, [XY, YX]
        )
        early_sends, ff_other = lax.optimization_barrier((early_sends, ff_other))
        early_arriving = [hop(send, step) for send, step in zip(early_sends, STEPS)]

    layer_out, gain_two_grad, grad_mid, grad_mid_low, *grad_projected, normed_part = (
        attention_backward(
            where,
            mid_stream,
            ff_parts,
            ff_other,
            grad_low,
            gain_two,
            in_proj,
            out_proj,
            query,
            key,
            value,
            probs,
        )
    )
    grad_embed_half, small = token_grad(
        where, tokens, grad_mid, normed_part, swap(normed_part), gain_one, gain_two_grad
    )

    first = hop(grad_embed_half, orders[0][0])
    lefts = [second_low, grad_low, normed_low, grad_mid_low, small]
    rights = [grad_hidden, active_low, *grad_projected, attended, jnp.eye(EXTRA, dtype=bf16)]
    side = EXTRA // 2
    if staged:
        portions = [
            [(0, 0, early_width, ff_local - early_width), (2, 2, 0, 256)],
            [(1, 1, early_width, ff_local - early_width)]
            + [(2, 2, 256, half_width - 256), (2, 3, 0, half_width - 256)],
            [(2, 3, half_width - 256, 256), (2, 4, 0, half_width)],
            [(3, 5, 0, half_width), (4, 6, 0, EXTRA)],
        ]
        widths = [sum(piece[3] for piece in portion) for portion in portions]
        sends, keeps = round_products(
            where, lefts, rights, ff_early, [XY, YX], portions, [XY, YX, ZX, ZY]
        )
        first = after(first, (sends, early_arriving))
    else:
        portions = [
            [(0, 0, 0, ff_local), (4, 6, 0, side)],
            [(1, 1, 0, ff_local), (4, 6, side, side)],
            [(2, 2 + k, 0, half_width) for k in range(3)] + [(3, 5, 0, half_width)],
        ]
        keeps, sends = row_products(orders, count, where, lefts, rights, portions, "weight_grads")
        first = after(first, sends)
    early, late = [], []
    for c, order in enumerate(orders):
        block = jnp.stack([grad_embed_half[:, span(c)], first[:, span(c)]])
        for step in order[1:-1]:
            block = jnp.concatenate([block, hop(block, step)], axis=0)
        early.append(block)
        late.append(hop(block, order[-1]))
    total, bias = kernel_grad(0, orders, where, band_mask, pixels, early, None, None)
    if staged:
        sends, keeps = early_sum(where, sends, keeps, after(early_arriving, early))
    sends, late, total = lax.optimization_barrier((sends, late, total))
    if staged:
        arriving = [hop(send, step) for send, step in zip(sends, STEPS)]
    else:
        arriving = [hop(send, order[-1]) for send, order in zip(sends, orders)]
    blocks = kernel_grad(1, orders, where, band_mask, pixels, late, total, bias)
    spread_blocks = lax.all_to_all(blocks, "band", 0, 0, tiled=True)
    early, late = after((early, late), blocks)
    own_pixels, other_pixels = pixel_grad(orders, where, band_mask, early, late, kernels)
    grad_pixels = (own_pixels.astype(f32) + swap(other_pixels).astype(f32)).astype(bf16)
    grad_pixels = grad_pixels[:, None]
    steps = len(orders[0])
    mixing = count // 2
    arriving = after(arriving, (spread_blocks, own_pixels))
    for t in range(steps - 1):
        last = t == steps - 2
        if not staged:
            sends, keeps = half_sum(where, keeps, arriving, last)
            if last:
                arriving = hop(sends[0], orders[0][0])
            else:
                arriving = [hop(send, order[-2 - t]) for send, order in zip(sends, orders)]
        elif t == 0:
            sends, keeps = second_sum(where, keeps, arriving, early_width, widths)
            arriving = [hop(send, step) for send, step in zip(sends, (2, 1, 4))]
        elif t == 1:
            sends, keeps = third_sum(where, keeps, arriving, early_width, widths)
            early_last, *arriving = [hop(send, step) for send, step in zip(sends, (8, 4, 2, 1))]
            early_kept, *keeps = keeps
        else:
            sends, keeps = fourth_sum(where, keeps, arriving)
            arriving = hop(sends, 8)
        if t == 0:
            grad_mix, wave_kernels, wave_biases = mix_grad(
                where, wave_ids, after(spread_blocks, sends), gen_rows, bias_gen, wave_count, count
            )
            grad_mix = grad_mix + swap(grad_mix)
        else:
            grad_mix = after(grad_mix, sends)
        while mixing and (t >= 2 or mixing > count // 8):
            grad_mix = grad_mix + hop(grad_mix, mixing)
            mixing //= 2
        if not last:
            arriving = after(arriving, grad_mix)
    hyper_grads = hyper_backward(
        where, grad_mix, wave_table, hyper_weights, hyper_gains, hyper_kept
    )
    grad_kernel_gen, grad_bias_gen = generator_grads(where, mix_low, wave_kernels, wave_biases)
    if staged:
        sums = last_sum(
            where, early_kept, early_last, keeps, arriving, ff_local, half_width, patches
        )
    else:
        sums = final_sum(where, keeps[0], arriving, ff_local, half_width, patches)
    grad_up, grad_down, grad_in_proj, grad_out_proj, grad_pos, *grad_gains = sums
    return (
        layer_out[None],
        grad_pixels,
        grad_pos.T,
        grad_in_proj,
        grad_out_proj.T,
        grad_up,
        grad_down.T,
        grad_gains[0][0],
        grad_gains[1][0],
        grad_kernel_gen.reshape(kernel_gen.shape),
        grad_bias_gen,
        *hyper_grads[:5],
        hyper_grads[5][0],
        hyper_grads[6][0],
    )


def solution(mesh):
    in_specs = (
        P(None, "band", None, None),
        P(),
        P(),
        P(),
        P(None, None, "head"),
        P("head", None),
        P(None, "head"),
        P("head", None),
        P(),
        P(),
        P(None, "band", "head"),
        P(None, "head"),
        P(),
        P(),
        P(),
        P(),
        P(),
        P(),
        P(),
        P("band", None, None),
    )
    out_specs = (
        P("band", None, None),
        P("head", "band", None, None),
        P(None, "band"),
        P(None, "band", "head"),
        P("head", "band"),
        P("band", "head"),
        P("head", "band"),
        P("band"),
        P("band"),
        P(None, "band", "head"),
        P(None, "head"),
        P(),
        P(),
        P(),
        P(),
        P(),
        P(),
        P(),
    )
    return jax.shard_map(shards, mesh=mesh, in_specs=in_specs, out_specs=out_specs, check_vma=False)
```

```python
import jax
import jax.numpy as jnp
import numpy as np
from jax import lax
from jax.experimental import pallas as pl
from jax.experimental.pallas import tpu as pltpu
from jax.sharding import PartitionSpec as P

HS = 64
HHEADS = 4
LANES = 128
EXTRA = 256
EARLY = 896
HBM = pltpu.HBM
PART = 208

highest = lax.Precision.HIGHEST
norm_epsilon = 1e-06
score_scale = 0.125
root_half = 0.7071067811865476
density_scale = 0.3989422804014327
f32 = jnp.float32
bf16 = jnp.bfloat16


def norm_parts(values):
    centered = values - jnp.mean(values, axis=-1, keepdims=True)
    variance = jnp.mean(centered * centered, axis=-1, keepdims=True)
    scale = lax.rsqrt(variance + norm_epsilon)
    return centered * scale, scale


def norm_grad(grad, normal, scale):
    inner = jnp.mean(grad, axis=-1, keepdims=True)
    along = jnp.mean(grad * normal, axis=-1, keepdims=True)
    return scale * (grad - inner - normal * along)


def gelu_parts(values):
    cumulative = 0.5 * (1.0 + lax.erf(values * root_half))
    density = jnp.exp(-0.5 * values * values) * density_scale
    return cumulative, cumulative + values * density


def contract_first(left, right):
    return lax.dot_general(left, right, (((0,), (0,)), ((), ())), preferred_element_type=f32)


def contract_last(left, right):
    return lax.dot_general(left, right, (((1,), (1,)), ((), ())), preferred_element_type=f32)


def exact(left, right, dims=((1,), (0,))):
    def product(a, b):
        return lax.dot_general(a, b, (dims, ((), ())), preferred_element_type=f32)

    left_high, right_high = left.astype(bf16), right.astype(bf16)
    left_low = (left - left_high.astype(f32)).astype(bf16)
    right_low = (right - right_high.astype(f32)).astype(bf16)
    return product(left_high, right_high) + (
        product(left_high, right_low) + product(left_low, right_high)
    )


FIRST = ((0,), (0,))
LAST = ((1,), (1,))


def low_dot(left, right):
    return jnp.dot(left, right, preferred_element_type=f32)


def equal_index(rows, columns, row_shift, column_shift, row_mask, column_mask):
    row = lax.broadcasted_iota(jnp.int32, (rows, columns), 0)
    column = lax.broadcasted_iota(jnp.int32, (rows, columns), 1)
    return ((row >> row_shift) & row_mask) == ((column >> column_shift) & column_mask)


def onehot_of(ids_ref, wave_count):
    slots = ids_ref.shape[1]
    row = lax.broadcasted_iota(jnp.int32, (slots, wave_count), 0)
    waves = jnp.zeros((slots, wave_count), jnp.int32)
    for s in range(slots):
        waves = jnp.where(row == s, ids_ref[0, s], waves)
    return waves == lax.broadcasted_iota(jnp.int32, (slots, wave_count), 1)


def spread(mix, piece):
    rows, width = mix.shape
    shift = piece.bit_length() - 1
    all_bits = 2**30 - 1
    repeat_rows = equal_index(rows * piece, rows, shift, 0, all_bits, all_bits)
    repeat_columns = equal_index(width, width * piece, 0, shift, all_bits, all_bits)
    tall = low_dot(repeat_rows.astype(bf16), mix).astype(bf16)
    return low_dot(tall, repeat_columns.astype(bf16))


def kron_identity(mix, piece):
    rows, width = mix.shape
    same = equal_index(rows * piece, width * piece, 0, 0, piece - 1, piece - 1)
    return jnp.where(same, spread(mix, piece), 0.0).astype(bf16)


def head_lanes(width, head_size, head):
    lane = lax.broadcasted_iota(jnp.int32, (1, width), 1)
    return (lane >> (head_size.bit_length() - 1)) == head


def hop(values, step):
    count = lax.axis_size("band")
    return lax.ppermute(values, "band", [(i, i ^ step) for i in range(count)])


def swap(values):
    return lax.ppermute(values, "head", [(0, 1), (1, 0)])


def head_sum(part):
    low = part.astype(bf16)
    return low.astype(f32) + swap(low).astype(f32)


def gather_orders(count):
    steps = []
    step = count // 2
    while step:
        steps.append(step)
        step //= 2
    if len(steps) < 4:
        return [tuple(steps)] * 3
    head, (c, b, a) = tuple(steps[:-3]), steps[-3:]
    return [head + (c, b, a), head + (a, c, b), head + (b, a, c)]


def relative_index(position, order):
    index = 0
    for t, step in enumerate(order):
        index = index + ((position >> t) & 1) * step
    return index


def position_of(index, order):
    position = 0
    for t, step in enumerate(order):
        position = position + (((index >> (step.bit_length() - 1)) & 1) << t)
    return position


def scatter_sum(keeps, sends, orders, arriving=None):
    if arriving is None:
        arriving = [hop(send, order[-1]) for send, order in zip(sends, orders)]
    for t in range(len(orders[0]) - 2, -1, -1):
        sends, kept = [], []
        for k, a in zip(keeps, arriving):
            half = k.shape[0] // 2
            sends.append((k[half:].astype(f32) + a[half:].astype(f32)).astype(bf16))
            kept.append(k[:half].astype(f32) + a[:half].astype(f32))
        keeps = kept
        if t == 0 and len({order[0] for order in orders}) == 1:
            merged = hop(jnp.concatenate(sends, axis=-1), orders[0][0])
            arriving, start = [], 0
            for send in sends:
                arriving.append(merged[..., start : start + send.shape[-1]])
                start += send.shape[-1]
        else:
            arriving = [hop(send, order[t]) for send, order in zip(sends, orders)]
    return [k.astype(f32) + a.astype(f32) for k, a in zip(keeps, arriving)]


def loop(count, body):
    if count <= 16:
        for q in range(count):
            body(q)
    else:

        def step(q, carry):
            body(q)
            return carry

        lax.fori_loop(0, count, step, 0)


def span(c):
    return slice(c * LANES, (c + 1) * LANES)


def local_call(
    kernel, where, tables, args, out_shape, scratch=(), name=None, flops=0, mebibytes=24,
    spaces=None,
):
    vmem = pl.BlockSpec(memory_space=pltpu.VMEM)
    smem = pl.BlockSpec(memory_space=pltpu.SMEM)
    moved = sum(x.size * x.dtype.itemsize for x in args)
    moved += sum(int(np.prod(s.shape)) * s.dtype.itemsize for s in out_shape)
    return pl.pallas_call(
        kernel,
        in_specs=[smem] * (1 + len(tables)) + [vmem] * len(args),
        out_specs=[
            pl.BlockSpec(memory_space=space or pltpu.VMEM)
            for space in spaces or [None] * len(out_shape)
        ],
        out_shape=list(out_shape),
        scratch_shapes=list(scratch),
        cost_estimate=pl.CostEstimate(flops=flops, bytes_accessed=moved, transcendentals=0),
        compiler_params=pltpu.CompilerParams(vmem_limit_bytes=mebibytes * 2**20),
        name=name,
    )(where, *tables, *args)


def hyper_forward(where, wave_ids, band_mask, table, weights, gains, gen_rows, bias_gen, count):
    slots = wave_ids.shape[1]
    wave_count, width = table.shape
    piece = gen_rows.shape[0] // width
    half_width = gen_rows.shape[1]
    inner = weights[2].shape[1]
    head_size = width // HHEADS

    def kernel(
        where_ref, ids_ref, mask_ref, table_ref, in_ref, out_ref, up_ref, down_ref, one_ref,
        two_ref, gen_ref, bias_ref, piece_out, image_bias_out, mix_out, projected_out, probs_out,
        attended_out, normal_one_out, scale_one_out, hidden_out, normal_two_out, scale_two_out,
    ):
        values = table_ref[...]
        projected = exact(values, in_ref[...])
        projected_out[...] = projected
        query, key, value = (projected[:, i * width : (i + 1) * width] for i in range(3))
        attended = jnp.zeros((wave_count, width), f32)
        for head in range(HHEADS):
            lanes = head_lanes(width, head_size, head)
            scores = exact(jnp.where(lanes, query, 0.0), key, LAST) * head_size ** (-0.5)
            scores = jnp.exp(scores - jnp.max(scores, axis=-1, keepdims=True))
            probs = scores / jnp.sum(scores, axis=-1, keepdims=True)
            probs_out[head] = probs
            attended += exact(probs, jnp.where(lanes, value, 0.0))
        attended_out[...] = attended
        normal_one, scale_one = norm_parts(values + exact(attended, out_ref[...]))
        first = normal_one * one_ref[...]
        hidden = exact(first, up_ref[...])
        factor, _ = gelu_parts(hidden)
        normal_two, scale_two = norm_parts(first + exact(hidden * factor, down_ref[...]))
        mix = (normal_two * two_ref[...]).astype(bf16)
        normal_one_out[...] = normal_one
        scale_one_out[...] = scale_one
        hidden_out[...] = hidden
        normal_two_out[...] = normal_two
        scale_two_out[...] = scale_two
        mix_out[...] = mix
        onehot = onehot_of(ids_ref, wave_count)
        slot_mix = low_dot(onehot.astype(bf16), mix).astype(bf16)
        piece_out[...] = low_dot(kron_identity(slot_mix, piece), gen_ref[...]).astype(bf16)
        image = lax.broadcasted_iota(jnp.int32, mask_ref.shape, 0) == where_ref[0]
        bands = jnp.sum(jnp.where(image, mask_ref[...], 0).astype(f32), axis=0, keepdims=True)
        waves = exact(bands, onehot.astype(f32))
        image_bias_out[...] = exact(waves, low_dot(mix, bias_ref[...]))

    def shape(*dims):
        return jax.ShapeDtypeStruct(dims, f32)

    return local_call(
        kernel,
        where,
        [wave_ids],
        [band_mask, table, *weights, *gains, gen_rows, bias_gen],
        [
            jax.ShapeDtypeStruct((slots * piece, half_width), bf16),
            shape(1, half_width),
            jax.ShapeDtypeStruct((wave_count, width), bf16),
            shape(wave_count, 3 * width),
            shape(HHEADS, wave_count, wave_count),
            shape(wave_count, width),
            shape(wave_count, width),
            shape(wave_count, 1),
            shape(wave_count, inner),
            shape(wave_count, width),
            shape(wave_count, 1),
        ],
        name="hyper_forward",
        mebibytes=56,
        flops=8 * slots * piece * gen_rows.size,
    )


def hyper_backward(where, grad_mix, table, weights, gains, kept):
    wave_count, width = table.shape
    head_size = width // HHEADS

    def kernel(
        where_ref, grad_ref, table_ref, in_ref, out_ref, up_ref, down_ref, one_ref, two_ref,
        projected_ref, probs_ref, attended_ref, normal_one_ref, scale_one_ref, hidden_ref,
        normal_two_ref, scale_two_ref, table_out, in_out, out_out, up_out, down_out, one_out,
        two_out,
    ):
        grad = grad_ref[...]
        normal_two = normal_two_ref[...]
        two_out[...] = jnp.sum(grad * normal_two, axis=0, keepdims=True)
        grad_two = norm_grad(grad * two_ref[...], normal_two, scale_two_ref[...])
        hidden = hidden_ref[...]
        factor, slope = gelu_parts(hidden)
        normal_one = normal_one_ref[...]
        first = normal_one * one_ref[...]
        grad_hidden = exact(grad_two, down_ref[...], LAST) * slope
        down_out[...] = exact(hidden * factor, grad_two, FIRST)
        up_out[...] = exact(first, grad_hidden, FIRST)
        grad_first = grad_two + exact(grad_hidden, up_ref[...], LAST)
        one_out[...] = jnp.sum(grad_first * normal_one, axis=0, keepdims=True)
        grad_one = norm_grad(grad_first * one_ref[...], normal_one, scale_one_ref[...])
        out_out[...] = exact(attended_ref[...], grad_one, FIRST)
        grad_attended = exact(grad_one, out_ref[...], LAST)
        projected = projected_ref[...]
        query, key, value = (projected[:, i * width : (i + 1) * width] for i in range(3))
        grads = [jnp.zeros((wave_count, width), f32) for _ in range(3)]
        for head in range(HHEADS):
            lanes = head_lanes(width, head_size, head)
            own = jnp.where(lanes, grad_attended, 0.0)
            probs = probs_ref[head]
            grad_probs = exact(own, value, LAST)
            grads[2] += exact(probs, own, FIRST)
            scores = probs * (grad_probs - jnp.sum(grad_probs * probs, axis=-1, keepdims=True))
            scores = scores * head_size ** (-0.5)
            grads[0] += exact(scores, jnp.where(lanes, key, 0.0))
            grads[1] += exact(scores, jnp.where(lanes, query, 0.0), FIRST)
        grad_projected = jnp.concatenate(grads, axis=1)
        in_out[...] = exact(table_ref[...], grad_projected, FIRST)
        table_out[...] = grad_one + exact(grad_projected, in_ref[...], LAST)

    arrays = [table, *weights, *gains]
    return local_call(
        kernel,
        where,
        [],
        [grad_mix, *arrays, *kept],
        [jax.ShapeDtypeStruct(a.shape, f32) for a in arrays],
        name="hyper_backward",
        flops=80 * wave_count * weights[2].size,
    )


def attention_forward(where, own, other, pos, gain, in_proj, out_proj):
    patches, half_width = own.shape
    width = 2 * half_width
    heads = half_width // HS

    def kernel(
        where_ref, own_ref, other_ref, pos_ref, gain_ref, in_ref, out_ref, tokens_out, normed_out,
        query_out, key_out, value_out, probs_out, attended_out, part_out,
    ):
        own_half, other_half = own_ref[...].astype(f32), other_ref[...].astype(f32)
        first = where_ref[1] == 0
        embed = jnp.concatenate(
            [jnp.where(first, own_half, other_half), jnp.where(first, other_half, own_half)], axis=1
        )
        tokens = embed + pos_ref[...].astype(f32)
        tokens_out[...] = tokens
        normal, _ = norm_parts(tokens)
        normed = (normal * gain_ref[...].astype(f32)).astype(bf16)
        normed_out[...] = normed
        projected = [low_dot(normed, in_ref[j]).astype(bf16) for j in range(3)]
        query_out[...], key_out[...], value_out[...] = projected
        for pair in range(heads // 2):
            lanes = slice(pair * 2 * HS, (pair + 1) * 2 * HS)
            query, key, value = (p[:, lanes] for p in projected)
            total = None
            for side in range(2):
                mine = head_lanes(2 * HS, HS, side)
                scores = contract_last(jnp.where(mine, query, 0), key) * score_scale
                scores = jnp.exp(scores - jnp.max(scores, axis=-1, keepdims=True))
                probs = scores / jnp.sum(scores, axis=-1, keepdims=True)
                probs_out[2 * pair + side] = probs
                part = low_dot(probs.astype(bf16), jnp.where(mine, value, 0))
                total = part if total is None else total + part
            attended_out[:, lanes] = total.astype(bf16)
        part_out[...] = low_dot(attended_out[...], out_ref[...]).astype(bf16)

    def low(*dims):
        return jax.ShapeDtypeStruct(dims, bf16)

    return local_call(
        kernel,
        where,
        [],
        [own, other, pos, gain, in_proj, out_proj],
        [
            jax.ShapeDtypeStruct((patches, width), f32),
            low(patches, width),
            low(patches, half_width),
            low(patches, half_width),
            low(patches, half_width),
            jax.ShapeDtypeStruct((heads, patches, patches), f32),
            low(patches, half_width),
            low(patches, width),
        ],
        name="attention_forward",
        flops=2 * patches * (in_proj.size + out_proj.size + 4 * patches * half_width),
    )


def feed_forward(where, tokens, own, other, gain, up, down, cotangent):
    patches, width = tokens.shape
    local = up.shape[1]
    tile = local // 3

    def kernel(
        where_ref, tokens_ref, own_ref, other_ref, gain_ref, up_ref, down_ref, cotangent_ref,
        mid_out, second_out, active_out, grad_hidden_out, parts_out,
    ):
        mid = tokens_ref[...] + (own_ref[...].astype(f32) + other_ref[...].astype(f32))
        mid_out[...] = mid
        normal, _ = norm_parts(mid)
        second = (normal * gain_ref[...].astype(f32)).astype(bf16)
        second_out[...] = second
        for t in range(3):
            columns = slice(t * tile, (t + 1) * tile)
            hidden = low_dot(second, up_ref[:, columns])
            factor, slope = gelu_parts(hidden)
            active_out[:, columns] = (hidden * factor).astype(bf16)
            grad_active = contract_last(cotangent_ref[...], down_ref[columns, :])
            grad_hidden_out[:, columns] = (grad_active * slope).astype(bf16)
        parts_out[:patches, :] = low_dot(active_out[...], down_ref[...]).astype(bf16)
        parts_out[PART : PART + patches, :] = contract_last(
            grad_hidden_out[...], up_ref[...]
        ).astype(bf16)

    return local_call(
        kernel,
        where,
        [],
        [tokens, own, other, gain, up, down, cotangent],
        [
            jax.ShapeDtypeStruct((patches, width), f32),
            jax.ShapeDtypeStruct((patches, width), bf16),
            jax.ShapeDtypeStruct((patches, local), bf16),
            jax.ShapeDtypeStruct((patches, local), bf16),
            jax.ShapeDtypeStruct((PART + patches, width), bf16),
        ],
        name="feed_forward",
        flops=8 * patches * up.size,
    )


def attention_backward(
    where, mid, own, other, cotangent, gain, in_proj, out_proj, query, key, value, probs
):
    patches, width = mid.shape
    half_width = width // 2
    heads = half_width // HS

    def kernel(
        where_ref, mid_ref, own_ref, other_ref, cotangent_ref, gain_ref, in_ref, out_ref,
        query_ref, key_ref, value_ref, probs_ref, layer_out, gain_out, grad_mid_out, low_out,
        query_out, key_out, value_out, part_out,
    ):
        mid_values = mid_ref[...]
        down = own_ref[:patches, :].astype(f32) + other_ref[:patches, :].astype(f32)
        layer_out[...] = (mid_values + down).astype(bf16)
        back = slice(PART, PART + patches)
        grad_second = own_ref[back, :].astype(f32) + other_ref[back, :].astype(f32)
        normal, scale = norm_parts(mid_values)
        gain_out[...] = jnp.sum(grad_second * normal, axis=0, keepdims=True)
        grad_mid = cotangent_ref[...].astype(f32) + norm_grad(
            grad_second * gain_ref[...].astype(f32), normal, scale
        )
        grad_mid_out[...] = grad_mid
        grad_low = grad_mid.astype(bf16)
        low_out[...] = grad_low
        grad_attended = contract_last(grad_low, out_ref[...]).astype(bf16)
        for pair in range(heads // 2):
            lanes = slice(pair * 2 * HS, (pair + 1) * 2 * HS)
            query, key, value = query_ref[:, lanes], key_ref[:, lanes], value_ref[:, lanes]
            totals = [None] * 3
            for side in range(2):
                mine = head_lanes(2 * HS, HS, side)
                own_grad = jnp.where(mine, grad_attended[:, lanes], 0)
                probs = probs_ref[2 * pair + side]
                grad_probs = contract_last(own_grad, value)
                inner = jnp.sum(grad_probs * probs, axis=-1, keepdims=True)
                scores = (probs * (grad_probs - inner)).astype(bf16)
                parts = (
                    low_dot(scores, jnp.where(mine, key, 0)),
                    contract_first(scores, jnp.where(mine, query, 0)),
                    contract_first(probs.astype(bf16), own_grad),
                )
                totals = [p if t is None else t + p for t, p in zip(totals, parts)]
            query_out[:, lanes] = (totals[0] * score_scale).astype(bf16)
            key_out[:, lanes] = (totals[1] * score_scale).astype(bf16)
            value_out[:, lanes] = totals[2].astype(bf16)
        part = contract_last(query_out[...], in_ref[0])
        part += contract_last(key_out[...], in_ref[1])
        part += contract_last(value_out[...], in_ref[2])
        part_out[...] = part.astype(bf16)

    def low(*dims):
        return jax.ShapeDtypeStruct(dims, bf16)

    return local_call(
        kernel,
        where,
        [],
        [mid, own, other, cotangent, gain, in_proj, out_proj, query, key, value, probs],
        [
            low(patches, width),
            jax.ShapeDtypeStruct((1, width), f32),
            jax.ShapeDtypeStruct((patches, width), f32),
            low(patches, width),
            low(patches, half_width),
            low(patches, half_width),
            low(patches, half_width),
            low(patches, width),
        ],
        name="attention_backward",
        flops=2 * patches * (in_proj.size + out_proj.size + 8 * patches * half_width),
    )


def token_grad(where, tokens, grad_mid, own, other, gain, gain_two_grad):
    patches, width = tokens.shape
    half_width = width // 2

    def kernel(
        where_ref, tokens_ref, grad_mid_ref, own_ref, other_ref, gain_ref, two_ref, half_out,
        small_out,
    ):
        grad_normed = own_ref[...].astype(f32) + other_ref[...].astype(f32)
        normal, scale = norm_parts(tokens_ref[...])
        grad_one = jnp.sum(grad_normed * normal, axis=0, keepdims=True)
        grad = grad_mid_ref[...] + norm_grad(
            grad_normed * gain_ref[...].astype(f32), normal, scale
        )
        low = grad.astype(bf16)
        half_out[...] = jnp.where(where_ref[1] == 0, low[:, :half_width], low[:, half_width:])
        small_out[...] = jnp.zeros_like(small_out)
        small_out[:patches, :] = low
        small_out[patches : patches + 1, :] = grad_one.astype(bf16)
        small_out[patches + 1 : patches + 2, :] = two_ref[...].astype(bf16)

    return local_call(
        kernel,
        where,
        [],
        [tokens, grad_mid, own, other, gain, gain_two_grad],
        [
            jax.ShapeDtypeStruct((patches, half_width), bf16),
            jax.ShapeDtypeStruct((EXTRA, width), bf16),
        ],
        name="token_grad",
    )


def wave_grads(ids_ref, blocks_ref, rows_ref, wave_count, piece):
    slots = ids_ref.shape[1]
    for s in range(slots):
        rows_ref[s * piece : (s + 1) * piece, :] = blocks_ref[s, :piece, :]
    onehot = onehot_of(ids_ref, wave_count)
    bits = 2**30 - 1
    shift = piece.bit_length() - 1
    tall = low_dot(
        equal_index(slots * piece, slots, shift, 0, bits, bits).astype(bf16), onehot.astype(bf16)
    ).astype(bf16)
    wide = low_dot(
        tall, equal_index(wave_count, wave_count * piece, 0, shift, bits, bits).astype(bf16)
    )
    same = equal_index(slots * piece, wave_count * piece, 0, 0, piece - 1, piece - 1)
    select = jnp.where(same, wide, 0.0).astype(bf16)
    kernels = contract_first(select, rows_ref[...]).astype(bf16)
    biases = jnp.concatenate(
        [
            blocks_ref[s, piece : piece + 1, :].astype(f32)
            + blocks_ref[s, piece + 1 : piece + 2, :].astype(f32)
            for s in range(slots)
        ],
        axis=0,
    )
    return kernels, exact(onehot.astype(f32), biases, FIRST)


def mix_grad(where, wave_ids, blocks, gen_rows, bias_gen, wave_count, count):
    width, half_width = bias_gen.shape
    piece = gen_rows.shape[0] // width

    def kernel(
        where_ref, ids_ref, blocks_ref, gen_ref, bias_ref, mix_out, kernels_out, biases_out, rows_ref
    ):
        kernels, biases = wave_grads(ids_ref, blocks_ref, rows_ref, wave_count, piece)
        kernels_out[...] = kernels
        biases_out[...] = biases
        products = contract_last(kernels, gen_ref[...])
        same = equal_index(*products.shape, 0, 0, piece - 1, piece - 1)
        products = jnp.where(same, products, 0.0)
        rows = jnp.sum(products.reshape(wave_count, piece, -1), axis=1)
        bits = 2**30 - 1
        gather = equal_index(
            width * piece, width, piece.bit_length() - 1, 0, bits, bits
        ).astype(f32)
        mix = exact(rows, gather)
        mix_out[...] = mix + exact(biases, bias_ref[...].astype(f32), LAST) * (1.0 / count)

    return local_call(
        kernel,
        where,
        [wave_ids],
        [blocks, gen_rows, bias_gen],
        [
            jax.ShapeDtypeStruct((wave_count, width), f32),
            jax.ShapeDtypeStruct((wave_count * piece, half_width), bf16),
            jax.ShapeDtypeStruct((wave_count, half_width), f32),
        ],
        scratch=[pltpu.VMEM((wave_ids.shape[1] * piece, half_width), bf16)],
        name="mix_grad",
        flops=2 * wave_count * piece * gen_rows.size,
    )


def generator_grads(where, mix_low, kernels, biases):
    wave_count, width = mix_low.shape
    piece = kernels.shape[0] // wave_count
    half_width = kernels.shape[1]

    def kernel(where_ref, mix_ref, kernels_ref, biases_ref, gen_out, bias_out):
        mix = mix_ref[...]
        gen_out[...] = contract_first(kron_identity(mix, piece), kernels_ref[...])
        bias_out[...] = exact(mix.astype(f32), biases_ref[...], FIRST)

    return local_call(
        kernel,
        where,
        [],
        [mix_low, kernels, biases],
        [
            jax.ShapeDtypeStruct((width * piece, half_width), f32),
            jax.ShapeDtypeStruct((width, half_width), f32),
        ],
        name="generator_grads",
        flops=2 * wave_count * piece * width * piece * half_width,
    )


def embed_part(upper, orders, where, mask, pixels, kernels):
    images, patches, pixel_count = pixels.shape
    half = images // 2

    def kernel(where_ref, mask_ref, pixel_ref, kernel_ref, *outs):
        band = where_ref[0]

        def body(q):
            for c, order in enumerate(orders):
                image = band ^ relative_index(q + half * upper, order)
                scale = mask_ref[image, band].astype(f32)
                product = jnp.dot(
                    pixel_ref[image], kernel_ref[:, span(c)], preferred_element_type=f32
                )
                outs[c][q] = (product * scale).astype(bf16)

        loop(half, body)

    return local_call(
        kernel,
        where,
        [mask],
        [pixels, kernels],
        [jax.ShapeDtypeStruct((half, patches, LANES), bf16)] * 3,
        name="embed_part",
        flops=images * patches * pixel_count * 3 * LANES,
    )


def kernel_grad(upper, orders, where, mask, pixels, grads, total, bias):
    images, patches, pixel_count = pixels.shape
    half = images // 2
    piece = pixel_count // images
    width = 3 * LANES

    def kernel(where_ref, mask_ref, pixel_ref, *refs):
        band = where_ref[0]
        grad_refs = refs[:3]
        if upper:
            old_total, old_bias, out_ref, total_ref, bias_ref = refs[3:]
            total_ref[...] = old_total[...]
            bias_ref[...] = old_bias[...]
        else:
            total_ref, bias_ref = refs[3:]
            total_ref[...] = jnp.zeros_like(total_ref)
            bias_ref[...] = jnp.zeros_like(bias_ref)

        def body(q):
            for c, order in enumerate(orders):
                image = band ^ relative_index(q + half * upper, order)

                @pl.when(mask_ref[image, band] != 0)
                def _(c=c, image=image):
                    grad = grad_refs[c][q]
                    total_ref[span(c), :] += contract_first(grad, pixel_ref[image])
                    bias_ref[:, span(c)] += jnp.sum(grad.astype(f32), axis=0, keepdims=True)

        loop(half, body)
        if upper:
            high = bias_ref[...].astype(bf16)
            low = (bias_ref[...] - high.astype(f32)).astype(bf16)
            whole = total_ref[...].T.astype(bf16)
            for k in range(images):
                out_ref[k, :piece, :] = whole[k * piece : (k + 1) * piece]
                out_ref[k, piece : piece + 1, :] = high
                out_ref[k, piece + 1 : piece + 2, :] = low

    accumulators = [
        jax.ShapeDtypeStruct((width, pixel_count), f32),
        jax.ShapeDtypeStruct((1, width), f32),
    ]
    flops = images * patches * pixel_count * width
    if not upper:
        return local_call(
            kernel, where, [mask], [pixels, *grads], accumulators, name="kernel_grad", flops=flops
        )
    return local_call(
        kernel,
        where,
        [mask],
        [pixels, *grads, total, bias],
        [jax.ShapeDtypeStruct((images, piece + 2, width), bf16)],
        scratch=[pltpu.VMEM(s.shape, f32) for s in accumulators],
        name="kernel_grad_end",
        flops=flops,
    )[0]


def pixel_grad(orders, where, mask, early, late, kernels):
    half, patches, _ = early[0].shape
    pixel_count = kernels.shape[0]

    def kernel(where_ref, mask_ref, *refs):
        early_refs, late_refs, kernel_ref, outs = refs[:3], refs[3:6], refs[6], refs[7:]
        band, head = where_ref[0], where_ref[1]

        def body(q):
            for side in range(2):
                first = head if side == 0 else 1 - head
                image = first * half + q
                parts = []
                for c, order in enumerate(orders):
                    position = position_of(image ^ band, order)
                    low = jnp.minimum(position, half - 1)
                    high = jnp.maximum(position - half, 0)
                    parts.append(
                        jnp.where(position < half, early_refs[c][low], late_refs[c][high])
                    )
                total = contract_last(jnp.concatenate(parts, axis=1), kernel_ref[...])
                outs[side][q] = (total * mask_ref[image, band].astype(f32)).astype(bf16)

        loop(half, body)

    return local_call(
        kernel,
        where,
        [mask],
        [*early, *late, kernels],
        [jax.ShapeDtypeStruct((half, patches, pixel_count), bf16)] * 2,
        name="pixel_grad",
        flops=4 * half * patches * pixel_count * 3 * LANES,
    )


def row_products(orders, count, where, lefts, rights, portions, name):
    rows = lefts[0].shape[1] // count
    half = count // 2 * rows
    widths = [sum(piece[3] for piece in portion) for portion in portions]
    if rows % 16:
        keeps, sends = [], []
        for portion, order in zip(portions, orders):
            places = jnp.asarray([relative_index(p, order) for p in range(count)], jnp.int32)
            columns = ((where[0] ^ places) * rows)[:, None] + jnp.arange(rows, dtype=jnp.int32)
            select = jnp.arange(count * rows, dtype=jnp.int32)[:, None] == columns.reshape(1, -1)
            turned = [jnp.dot(left, select.astype(bf16)) for left in lefts]
            whole = jnp.concatenate(
                [contract_first(turned[i], rights[j][:, s : s + w]) for i, j, s, w in portion],
                axis=1,
            ).astype(bf16)
            keeps.append(whole[:half])
            sends.append(whole[half:])
        return keeps, sends
    uses = sorted({(piece[0], c) for c, portion in enumerate(portions) for piece in portion})

    def kernel(where_ref, *refs):
        left_refs = refs[: len(lefts)]
        right_refs = refs[len(lefts) : len(lefts) + len(rights)]
        outs = refs[len(lefts) + len(rights) : len(lefts) + len(rights) + 6]
        turned_refs = refs[len(lefts) + len(rights) + 6 : -len(uses) - 7]
        ordered = dict(zip(uses, refs[-len(uses) - 7 : -7]))
        made, sems = refs[-7:-1], refs[-1]
        band = where_ref[0]
        for left_ref, turned_ref in zip(left_refs, turned_refs):
            turned_ref[...] = left_ref[...].T
        for (i, c), ordered_ref in ordered.items():
            for p in range(count):
                block = (band ^ relative_index(p, orders[c])) * rows
                ordered_ref[p * rows : (p + 1) * rows, :] = turned_refs[i][
                    pl.ds(pl.multiple_of(block, 16), rows), :
                ]
        copies = []
        for side in (1, 0):
            for c, portion in enumerate(portions):
                place = 0
                slot = 3 - 3 * side + c
                for i, j, start, width in portion:
                    left = ordered[i, c][side * half : (side + 1) * half, :]
                    for column in range(0, width, 256):
                        wide = min(256, width - column)
                        made[slot][:, place : place + wide] = jnp.dot(
                            left,
                            right_refs[j][:, start + column : start + column + wide],
                            preferred_element_type=f32,
                        ).astype(bf16)
                        place += wide
                copies.append(pltpu.make_async_copy(made[slot], outs[slot], sems.at[slot]))
                copies[-1].start()
        for copy in copies:
            copy.wait()

    shapes = [jax.ShapeDtypeStruct((half, width), bf16) for width in widths] * 2
    turned = [pltpu.VMEM((left.shape[1], left.shape[0]), bf16) for left in lefts]
    ordered = [pltpu.VMEM((lefts[i].shape[1], lefts[i].shape[0]), bf16) for i, _ in uses]
    outs = local_call(
        kernel,
        where,
        [],
        [*lefts, *rights],
        shapes,
        scratch=turned
        + ordered
        + [pltpu.VMEM(shape.shape, bf16) for shape in shapes]
        + [pltpu.SemaphoreType.DMA((6,))],
        spaces=[HBM] * 6,
        name=name,
        flops=2 * lefts[0].size * sum(widths),
        mebibytes=32,
    )
    return outs[3:], outs[:3]


def half_sum(where, keeps, arriving, last):
    half = keeps[0].shape[0] // 2
    widths = [keep.shape[1] for keep in keeps]

    def kernel(where_ref, *refs):
        keep_refs, arriving_refs = refs[:3], refs[3:6]
        sends, kept = (refs[6:7], refs[7:8]) if last else (refs[6:9], refs[9:12])
        place = 0
        for c in range(3):
            total = keep_refs[c][...].astype(f32) + arriving_refs[c][...].astype(f32)
            at = slice(place, place + widths[c]) if last else slice(None)
            out = 0 if last else c
            kept[out][:, at] = total[:half]
            sends[out][:, at] = total[half:].astype(bf16)
            place += widths[c]

    shapes = [(half, sum(widths))] if last else [(half, width) for width in widths]
    outs = local_call(
        kernel,
        where,
        [],
        [*keeps, *arriving],
        [jax.ShapeDtypeStruct(shape, bf16) for shape in shapes]
        + [jax.ShapeDtypeStruct(shape, f32) for shape in shapes],
        name="half_sum",
    )
    return outs[: len(shapes)], outs[len(shapes) :]


def final_sum(where, kept, arriving, ff_local, half_width, patches):
    rows = kept.shape[0]

    def kernel(
        where_ref, kept_ref, arriving_ref, up_out, down_out, in_out, out_out, pos_out, one_out,
        two_out,
    ):
        total = kept_ref[...] + arriving_ref[...].astype(f32)
        side = ff_local + EXTRA // 2
        up_out[...] = total[:, :ff_local]
        down_out[...] = total[:, side : side + ff_local]
        for k in range(3):
            in_out[k] = total[:, 2 * side + k * half_width : 2 * side + (k + 1) * half_width]
        out_out[...] = total[:, 2 * side + 3 * half_width :]
        extra = jnp.concatenate(
            [total[:, ff_local:side], total[:, side + ff_local : 2 * side]], axis=1
        )
        pos_out[...] = extra[:, :patches]
        extra = extra.T
        one_out[...] = extra[patches : patches + 1]
        two_out[...] = extra[patches + 1 : patches + 2]

    def shape(*dims):
        return jax.ShapeDtypeStruct(dims, f32)

    return local_call(
        kernel,
        where,
        [],
        [kept, arriving],
        [
            shape(rows, ff_local),
            shape(rows, ff_local),
            shape(3, rows, half_width),
            shape(rows, half_width),
            shape(rows, patches),
            shape(1, rows),
            shape(1, rows),
        ],
        name="final_sum",
    )


STEPS = (1, 2, 4, 8)
XY, YX, ZX, ZY = (8, 4, 2, 1), (8, 4, 1, 2), (8, 2, 1, 4), (8, 1, 2, 4)


def product_scratch(lefts, uses):
    return [pltpu.VMEM((left.shape[1], left.shape[0]), bf16) for left in lefts] + [
        pltpu.VMEM((lefts[i].shape[1], lefts[i].shape[0]), bf16) for i, _ in uses
    ]


def order_rows(band, left_refs, turned_refs, ordered, positions):
    rows = left_refs[0].shape[1] // 16
    for left_ref, turned_ref in zip(left_refs, turned_refs):
        turned_ref[...] = left_ref[...].T
    for (i, order), ordered_ref in ordered.items():
        for p in positions:
            block = (band ^ relative_index(p, order)) * rows
            ordered_ref[p * rows : (p + 1) * rows, :] = turned_refs[i][
                pl.ds(pl.multiple_of(block, 16), rows), :
            ]


def product_tiles(left, right_refs, portion, ordered, order, rows):
    place = 0
    for i, j, start, width in portion:
        for column in range(0, width, 256):
            wide = min(256, width - column)
            yield (
                place,
                wide,
                jnp.dot(
                    ordered[i, order][rows, :],
                    right_refs[j][:, start + column : start + column + wide],
                    preferred_element_type=f32,
                ).astype(bf16),
            )
            place += wide


def early_products(where, lefts, rights, portions, orders):
    uses = sorted({(piece[0], order) for portion, order in zip(portions, orders) for piece in portion})
    half = lefts[0].shape[1] // 2
    widths = [sum(piece[3] for piece in portion) for portion in portions]
    n = len(lefts) + len(rights)

    def kernel(where_ref, *refs):
        left_refs, right_refs = refs[: len(lefts)], refs[len(lefts) : n]
        outs, scratch = refs[n : n + len(portions)], refs[n + len(portions) :]
        ordered = dict(zip(uses, scratch[len(lefts) :]))
        order_rows(where_ref[0], left_refs, scratch[: len(lefts)], ordered, range(8, 16))
        for out, portion, order in zip(outs, portions, orders):
            tiles = product_tiles(
                None, right_refs, portion, ordered, order, slice(half, 2 * half)
            )
            for place, wide, product in tiles:
                out[:, place : place + wide] = product

    return local_call(
        kernel,
        where,
        [],
        [*lefts, *rights],
        [jax.ShapeDtypeStruct((half, width), bf16) for width in widths],
        scratch=product_scratch(lefts, uses),
        name="early_products",
        flops=lefts[0].size * sum(widths),
    )


def round_products(where, lefts, rights, early, early_orders, portions, orders):
    early_of = {0: 1, 1: 0}
    groups = [(0,), (1,), (2, 3)]
    uses = sorted(
        {
            (piece[0], order)
            for portion, order in zip([*early, *portions], [*early_orders, *orders])
            for piece in portion
        }
    )
    quarter = lefts[0].shape[1] // 4
    early_width = sum(piece[3] for piece in early[0])
    widths = [sum(piece[3] for piece in portion) for portion in portions]
    shapes = []
    for g, group in enumerate(groups):
        width = 2 * sum(widths[c] for c in group) + (early_width if g in early_of else 0)
        shapes.append(jax.ShapeDtypeStruct((quarter, width), bf16))
    n = len(lefts) + len(rights)

    def kernel(where_ref, *refs):
        left_refs, right_refs = refs[: len(lefts)], refs[len(lefts) : n]
        outs, made, sems = refs[n : n + 6], refs[-7:-1], refs[-1]
        scratch = refs[n + 6 : -7]
        ordered = dict(zip(uses, scratch[len(lefts) :]))
        order_rows(where_ref[0], left_refs, scratch[: len(lefts)], ordered, range(16))
        copies = []
        for side in (1, 0):
            for g, group in enumerate(groups):
                slot = 3 * (1 - side) + g
                base = 0
                if g in early_of:
                    e = early_of[g]
                    rows = slice(side * quarter, (side + 1) * quarter)
                    tiles = product_tiles(
                        None, right_refs, early[e], ordered, early_orders[e], rows
                    )
                    for place, wide, product in tiles:
                        made[slot][:, place : place + wide] = product
                    base = early_width
                for c in group:
                    rows = slice(side * 2 * quarter, (side + 1) * 2 * quarter)
                    tiles = product_tiles(None, right_refs, portions[c], ordered, orders[c], rows)
                    for place, wide, product in tiles:
                        for k in range(2):
                            at = base + k * widths[c] + place
                            made[slot][:, at : at + wide] = product[k * quarter : (k + 1) * quarter]
                    base += 2 * widths[c]
                copies.append(pltpu.make_async_copy(made[slot], outs[slot], sems.at[slot]))
                copies[-1].start()
        for copy in copies:
            copy.wait()

    outs = local_call(
        kernel,
        where,
        [],
        [*lefts, *rights],
        shapes * 2,
        scratch=product_scratch(lefts, uses)
        + [pltpu.VMEM(shape.shape, bf16) for shape in shapes * 2]
        + [pltpu.SemaphoreType.DMA((6,))],
        spaces=[HBM] * 6,
        name="round_products",
        flops=2 * lefts[0].size * sum(widths) + lefts[0].size * early_width,
        mebibytes=32,
    )
    return outs[:3], outs[3:]


def early_sum(where, sends, keeps, arriving):
    quarter = sends[0].shape[0]
    width = arriving[0].shape[1]
    buffers = [sends[0], keeps[0], sends[1], keeps[1]]

    def kernel(where_ref, *refs):
        arriving_refs, outs, parts, sems = refs[4:6], refs[6:10], refs[10], refs[11]
        loads = []
        for k in range(4):
            loads.append(
                pltpu.make_async_copy(refs[k].at[:, pl.ds(0, width)], parts.at[k], sems.at[k])
            )
            loads[-1].start()
        stores = []
        for k in range(4):
            loads[k].wait()
            rows = slice(quarter, 2 * quarter) if k % 2 == 0 else slice(0, quarter)
            added = arriving_refs[1 - k // 2][rows, :].astype(f32)
            parts[k] = (parts[k].astype(f32) + added).astype(bf16)
            stores.append(
                pltpu.make_async_copy(parts.at[k], outs[k].at[:, pl.ds(0, width)], sems.at[4 + k])
            )
            stores[-1].start()
        for store in stores:
            store.wait()

    smem = pl.BlockSpec(memory_space=pltpu.SMEM)
    outs = pl.pallas_call(
        kernel,
        in_specs=[smem]
        + [pl.BlockSpec(memory_space=HBM)] * 4
        + [pl.BlockSpec(memory_space=pltpu.VMEM)] * 2,
        out_specs=[pl.BlockSpec(memory_space=HBM)] * 4,
        out_shape=[jax.ShapeDtypeStruct(b.shape, bf16) for b in buffers],
        input_output_aliases={1: 0, 2: 1, 3: 2, 4: 3},
        scratch_shapes=[
            pltpu.VMEM((4, quarter, width), bf16),
            pltpu.SemaphoreType.DMA((8,)),
        ],
        compiler_params=pltpu.CompilerParams(vmem_limit_bytes=24 * 2**20),
        name="early_sum",
    )(where, *buffers, *arriving)
    return [outs[0], outs[2], sends[2]], [outs[1], outs[3], keeps[2]]


def second_sum(where, keeps, arriving, early_width, widths):
    quarter = keeps[0].shape[0]
    pair = quarter // 2
    wa, wb, wc, wd = widths

    def kernel(where_ref, *refs):
        keep_refs, arriving_refs = refs[:3], refs[3:6]
        send_y, send_x, send_z, keep_y, keep_x, keep_z = refs[6:]
        totals = [k[...].astype(f32) + a[...].astype(f32) for k, a in zip(keep_refs, arriving_refs)]
        for e, g in ((0, 1), (1, 0)):
            at = slice(e * early_width, (e + 1) * early_width)
            keep_z[:, at] = totals[g][:pair, :early_width]
            send_z[:, at] = totals[g][pair:, :early_width].astype(bf16)
        for total, start, width, keep, send, place in (
            (totals[0], early_width, wa, keep_y, send_y, 0),
            (totals[2], 2 * wc, wd, keep_y, send_y, 2 * wa),
            (totals[1], early_width, wb, keep_x, send_x, 0),
            (totals[2], 0, wc, keep_x, send_x, 2 * wb),
        ):
            for k in range(2):
                rows = slice(k * pair, (k + 1) * pair)
                at = slice(place + k * width, place + (k + 1) * width)
                keep[:, at] = total[rows, start : start + width]
                send[:, at] = total[rows, start + width : start + 2 * width].astype(bf16)

    shapes = [(pair, 2 * (wa + wd)), (pair, 2 * (wb + wc)), (pair, 2 * early_width)]
    outs = local_call(
        kernel,
        where,
        [],
        [*keeps, *arriving],
        [jax.ShapeDtypeStruct(shape, bf16) for shape in shapes]
        + [jax.ShapeDtypeStruct(shape, f32) for shape in shapes],
        name="second_sum",
    )
    return outs[:3], outs[3:]


def third_sum(where, keeps, arriving, early_width, widths):
    pair = keeps[0].shape[0]
    rows = pair // 2
    wa, wb, wc, wd = widths

    def kernel(where_ref, *refs):
        keep_refs, arriving_refs = refs[:3], refs[3:6]
        send_e, send_ab, send_c, send_d, keep_e, keep_ab, keep_c, keep_d = refs[6:]
        y, x, z = (k[...] + a[...].astype(f32) for k, a in zip(keep_refs, arriving_refs))
        keep_e[...] = z[:rows]
        send_e[...] = z[rows:].astype(bf16)
        for total, start, width, keep, send, place in (
            (y, 0, wa, keep_ab, send_ab, 0),
            (x, 0, wb, keep_ab, send_ab, wa),
            (x, 2 * wb, wc, keep_c, send_c, 0),
            (y, 2 * wa, wd, keep_d, send_d, 0),
        ):
            keep[:, place : place + width] = total[:, start : start + width]
            send[:, place : place + width] = total[:, start + width : start + 2 * width].astype(bf16)

    shapes = [(rows, 2 * early_width), (pair, wa + wb), (pair, wc), (pair, wd)]
    outs = local_call(
        kernel,
        where,
        [],
        [*keeps, *arriving],
        [jax.ShapeDtypeStruct(shape, bf16) for shape in shapes]
        + [jax.ShapeDtypeStruct(shape, f32) for shape in shapes],
        name="third_sum",
    )
    return outs[:4], outs[4:]


def fourth_sum(where, keeps, arriving):
    rows = keeps[0].shape[0] // 2
    widths = [keep.shape[1] for keep in keeps]

    def kernel(where_ref, *refs):
        send, kept = refs[6:]
        place = 0
        for keep, arrived, width in zip(refs[:3], refs[3:6], widths):
            total = keep[...] + arrived[...].astype(f32)
            kept[:, place : place + width] = total[:rows]
            send[:, place : place + width] = total[rows:].astype(bf16)
            place += width

    return local_call(
        kernel,
        where,
        [],
        [*keeps, *arriving],
        [
            jax.ShapeDtypeStruct((rows, sum(widths)), bf16),
            jax.ShapeDtypeStruct((rows, sum(widths)), f32),
        ],
        name="fourth_sum",
    )


def last_sum(where, early, early_arriving, kept, arriving, ff_local, half_width, patches):
    rows = kept.shape[0]
    early_width = early.shape[1] // 2
    rest = ff_local - early_width

    def kernel(
        where_ref, early_ref, early_arriving_ref, kept_ref, arriving_ref, up_out, down_out, in_out,
        out_out, pos_out, one_out, two_out,
    ):
        first = early_ref[...] + early_arriving_ref[...].astype(f32)
        total = kept_ref[...] + arriving_ref[...].astype(f32)
        up_out[:, :early_width] = first[:, :early_width]
        down_out[:, :early_width] = first[:, early_width:]
        up_out[:, early_width:] = total[:, :rest]
        b = rest + 256
        down_out[:, early_width:] = total[:, b : b + rest]
        in_out[0, :, :256] = total[:, rest:b]
        at = b + rest
        in_out[0, :, 256:] = total[:, at : at + half_width - 256]
        at += half_width - 256
        in_out[1] = total[:, at : at + half_width]
        in_out[2] = total[:, at + half_width : at + 2 * half_width]
        at += 2 * half_width
        out_out[...] = total[:, at : at + half_width]
        extra = total[:, at + half_width :].T
        pos_out[...] = total[:, at + half_width : at + half_width + patches]
        one_out[...] = extra[patches : patches + 1]
        two_out[...] = extra[patches + 1 : patches + 2]

    def shape(*dims):
        return jax.ShapeDtypeStruct(dims, f32)

    return local_call(
        kernel,
        where,
        [],
        [early, early_arriving, kept, arriving],
        [
            shape(rows, ff_local),
            shape(rows, ff_local),
            shape(3, rows, half_width),
            shape(rows, half_width),
            shape(rows, patches),
            shape(1, rows),
            shape(1, rows),
        ],
        name="last_sum",
    )


def in_hbm(arrays):
    return [pltpu.with_memory_space_constraint(array, pltpu.HBM) for array in arrays]


def after(values, *others):
    return lax.optimization_barrier((values, others))[0]


def shards(
    pixels,
    band_mask,
    wave_ids,
    pos_embed,
    in_proj,
    out_proj,
    up_proj,
    down_proj,
    gain_one,
    gain_two,
    kernel_gen,
    bias_gen,
    wave_table,
    hyper_in,
    hyper_out,
    hyper_up,
    hyper_down,
    hyper_gain_one,
    hyper_gain_two,
    cotangent,
):
    band_index = lax.axis_index("band")
    head_index = lax.axis_index("head")
    count = lax.axis_size("band")
    images, slot_local, patches, pixel_count = pixels.shape
    model_width = in_proj.shape[1]
    half_width = in_proj.shape[2]
    wave_count, hyper_width = wave_table.shape
    assert images == count and slot_local == 1
    orders = gather_orders(count)
    where = jnp.stack([band_index, head_index]).astype(jnp.int32)
    pixels = pixels.reshape(images, patches, pixel_count)
    wave_ids = wave_ids.reshape(1, -1)

    gen_rows = kernel_gen.reshape(-1, half_width)
    hyper_weights = [hyper_in, hyper_out, hyper_up, hyper_down]
    hyper_gains = [hyper_gain_one[None], hyper_gain_two[None]]
    slot_piece, image_bias, mix_low, *hyper_kept = hyper_forward(
        where,
        wave_ids,
        band_mask,
        wave_table,
        hyper_weights,
        hyper_gains,
        gen_rows,
        bias_gen,
        count,
    )
    slot_piece = slot_piece.reshape(count, -1, half_width)
    kernels = lax.all_to_all(slot_piece, "band", 0, 0, tiled=True).reshape(pixel_count, half_width)

    sends = embed_part(1, orders, where, band_mask, pixels, kernels)
    arriving = [hop(send, order[-1]) for send, order in zip(sends, orders)]
    keeps = embed_part(0, orders, where, band_mask, pixels, kernels)
    embed_half = jnp.concatenate(
        [part[0] for part in scatter_sum(keeps, None, orders, arriving)], axis=1
    )
    embed_low = (embed_half + image_bias).astype(bf16)
    gain_one = gain_one[None]
    gain_two = gain_two[None]
    tokens, normed_low, query, key, value, probs, attended, attn_part = attention_forward(
        where,
        embed_low,
        swap(embed_low),
        pltpu.with_memory_space_constraint(pos_embed, pltpu.HBM),
        gain_one,
        in_proj,
        out_proj,
    )
    grad_low = cotangent[0]
    mid_stream, second_low, active_low, grad_hidden, ff_parts = feed_forward(
        where,
        tokens,
        attn_part,
        swap(attn_part),
        gain_two,
        up_proj,
        pltpu.with_memory_space_constraint(down_proj, pltpu.HBM),
        grad_low,
    )
    ff_other = swap(ff_parts)

    ff_local = up_proj.shape[1]
    staged = count == 16
    if staged:
        early_width = EARLY
        ff_early = [[(0, 0, 0, early_width)], [(1, 1, 0, early_width)]]
        early_sends = early_products(
            where, [second_low, grad_low], [grad_hidden, active_low], ff_early, [XY, YX]
        )
        early_sends, ff_other = lax.optimization_barrier((early_sends, ff_other))
        early_arriving = [hop(send, step) for send, step in zip(early_sends, STEPS)]

    layer_out, gain_two_grad, grad_mid, grad_mid_low, *grad_projected, normed_part = (
        attention_backward(
            where,
            mid_stream,
            ff_parts,
            ff_other,
            grad_low,
            gain_two,
            in_proj,
            out_proj,
            query,
            key,
            value,
            probs,
        )
    )
    grad_embed_half, small = token_grad(
        where, tokens, grad_mid, normed_part, swap(normed_part), gain_one, gain_two_grad
    )

    first = hop(grad_embed_half, orders[0][0])
    lefts = [second_low, grad_low, normed_low, grad_mid_low, small]
    rights = [grad_hidden, active_low, *grad_projected, attended, jnp.eye(EXTRA, dtype=bf16)]
    side = EXTRA // 2
    if staged:
        portions = [
            [(0, 0, early_width, ff_local - early_width), (2, 2, 0, 256)],
            [(1, 1, early_width, ff_local - early_width)]
            + [(2, 2, 256, half_width - 256), (2, 3, 0, half_width - 256)],
            [(2, 3, half_width - 256, 256), (2, 4, 0, half_width)],
            [(3, 5, 0, half_width), (4, 6, 0, EXTRA)],
        ]
        widths = [sum(piece[3] for piece in portion) for portion in portions]
        sends, keeps = round_products(
            where, lefts, rights, ff_early, [XY, YX], portions, [XY, YX, ZX, ZY]
        )
        sends, keeps = early_sum(where, sends, keeps, early_arriving)
        first = after(first, (sends, keeps))
    else:
        portions = [
            [(0, 0, 0, ff_local), (4, 6, 0, side)],
            [(1, 1, 0, ff_local), (4, 6, side, side)],
            [(2, 2 + k, 0, half_width) for k in range(3)] + [(3, 5, 0, half_width)],
        ]
        keeps, sends = row_products(orders, count, where, lefts, rights, portions, "weight_grads")
        first = after(first, sends)
    early, late = [], []
    for c, order in enumerate(orders):
        block = jnp.stack([grad_embed_half[:, span(c)], first[:, span(c)]])
        for step in order[1:-1]:
            block = jnp.concatenate([block, hop(block, step)], axis=0)
        early.append(block)
        late.append(hop(block, order[-1]))
    total, bias = kernel_grad(0, orders, where, band_mask, pixels, early, None, None)
    sends, late, total = lax.optimization_barrier((sends, late, total))
    if staged:
        arriving = [hop(send, step) for send, step in zip(sends, STEPS)]
    else:
        arriving = [hop(send, order[-1]) for send, order in zip(sends, orders)]
    own_pixels, other_pixels = pixel_grad(orders, where, band_mask, early, late, kernels)
    blocks = kernel_grad(1, orders, where, band_mask, pixels, late, total, bias)
    blocks = after(blocks, own_pixels)
    spread_blocks = lax.all_to_all(blocks, "band", 0, 0, tiled=True)
    grad_pixels = (own_pixels.astype(f32) + swap(other_pixels).astype(f32)).astype(bf16)
    grad_pixels = grad_pixels[:, None]
    steps = len(orders[0])
    mixing = count // 2
    arriving = after(arriving, (spread_blocks, own_pixels))
    for t in range(steps - 1):
        last = t == steps - 2
        if not staged:
            sends, keeps = half_sum(where, keeps, arriving, last)
            if last:
                arriving = hop(sends[0], orders[0][0])
            else:
                arriving = [hop(send, order[-2 - t]) for send, order in zip(sends, orders)]
        elif t == 0:
            sends, keeps = second_sum(where, keeps, arriving, early_width, widths)
            arriving = [hop(send, step) for send, step in zip(sends, (2, 1, 4))]
        elif t == 1:
            sends, keeps = third_sum(where, keeps, arriving, early_width, widths)
            early_last, *arriving = [hop(send, step) for send, step in zip(sends, (8, 4, 2, 1))]
            early_kept, *keeps = keeps
        else:
            sends, keeps = fourth_sum(where, keeps, arriving)
            arriving = hop(sends, 8)
        if t == 0:
            grad_mix, wave_kernels, wave_biases = mix_grad(
                where, wave_ids, after(spread_blocks, sends), gen_rows, bias_gen, wave_count, count
            )
            grad_mix = grad_mix + swap(grad_mix)
        else:
            grad_mix = after(grad_mix, sends)
        while mixing and (t >= 2 or mixing > count // 8):
            grad_mix = grad_mix + hop(grad_mix, mixing)
            mixing //= 2
        if not last:
            arriving = after(arriving, grad_mix)
    hyper_grads = hyper_backward(
        where, grad_mix, wave_table, hyper_weights, hyper_gains, hyper_kept
    )
    grad_kernel_gen, grad_bias_gen = generator_grads(where, mix_low, wave_kernels, wave_biases)
    if staged:
        sums = last_sum(
            where, early_kept, early_last, keeps, arriving, ff_local, half_width, patches
        )
    else:
        sums = final_sum(where, keeps[0], arriving, ff_local, half_width, patches)
    grad_up, grad_down, grad_in_proj, grad_out_proj, grad_pos, *grad_gains = sums
    return (
        layer_out[None],
        grad_pixels,
        grad_pos.T,
        grad_in_proj,
        grad_out_proj.T,
        grad_up,
        grad_down.T,
        grad_gains[0][0],
        grad_gains[1][0],
        grad_kernel_gen.reshape(kernel_gen.shape),
        grad_bias_gen,
        *hyper_grads[:5],
        hyper_grads[5][0],
        hyper_grads[6][0],
    )


def solution(mesh):
    in_specs = (
        P(None, "band", None, None),
        P(),
        P(),
        P(),
        P(None, None, "head"),
        P("head", None),
        P(None, "head"),
        P("head", None),
        P(),
        P(),
        P(None, "band", "head"),
        P(None, "head"),
        P(),
        P(),
        P(),
        P(),
        P(),
        P(),
        P(),
        P("band", None, None),
    )
    out_specs = (
        P("band", None, None),
        P("head", "band", None, None),
        P(None, "band"),
        P(None, "band", "head"),
        P("head", "band"),
        P("band", "head"),
        P("head", "band"),
        P("band"),
        P("band"),
        P(None, "band", "head"),
        P(None, "head"),
        P(),
        P(),
        P(),
        P(),
        P(),
        P(),
        P(),
    )
    return jax.shard_map(shards, mesh=mesh, in_specs=in_specs, out_specs=out_specs, check_vma=False)
```

```python
import jax
import jax.numpy as jnp
import numpy as np
from jax import lax
from jax.experimental import pallas as pl
from jax.experimental.pallas import tpu as pltpu
from jax.sharding import PartitionSpec as P

HS = 64
HHEADS = 4
LANES = 128
EXTRA = 256
EARLY = 896
HBM = pltpu.HBM
PART = 208

highest = lax.Precision.HIGHEST
norm_epsilon = 1e-06
score_scale = 0.125
root_half = 0.7071067811865476
density_scale = 0.3989422804014327
f32 = jnp.float32
bf16 = jnp.bfloat16


def norm_parts(values):
    centered = values - jnp.mean(values, axis=-1, keepdims=True)
    variance = jnp.mean(centered * centered, axis=-1, keepdims=True)
    scale = lax.rsqrt(variance + norm_epsilon)
    return centered * scale, scale


def norm_grad(grad, normal, scale):
    inner = jnp.mean(grad, axis=-1, keepdims=True)
    along = jnp.mean(grad * normal, axis=-1, keepdims=True)
    return scale * (grad - inner - normal * along)


def gelu_parts(values):
    cumulative = 0.5 * (1.0 + lax.erf(values * root_half))
    density = jnp.exp(-0.5 * values * values) * density_scale
    return cumulative, cumulative + values * density


def contract_first(left, right):
    return lax.dot_general(left, right, (((0,), (0,)), ((), ())), preferred_element_type=f32)


def contract_last(left, right):
    return lax.dot_general(left, right, (((1,), (1,)), ((), ())), preferred_element_type=f32)


def exact(left, right, dims=((1,), (0,))):
    def product(a, b):
        return lax.dot_general(a, b, (dims, ((), ())), preferred_element_type=f32)

    left_high, right_high = left.astype(bf16), right.astype(bf16)
    left_low = (left - left_high.astype(f32)).astype(bf16)
    right_low = (right - right_high.astype(f32)).astype(bf16)
    return product(left_high, right_high) + (
        product(left_high, right_low) + product(left_low, right_high)
    )


FIRST = ((0,), (0,))
LAST = ((1,), (1,))


def low_dot(left, right):
    return jnp.dot(left, right, preferred_element_type=f32)


def equal_index(rows, columns, row_shift, column_shift, row_mask, column_mask):
    row = lax.broadcasted_iota(jnp.int32, (rows, columns), 0)
    column = lax.broadcasted_iota(jnp.int32, (rows, columns), 1)
    return ((row >> row_shift) & row_mask) == ((column >> column_shift) & column_mask)


def onehot_of(ids_ref, wave_count):
    slots = ids_ref.shape[1]
    row = lax.broadcasted_iota(jnp.int32, (slots, wave_count), 0)
    waves = jnp.zeros((slots, wave_count), jnp.int32)
    for s in range(slots):
        waves = jnp.where(row == s, ids_ref[0, s], waves)
    return waves == lax.broadcasted_iota(jnp.int32, (slots, wave_count), 1)


def spread(mix, piece):
    rows, width = mix.shape
    shift = piece.bit_length() - 1
    all_bits = 2**30 - 1
    repeat_rows = equal_index(rows * piece, rows, shift, 0, all_bits, all_bits)
    repeat_columns = equal_index(width, width * piece, 0, shift, all_bits, all_bits)
    tall = low_dot(repeat_rows.astype(bf16), mix).astype(bf16)
    return low_dot(tall, repeat_columns.astype(bf16))


def kron_identity(mix, piece):
    rows, width = mix.shape
    same = equal_index(rows * piece, width * piece, 0, 0, piece - 1, piece - 1)
    return jnp.where(same, spread(mix, piece), 0.0).astype(bf16)


def head_lanes(width, head_size, head):
    lane = lax.broadcasted_iota(jnp.int32, (1, width), 1)
    return (lane >> (head_size.bit_length() - 1)) == head


def hop(values, step):
    count = lax.axis_size("band")
    return lax.ppermute(values, "band", [(i, i ^ step) for i in range(count)])


def swap(values):
    return lax.ppermute(values, "head", [(0, 1), (1, 0)])


def head_sum(part):
    low = part.astype(bf16)
    return low.astype(f32) + swap(low).astype(f32)


def gather_orders(count):
    steps = []
    step = count // 2
    while step:
        steps.append(step)
        step //= 2
    if len(steps) < 4:
        return [tuple(steps)] * 3
    head, (c, b, a) = tuple(steps[:-3]), steps[-3:]
    return [head + (c, b, a), head + (a, c, b), head + (b, a, c)]


def relative_index(position, order):
    index = 0
    for t, step in enumerate(order):
        index = index + ((position >> t) & 1) * step
    return index


def position_of(index, order):
    position = 0
    for t, step in enumerate(order):
        position = position + (((index >> (step.bit_length() - 1)) & 1) << t)
    return position


def scatter_sum(keeps, sends, orders, arriving=None):
    if arriving is None:
        arriving = [hop(send, order[-1]) for send, order in zip(sends, orders)]
    for t in range(len(orders[0]) - 2, -1, -1):
        sends, kept = [], []
        for k, a in zip(keeps, arriving):
            half = k.shape[0] // 2
            sends.append((k[half:].astype(f32) + a[half:].astype(f32)).astype(bf16))
            kept.append(k[:half].astype(f32) + a[:half].astype(f32))
        keeps = kept
        if t == 0 and len({order[0] for order in orders}) == 1:
            merged = hop(jnp.concatenate(sends, axis=-1), orders[0][0])
            arriving, start = [], 0
            for send in sends:
                arriving.append(merged[..., start : start + send.shape[-1]])
                start += send.shape[-1]
        else:
            arriving = [hop(send, order[t]) for send, order in zip(sends, orders)]
    return [k.astype(f32) + a.astype(f32) for k, a in zip(keeps, arriving)]


def loop(count, body):
    if count <= 16:
        for q in range(count):
            body(q)
    else:

        def step(q, carry):
            body(q)
            return carry

        lax.fori_loop(0, count, step, 0)


def span(c):
    return slice(c * LANES, (c + 1) * LANES)


def local_call(
    kernel, where, tables, args, out_shape, scratch=(), name=None, flops=0, mebibytes=24,
    spaces=None,
):
    vmem = pl.BlockSpec(memory_space=pltpu.VMEM)
    smem = pl.BlockSpec(memory_space=pltpu.SMEM)
    moved = sum(x.size * x.dtype.itemsize for x in args)
    moved += sum(int(np.prod(s.shape)) * s.dtype.itemsize for s in out_shape)
    return pl.pallas_call(
        kernel,
        in_specs=[smem] * (1 + len(tables)) + [vmem] * len(args),
        out_specs=[
            pl.BlockSpec(memory_space=space or pltpu.VMEM)
            for space in spaces or [None] * len(out_shape)
        ],
        out_shape=list(out_shape),
        scratch_shapes=list(scratch),
        cost_estimate=pl.CostEstimate(flops=flops, bytes_accessed=moved, transcendentals=0),
        compiler_params=pltpu.CompilerParams(vmem_limit_bytes=mebibytes * 2**20),
        name=name,
    )(where, *tables, *args)


def hyper_forward(where, wave_ids, band_mask, table, weights, gains, gen_rows, bias_gen, count):
    slots = wave_ids.shape[1]
    wave_count, width = table.shape
    piece = gen_rows.shape[0] // width
    half_width = gen_rows.shape[1]
    inner = weights[2].shape[1]
    head_size = width // HHEADS

    def kernel(
        where_ref, ids_ref, mask_ref, table_ref, in_ref, out_ref, up_ref, down_ref, one_ref,
        two_ref, gen_ref, bias_ref, piece_out, image_bias_out, mix_out, projected_out, probs_out,
        attended_out, normal_one_out, scale_one_out, hidden_out, normal_two_out, scale_two_out,
    ):
        values = table_ref[...]
        projected = exact(values, in_ref[...])
        projected_out[...] = projected
        query, key, value = (projected[:, i * width : (i + 1) * width] for i in range(3))
        attended = jnp.zeros((wave_count, width), f32)
        for head in range(HHEADS):
            lanes = head_lanes(width, head_size, head)
            scores = exact(jnp.where(lanes, query, 0.0), key, LAST) * head_size ** (-0.5)
            scores = jnp.exp(scores - jnp.max(scores, axis=-1, keepdims=True))
            probs = scores / jnp.sum(scores, axis=-1, keepdims=True)
            probs_out[head] = probs
            attended += exact(probs, jnp.where(lanes, value, 0.0))
        attended_out[...] = attended
        normal_one, scale_one = norm_parts(values + exact(attended, out_ref[...]))
        first = normal_one * one_ref[...]
        hidden = exact(first, up_ref[...])
        factor, _ = gelu_parts(hidden)
        normal_two, scale_two = norm_parts(first + exact(hidden * factor, down_ref[...]))
        mix = (normal_two * two_ref[...]).astype(bf16)
        normal_one_out[...] = normal_one
        scale_one_out[...] = scale_one
        hidden_out[...] = hidden
        normal_two_out[...] = normal_two
        scale_two_out[...] = scale_two
        mix_out[...] = mix
        onehot = onehot_of(ids_ref, wave_count)
        slot_mix = low_dot(onehot.astype(bf16), mix).astype(bf16)
        piece_out[...] = low_dot(kron_identity(slot_mix, piece), gen_ref[...]).astype(bf16)
        image = lax.broadcasted_iota(jnp.int32, mask_ref.shape, 0) == where_ref[0]
        bands = jnp.sum(jnp.where(image, mask_ref[...], 0).astype(f32), axis=0, keepdims=True)
        waves = exact(bands, onehot.astype(f32))
        image_bias_out[...] = exact(waves, low_dot(mix, bias_ref[...]))

    def shape(*dims):
        return jax.ShapeDtypeStruct(dims, f32)

    return local_call(
        kernel,
        where,
        [wave_ids],
        [band_mask, table, *weights, *gains, gen_rows, bias_gen],
        [
            jax.ShapeDtypeStruct((slots * piece, half_width), bf16),
            shape(1, half_width),
            jax.ShapeDtypeStruct((wave_count, width), bf16),
            shape(wave_count, 3 * width),
            shape(HHEADS, wave_count, wave_count),
            shape(wave_count, width),
            shape(wave_count, width),
            shape(wave_count, 1),
            shape(wave_count, inner),
            shape(wave_count, width),
            shape(wave_count, 1),
        ],
        name="hyper_forward",
        mebibytes=56,
        flops=8 * slots * piece * gen_rows.size,
    )


def hyper_backward(where, grad_mix, table, weights, gains, kept):
    wave_count, width = table.shape
    head_size = width // HHEADS

    def kernel(
        where_ref, grad_ref, table_ref, in_ref, out_ref, up_ref, down_ref, one_ref, two_ref,
        projected_ref, probs_ref, attended_ref, normal_one_ref, scale_one_ref, hidden_ref,
        normal_two_ref, scale_two_ref, table_out, in_out, out_out, up_out, down_out, one_out,
        two_out,
    ):
        grad = grad_ref[...]
        normal_two = normal_two_ref[...]
        two_out[...] = jnp.sum(grad * normal_two, axis=0, keepdims=True)
        grad_two = norm_grad(grad * two_ref[...], normal_two, scale_two_ref[...])
        hidden = hidden_ref[...]
        factor, slope = gelu_parts(hidden)
        normal_one = normal_one_ref[...]
        first = normal_one * one_ref[...]
        grad_hidden = exact(grad_two, down_ref[...], LAST) * slope
        down_out[...] = exact(hidden * factor, grad_two, FIRST)
        up_out[...] = exact(first, grad_hidden, FIRST)
        grad_first = grad_two + exact(grad_hidden, up_ref[...], LAST)
        one_out[...] = jnp.sum(grad_first * normal_one, axis=0, keepdims=True)
        grad_one = norm_grad(grad_first * one_ref[...], normal_one, scale_one_ref[...])
        out_out[...] = exact(attended_ref[...], grad_one, FIRST)
        grad_attended = exact(grad_one, out_ref[...], LAST)
        projected = projected_ref[...]
        query, key, value = (projected[:, i * width : (i + 1) * width] for i in range(3))
        grads = [jnp.zeros((wave_count, width), f32) for _ in range(3)]
        for head in range(HHEADS):
            lanes = head_lanes(width, head_size, head)
            own = jnp.where(lanes, grad_attended, 0.0)
            probs = probs_ref[head]
            grad_probs = exact(own, value, LAST)
            grads[2] += exact(probs, own, FIRST)
            scores = probs * (grad_probs - jnp.sum(grad_probs * probs, axis=-1, keepdims=True))
            scores = scores * head_size ** (-0.5)
            grads[0] += exact(scores, jnp.where(lanes, key, 0.0))
            grads[1] += exact(scores, jnp.where(lanes, query, 0.0), FIRST)
        grad_projected = jnp.concatenate(grads, axis=1)
        in_out[...] = exact(table_ref[...], grad_projected, FIRST)
        table_out[...] = grad_one + exact(grad_projected, in_ref[...], LAST)

    arrays = [table, *weights, *gains]
    return local_call(
        kernel,
        where,
        [],
        [grad_mix, *arrays, *kept],
        [jax.ShapeDtypeStruct(a.shape, f32) for a in arrays],
        name="hyper_backward",
        flops=80 * wave_count * weights[2].size,
    )


def attention_forward(where, own, other, pos, gain, in_proj, out_proj):
    patches, half_width = own.shape
    width = 2 * half_width
    heads = half_width // HS

    def kernel(
        where_ref, own_ref, other_ref, pos_ref, gain_ref, in_ref, out_ref, tokens_out, normed_out,
        query_out, key_out, value_out, probs_out, attended_out, part_out,
    ):
        own_half, other_half = own_ref[...].astype(f32), other_ref[...].astype(f32)
        first = where_ref[1] == 0
        embed = jnp.concatenate(
            [jnp.where(first, own_half, other_half), jnp.where(first, other_half, own_half)], axis=1
        )
        tokens = embed + pos_ref[...].astype(f32)
        tokens_out[...] = tokens
        normal, _ = norm_parts(tokens)
        normed = (normal * gain_ref[...].astype(f32)).astype(bf16)
        normed_out[...] = normed
        projected = [low_dot(normed, in_ref[j]).astype(bf16) for j in range(3)]
        query_out[...], key_out[...], value_out[...] = projected
        for pair in range(heads // 2):
            lanes = slice(pair * 2 * HS, (pair + 1) * 2 * HS)
            query, key, value = (p[:, lanes] for p in projected)
            total = None
            for side in range(2):
                mine = head_lanes(2 * HS, HS, side)
                scores = contract_last(jnp.where(mine, query, 0), key) * score_scale
                scores = jnp.exp(scores - jnp.max(scores, axis=-1, keepdims=True))
                probs = scores / jnp.sum(scores, axis=-1, keepdims=True)
                probs_out[2 * pair + side] = probs
                part = low_dot(probs.astype(bf16), jnp.where(mine, value, 0))
                total = part if total is None else total + part
            attended_out[:, lanes] = total.astype(bf16)
        part_out[...] = low_dot(attended_out[...], out_ref[...]).astype(bf16)

    def low(*dims):
        return jax.ShapeDtypeStruct(dims, bf16)

    return local_call(
        kernel,
        where,
        [],
        [own, other, pos, gain, in_proj, out_proj],
        [
            jax.ShapeDtypeStruct((patches, width), f32),
            low(patches, width),
            low(patches, half_width),
            low(patches, half_width),
            low(patches, half_width),
            jax.ShapeDtypeStruct((heads, patches, patches), f32),
            low(patches, half_width),
            low(patches, width),
        ],
        name="attention_forward",
        flops=2 * patches * (in_proj.size + out_proj.size + 4 * patches * half_width),
    )


def feed_forward(where, tokens, own, other, gain, up, down, cotangent):
    patches, width = tokens.shape
    local = up.shape[1]
    tile = local // 3

    def kernel(
        where_ref, tokens_ref, own_ref, other_ref, gain_ref, up_ref, down_ref, cotangent_ref,
        mid_out, second_out, active_out, grad_hidden_out, parts_out,
    ):
        mid = tokens_ref[...] + (own_ref[...].astype(f32) + other_ref[...].astype(f32))
        mid_out[...] = mid
        normal, _ = norm_parts(mid)
        second = (normal * gain_ref[...].astype(f32)).astype(bf16)
        second_out[...] = second
        for t in range(3):
            columns = slice(t * tile, (t + 1) * tile)
            hidden = low_dot(second, up_ref[:, columns])
            factor, slope = gelu_parts(hidden)
            active_out[:, columns] = (hidden * factor).astype(bf16)
            grad_active = contract_last(cotangent_ref[...], down_ref[columns, :])
            grad_hidden_out[:, columns] = (grad_active * slope).astype(bf16)
        parts_out[:patches, :] = low_dot(active_out[...], down_ref[...]).astype(bf16)
        parts_out[PART : PART + patches, :] = contract_last(
            grad_hidden_out[...], up_ref[...]
        ).astype(bf16)

    return local_call(
        kernel,
        where,
        [],
        [tokens, own, other, gain, up, down, cotangent],
        [
            jax.ShapeDtypeStruct((patches, width), f32),
            jax.ShapeDtypeStruct((patches, width), bf16),
            jax.ShapeDtypeStruct((patches, local), bf16),
            jax.ShapeDtypeStruct((patches, local), bf16),
            jax.ShapeDtypeStruct((PART + patches, width), bf16),
        ],
        name="feed_forward",
        flops=8 * patches * up.size,
    )


def attention_backward(
    where, mid, own, other, cotangent, gain, in_proj, out_proj, query, key, value, probs
):
    patches, width = mid.shape
    half_width = width // 2
    heads = half_width // HS

    def kernel(
        where_ref, mid_ref, own_ref, other_ref, cotangent_ref, gain_ref, in_ref, out_ref,
        query_ref, key_ref, value_ref, probs_ref, layer_out, gain_out, grad_mid_out, low_out,
        query_out, key_out, value_out, part_out,
    ):
        mid_values = mid_ref[...]
        down = own_ref[:patches, :].astype(f32) + other_ref[:patches, :].astype(f32)
        layer_out[...] = (mid_values + down).astype(bf16)
        back = slice(PART, PART + patches)
        grad_second = own_ref[back, :].astype(f32) + other_ref[back, :].astype(f32)
        normal, scale = norm_parts(mid_values)
        gain_out[...] = jnp.sum(grad_second * normal, axis=0, keepdims=True)
        grad_mid = cotangent_ref[...].astype(f32) + norm_grad(
            grad_second * gain_ref[...].astype(f32), normal, scale
        )
        grad_mid_out[...] = grad_mid
        grad_low = grad_mid.astype(bf16)
        low_out[...] = grad_low
        grad_attended = contract_last(grad_low, out_ref[...]).astype(bf16)
        for pair in range(heads // 2):
            lanes = slice(pair * 2 * HS, (pair + 1) * 2 * HS)
            query, key, value = query_ref[:, lanes], key_ref[:, lanes], value_ref[:, lanes]
            totals = [None] * 3
            for side in range(2):
                mine = head_lanes(2 * HS, HS, side)
                own_grad = jnp.where(mine, grad_attended[:, lanes], 0)
                probs = probs_ref[2 * pair + side]
                grad_probs = contract_last(own_grad, value)
                inner = jnp.sum(grad_probs * probs, axis=-1, keepdims=True)
                scores = (probs * (grad_probs - inner)).astype(bf16)
                parts = (
                    low_dot(scores, jnp.where(mine, key, 0)),
                    contract_first(scores, jnp.where(mine, query, 0)),
                    contract_first(probs.astype(bf16), own_grad),
                )
                totals = [p if t is None else t + p for t, p in zip(totals, parts)]
            query_out[:, lanes] = (totals[0] * score_scale).astype(bf16)
            key_out[:, lanes] = (totals[1] * score_scale).astype(bf16)
            value_out[:, lanes] = totals[2].astype(bf16)
        part = contract_last(query_out[...], in_ref[0])
        part += contract_last(key_out[...], in_ref[1])
        part += contract_last(value_out[...], in_ref[2])
        part_out[...] = part.astype(bf16)

    def low(*dims):
        return jax.ShapeDtypeStruct(dims, bf16)

    return local_call(
        kernel,
        where,
        [],
        [mid, own, other, cotangent, gain, in_proj, out_proj, query, key, value, probs],
        [
            low(patches, width),
            jax.ShapeDtypeStruct((1, width), f32),
            jax.ShapeDtypeStruct((patches, width), f32),
            low(patches, width),
            low(patches, half_width),
            low(patches, half_width),
            low(patches, half_width),
            low(patches, width),
        ],
        name="attention_backward",
        flops=2 * patches * (in_proj.size + out_proj.size + 8 * patches * half_width),
    )


def token_grad(where, tokens, grad_mid, own, other, gain, gain_two_grad):
    patches, width = tokens.shape
    half_width = width // 2

    def kernel(
        where_ref, tokens_ref, grad_mid_ref, own_ref, other_ref, gain_ref, two_ref, half_out,
        small_out,
    ):
        grad_normed = own_ref[...].astype(f32) + other_ref[...].astype(f32)
        normal, scale = norm_parts(tokens_ref[...])
        grad_one = jnp.sum(grad_normed * normal, axis=0, keepdims=True)
        grad = grad_mid_ref[...] + norm_grad(
            grad_normed * gain_ref[...].astype(f32), normal, scale
        )
        low = grad.astype(bf16)
        half_out[...] = jnp.where(where_ref[1] == 0, low[:, :half_width], low[:, half_width:])
        small_out[...] = jnp.zeros_like(small_out)
        small_out[:patches, :] = low
        small_out[patches : patches + 1, :] = grad_one.astype(bf16)
        small_out[patches + 1 : patches + 2, :] = two_ref[...].astype(bf16)

    return local_call(
        kernel,
        where,
        [],
        [tokens, grad_mid, own, other, gain, gain_two_grad],
        [
            jax.ShapeDtypeStruct((patches, half_width), bf16),
            jax.ShapeDtypeStruct((EXTRA, width), bf16),
        ],
        name="token_grad",
    )


def wave_grads(ids_ref, blocks_ref, rows_ref, wave_count, piece):
    slots = ids_ref.shape[1]
    for s in range(slots):
        rows_ref[s * piece : (s + 1) * piece, :] = blocks_ref[s, :piece, :]
    onehot = onehot_of(ids_ref, wave_count)
    bits = 2**30 - 1
    shift = piece.bit_length() - 1
    tall = low_dot(
        equal_index(slots * piece, slots, shift, 0, bits, bits).astype(bf16), onehot.astype(bf16)
    ).astype(bf16)
    wide = low_dot(
        tall, equal_index(wave_count, wave_count * piece, 0, shift, bits, bits).astype(bf16)
    )
    same = equal_index(slots * piece, wave_count * piece, 0, 0, piece - 1, piece - 1)
    select = jnp.where(same, wide, 0.0).astype(bf16)
    kernels = contract_first(select, rows_ref[...]).astype(bf16)
    biases = jnp.concatenate(
        [
            blocks_ref[s, piece : piece + 1, :].astype(f32)
            + blocks_ref[s, piece + 1 : piece + 2, :].astype(f32)
            for s in range(slots)
        ],
        axis=0,
    )
    return kernels, exact(onehot.astype(f32), biases, FIRST)


def mix_grad(where, wave_ids, blocks, gen_rows, bias_gen, wave_count, count):
    width, half_width = bias_gen.shape
    piece = gen_rows.shape[0] // width

    def kernel(
        where_ref, ids_ref, blocks_ref, gen_ref, bias_ref, mix_out, kernels_out, biases_out, rows_ref
    ):
        kernels, biases = wave_grads(ids_ref, blocks_ref, rows_ref, wave_count, piece)
        kernels_out[...] = kernels
        biases_out[...] = biases
        products = contract_last(kernels, gen_ref[...])
        same = equal_index(*products.shape, 0, 0, piece - 1, piece - 1)
        products = jnp.where(same, products, 0.0)
        rows = jnp.sum(products.reshape(wave_count, piece, -1), axis=1)
        bits = 2**30 - 1
        gather = equal_index(
            width * piece, width, piece.bit_length() - 1, 0, bits, bits
        ).astype(f32)
        mix = exact(rows, gather)
        mix_out[...] = mix + exact(biases, bias_ref[...].astype(f32), LAST) * (1.0 / count)

    return local_call(
        kernel,
        where,
        [wave_ids],
        [blocks, gen_rows, bias_gen],
        [
            jax.ShapeDtypeStruct((wave_count, width), f32),
            jax.ShapeDtypeStruct((wave_count * piece, half_width), bf16),
            jax.ShapeDtypeStruct((wave_count, half_width), f32),
        ],
        scratch=[pltpu.VMEM((wave_ids.shape[1] * piece, half_width), bf16)],
        name="mix_grad",
        flops=2 * wave_count * piece * gen_rows.size,
    )


def generator_grads(where, mix_low, kernels, biases):
    wave_count, width = mix_low.shape
    piece = kernels.shape[0] // wave_count
    half_width = kernels.shape[1]

    def kernel(where_ref, mix_ref, kernels_ref, biases_ref, gen_out, bias_out):
        mix = mix_ref[...]
        gen_out[...] = contract_first(kron_identity(mix, piece), kernels_ref[...])
        bias_out[...] = exact(mix.astype(f32), biases_ref[...], FIRST)

    return local_call(
        kernel,
        where,
        [],
        [mix_low, kernels, biases],
        [
            jax.ShapeDtypeStruct((width * piece, half_width), f32),
            jax.ShapeDtypeStruct((width, half_width), f32),
        ],
        name="generator_grads",
        flops=2 * wave_count * piece * width * piece * half_width,
    )


def embed_part(upper, orders, where, mask, pixels, kernels):
    images, patches, pixel_count = pixels.shape
    half = images // 2

    def kernel(where_ref, mask_ref, pixel_ref, kernel_ref, *outs):
        band = where_ref[0]

        def body(q):
            for c, order in enumerate(orders):
                image = band ^ relative_index(q + half * upper, order)
                scale = mask_ref[image, band].astype(f32)
                product = jnp.dot(
                    pixel_ref[image], kernel_ref[:, span(c)], preferred_element_type=f32
                )
                outs[c][q] = (product * scale).astype(bf16)

        loop(half, body)

    return local_call(
        kernel,
        where,
        [mask],
        [pixels, kernels],
        [jax.ShapeDtypeStruct((half, patches, LANES), bf16)] * 3,
        name="embed_part",
        flops=images * patches * pixel_count * 3 * LANES,
    )


def kernel_grad(upper, orders, where, mask, pixels, grads, total, bias):
    images, patches, pixel_count = pixels.shape
    half = images // 2
    piece = pixel_count // images
    width = 3 * LANES

    def kernel(where_ref, mask_ref, pixel_ref, *refs):
        band = where_ref[0]
        grad_refs = refs[:3]
        if upper:
            old_total, old_bias, out_ref, total_ref, bias_ref = refs[3:]
            total_ref[...] = old_total[...]
            bias_ref[...] = old_bias[...]
        else:
            total_ref, bias_ref = refs[3:]
            total_ref[...] = jnp.zeros_like(total_ref)
            bias_ref[...] = jnp.zeros_like(bias_ref)

        def body(q):
            for c, order in enumerate(orders):
                image = band ^ relative_index(q + half * upper, order)

                @pl.when(mask_ref[image, band] != 0)
                def _(c=c, image=image):
                    grad = grad_refs[c][q]
                    total_ref[span(c), :] += contract_first(grad, pixel_ref[image])
                    bias_ref[:, span(c)] += jnp.sum(grad.astype(f32), axis=0, keepdims=True)

        loop(half, body)
        if upper:
            high = bias_ref[...].astype(bf16)
            low = (bias_ref[...] - high.astype(f32)).astype(bf16)
            whole = total_ref[...].T.astype(bf16)
            for k in range(images):
                out_ref[k, :piece, :] = whole[k * piece : (k + 1) * piece]
                out_ref[k, piece : piece + 1, :] = high
                out_ref[k, piece + 1 : piece + 2, :] = low

    accumulators = [
        jax.ShapeDtypeStruct((width, pixel_count), f32),
        jax.ShapeDtypeStruct((1, width), f32),
    ]
    flops = images * patches * pixel_count * width
    if not upper:
        return local_call(
            kernel, where, [mask], [pixels, *grads], accumulators, name="kernel_grad", flops=flops
        )
    return local_call(
        kernel,
        where,
        [mask],
        [pixels, *grads, total, bias],
        [jax.ShapeDtypeStruct((images, piece + 2, width), bf16)],
        scratch=[pltpu.VMEM(s.shape, f32) for s in accumulators],
        name="kernel_grad_end",
        flops=flops,
    )[0]


def pixel_grad(orders, where, mask, early, late, kernels):
    half, patches, _ = early[0].shape
    pixel_count = kernels.shape[0]

    def kernel(where_ref, mask_ref, *refs):
        early_refs, late_refs, kernel_ref, outs = refs[:3], refs[3:6], refs[6], refs[7:]
        band, head = where_ref[0], where_ref[1]

        def body(q):
            for side in range(2):
                first = head if side == 0 else 1 - head
                image = first * half + q
                parts = []
                for c, order in enumerate(orders):
                    position = position_of(image ^ band, order)
                    low = jnp.minimum(position, half - 1)
                    high = jnp.maximum(position - half, 0)
                    parts.append(
                        jnp.where(position < half, early_refs[c][low], late_refs[c][high])
                    )
                total = contract_last(jnp.concatenate(parts, axis=1), kernel_ref[...])
                outs[side][q] = (total * mask_ref[image, band].astype(f32)).astype(bf16)

        loop(half, body)

    return local_call(
        kernel,
        where,
        [mask],
        [*early, *late, kernels],
        [jax.ShapeDtypeStruct((half, patches, pixel_count), bf16)] * 2,
        name="pixel_grad",
        flops=4 * half * patches * pixel_count * 3 * LANES,
    )


def row_products(orders, count, where, lefts, rights, portions, name):
    rows = lefts[0].shape[1] // count
    half = count // 2 * rows
    widths = [sum(piece[3] for piece in portion) for portion in portions]
    if rows % 16:
        keeps, sends = [], []
        for portion, order in zip(portions, orders):
            places = jnp.asarray([relative_index(p, order) for p in range(count)], jnp.int32)
            columns = ((where[0] ^ places) * rows)[:, None] + jnp.arange(rows, dtype=jnp.int32)
            select = jnp.arange(count * rows, dtype=jnp.int32)[:, None] == columns.reshape(1, -1)
            turned = [jnp.dot(left, select.astype(bf16)) for left in lefts]
            whole = jnp.concatenate(
                [contract_first(turned[i], rights[j][:, s : s + w]) for i, j, s, w in portion],
                axis=1,
            ).astype(bf16)
            keeps.append(whole[:half])
            sends.append(whole[half:])
        return keeps, sends
    uses = sorted({(piece[0], c) for c, portion in enumerate(portions) for piece in portion})

    def kernel(where_ref, *refs):
        left_refs = refs[: len(lefts)]
        right_refs = refs[len(lefts) : len(lefts) + len(rights)]
        outs = refs[len(lefts) + len(rights) : len(lefts) + len(rights) + 6]
        turned_refs = refs[len(lefts) + len(rights) + 6 : -len(uses) - 7]
        ordered = dict(zip(uses, refs[-len(uses) - 7 : -7]))
        made, sems = refs[-7:-1], refs[-1]
        band = where_ref[0]
        for left_ref, turned_ref in zip(left_refs, turned_refs):
            turned_ref[...] = left_ref[...].T
        for (i, c), ordered_ref in ordered.items():
            for p in range(count):
                block = (band ^ relative_index(p, orders[c])) * rows
                ordered_ref[p * rows : (p + 1) * rows, :] = turned_refs[i][
                    pl.ds(pl.multiple_of(block, 16), rows), :
                ]
        copies = []
        for side in (1, 0):
            for c, portion in enumerate(portions):
                place = 0
                slot = 3 - 3 * side + c
                for i, j, start, width in portion:
                    left = ordered[i, c][side * half : (side + 1) * half, :]
                    for column in range(0, width, 256):
                        wide = min(256, width - column)
                        made[slot][:, place : place + wide] = jnp.dot(
                            left,
                            right_refs[j][:, start + column : start + column + wide],
                            preferred_element_type=f32,
                        ).astype(bf16)
                        place += wide
                copies.append(pltpu.make_async_copy(made[slot], outs[slot], sems.at[slot]))
                copies[-1].start()
        for copy in copies:
            copy.wait()

    shapes = [jax.ShapeDtypeStruct((half, width), bf16) for width in widths] * 2
    turned = [pltpu.VMEM((left.shape[1], left.shape[0]), bf16) for left in lefts]
    ordered = [pltpu.VMEM((lefts[i].shape[1], lefts[i].shape[0]), bf16) for i, _ in uses]
    outs = local_call(
        kernel,
        where,
        [],
        [*lefts, *rights],
        shapes,
        scratch=turned
        + ordered
        + [pltpu.VMEM(shape.shape, bf16) for shape in shapes]
        + [pltpu.SemaphoreType.DMA((6,))],
        spaces=[HBM] * 6,
        name=name,
        flops=2 * lefts[0].size * sum(widths),
        mebibytes=32,
    )
    return outs[3:], outs[:3]


def half_sum(where, keeps, arriving, last):
    half = keeps[0].shape[0] // 2
    widths = [keep.shape[1] for keep in keeps]

    def kernel(where_ref, *refs):
        keep_refs, arriving_refs = refs[:3], refs[3:6]
        sends, kept = (refs[6:7], refs[7:8]) if last else (refs[6:9], refs[9:12])
        place = 0
        for c in range(3):
            total = keep_refs[c][...].astype(f32) + arriving_refs[c][...].astype(f32)
            at = slice(place, place + widths[c]) if last else slice(None)
            out = 0 if last else c
            kept[out][:, at] = total[:half]
            sends[out][:, at] = total[half:].astype(bf16)
            place += widths[c]

    shapes = [(half, sum(widths))] if last else [(half, width) for width in widths]
    outs = local_call(
        kernel,
        where,
        [],
        [*keeps, *arriving],
        [jax.ShapeDtypeStruct(shape, bf16) for shape in shapes]
        + [jax.ShapeDtypeStruct(shape, f32) for shape in shapes],
        name="half_sum",
    )
    return outs[: len(shapes)], outs[len(shapes) :]


def final_sum(where, kept, arriving, ff_local, half_width, patches):
    rows = kept.shape[0]

    def kernel(
        where_ref, kept_ref, arriving_ref, up_out, down_out, in_out, out_out, pos_out, one_out,
        two_out,
    ):
        total = kept_ref[...] + arriving_ref[...].astype(f32)
        side = ff_local + EXTRA // 2
        up_out[...] = total[:, :ff_local]
        down_out[...] = total[:, side : side + ff_local]
        for k in range(3):
            in_out[k] = total[:, 2 * side + k * half_width : 2 * side + (k + 1) * half_width]
        out_out[...] = total[:, 2 * side + 3 * half_width :]
        extra = jnp.concatenate(
            [total[:, ff_local:side], total[:, side + ff_local : 2 * side]], axis=1
        )
        pos_out[...] = extra[:, :patches]
        extra = extra.T
        one_out[...] = extra[patches : patches + 1]
        two_out[...] = extra[patches + 1 : patches + 2]

    def shape(*dims):
        return jax.ShapeDtypeStruct(dims, f32)

    return local_call(
        kernel,
        where,
        [],
        [kept, arriving],
        [
            shape(rows, ff_local),
            shape(rows, ff_local),
            shape(3, rows, half_width),
            shape(rows, half_width),
            shape(rows, patches),
            shape(1, rows),
            shape(1, rows),
        ],
        name="final_sum",
    )


STEPS = (1, 2, 4, 8)
XY, YX, ZX, ZY = (8, 4, 2, 1), (8, 4, 1, 2), (8, 2, 1, 4), (8, 1, 2, 4)
XZ, YZ = (8, 2, 4, 1), (8, 1, 4, 2)


def product_scratch(lefts, uses):
    return [pltpu.VMEM((left.shape[1], left.shape[0]), bf16) for left in lefts] + [
        pltpu.VMEM((lefts[i].shape[1], lefts[i].shape[0]), bf16) for i, _ in uses
    ]


def order_rows(band, left_refs, turned_refs, ordered, positions):
    rows = left_refs[0].shape[1] // 16
    for left_ref, turned_ref in zip(left_refs, turned_refs):
        turned_ref[...] = left_ref[...].T
    for (i, order), ordered_ref in ordered.items():
        for p in positions:
            block = (band ^ relative_index(p, order)) * rows
            ordered_ref[p * rows : (p + 1) * rows, :] = turned_refs[i][
                pl.ds(pl.multiple_of(block, 16), rows), :
            ]


def product_tiles(left, right_refs, portion, ordered, order, rows):
    place = 0
    for i, j, start, width in portion:
        for column in range(0, width, 256):
            wide = min(256, width - column)
            yield (
                place,
                wide,
                jnp.dot(
                    ordered[i, order][rows, :],
                    right_refs[j][:, start + column : start + column + wide],
                    preferred_element_type=f32,
                ).astype(bf16),
            )
            place += wide


def early_products(where, lefts, rights, portions, orders):
    uses = sorted({(piece[0], order) for portion, order in zip(portions, orders) for piece in portion})
    half = lefts[0].shape[1] // 2
    widths = [sum(piece[3] for piece in portion) for portion in portions]
    n = len(lefts) + len(rights)

    def kernel(where_ref, *refs):
        left_refs, right_refs = refs[: len(lefts)], refs[len(lefts) : n]
        outs, scratch = refs[n : n + len(portions)], refs[n + len(portions) :]
        ordered = dict(zip(uses, scratch[len(lefts) :]))
        order_rows(where_ref[0], left_refs, scratch[: len(lefts)], ordered, range(8, 16))
        for out, portion, order in zip(outs, portions, orders):
            tiles = product_tiles(
                None, right_refs, portion, ordered, order, slice(half, 2 * half)
            )
            for place, wide, product in tiles:
                out[:, place : place + wide] = product

    return local_call(
        kernel,
        where,
        [],
        [*lefts, *rights],
        [jax.ShapeDtypeStruct((half, width), bf16) for width in widths],
        scratch=product_scratch(lefts, uses),
        name="early_products",
        flops=lefts[0].size * sum(widths),
    )


def round_products(where, lefts, rights, early, early_orders, portions, orders):
    early_of = {0: 1, 1: 0}
    groups = [(0, 1), (2, 3), (4, 5)]
    uses = sorted(
        {
            (piece[0], order)
            for portion, order in zip([*early, *portions], [*early_orders, *orders])
            for piece in portion
        }
    )
    quarter = lefts[0].shape[1] // 4
    early_width = sum(piece[3] for piece in early[0])
    widths = [sum(piece[3] for piece in portion) for portion in portions]
    shapes = []
    for g, group in enumerate(groups):
        width = 2 * sum(widths[c] for c in group) + (early_width if g in early_of else 0)
        shapes.append(jax.ShapeDtypeStruct((quarter, width), bf16))
    n = len(lefts) + len(rights)

    def kernel(where_ref, *refs):
        left_refs, right_refs = refs[: len(lefts)], refs[len(lefts) : n]
        outs, made, sems = refs[n : n + 6], refs[-7:-1], refs[-1]
        scratch = refs[n + 6 : -7]
        ordered = dict(zip(uses, scratch[len(lefts) :]))
        order_rows(where_ref[0], left_refs, scratch[: len(lefts)], ordered, range(16))
        copies = []
        for side in (1, 0):
            for g, group in enumerate(groups):
                slot = 3 * (1 - side) + g
                base = 0
                if g in early_of:
                    e = early_of[g]
                    rows = slice(side * quarter, (side + 1) * quarter)
                    tiles = product_tiles(
                        None, right_refs, early[e], ordered, early_orders[e], rows
                    )
                    for place, wide, product in tiles:
                        made[slot][:, place : place + wide] = product
                    base = early_width
                for c in group:
                    rows = slice(side * 2 * quarter, (side + 1) * 2 * quarter)
                    tiles = product_tiles(None, right_refs, portions[c], ordered, orders[c], rows)
                    for place, wide, product in tiles:
                        for k in range(2):
                            at = base + k * widths[c] + place
                            made[slot][:, at : at + wide] = product[k * quarter : (k + 1) * quarter]
                    base += 2 * widths[c]
                copies.append(pltpu.make_async_copy(made[slot], outs[slot], sems.at[slot]))
                copies[-1].start()
        for copy in copies:
            copy.wait()

    outs = local_call(
        kernel,
        where,
        [],
        [*lefts, *rights],
        shapes * 2,
        scratch=product_scratch(lefts, uses)
        + [pltpu.VMEM(shape.shape, bf16) for shape in shapes * 2]
        + [pltpu.SemaphoreType.DMA((6,))],
        spaces=[HBM] * 6,
        name="round_products",
        flops=2 * lefts[0].size * sum(widths) + lefts[0].size * early_width,
        mebibytes=32,
    )
    return outs[:3], outs[3:]


def early_sum(where, sends, keeps, arriving):
    quarter = sends[0].shape[0]
    width = arriving[0].shape[1]
    buffers = [sends[0], keeps[0], sends[1], keeps[1]]

    def kernel(where_ref, *refs):
        arriving_refs, outs, parts, sems = refs[4:6], refs[6:10], refs[10], refs[11]
        loads = []
        for k in range(4):
            loads.append(
                pltpu.make_async_copy(refs[k].at[:, pl.ds(0, width)], parts.at[k], sems.at[k])
            )
            loads[-1].start()
        stores = []
        for k in range(4):
            loads[k].wait()
            rows = slice(quarter, 2 * quarter) if k % 2 == 0 else slice(0, quarter)
            added = arriving_refs[1 - k // 2][rows, :].astype(f32)
            parts[k] = (parts[k].astype(f32) + added).astype(bf16)
            stores.append(
                pltpu.make_async_copy(parts.at[k], outs[k].at[:, pl.ds(0, width)], sems.at[4 + k])
            )
            stores[-1].start()
        for store in stores:
            store.wait()

    smem = pl.BlockSpec(memory_space=pltpu.SMEM)
    outs = pl.pallas_call(
        kernel,
        in_specs=[smem]
        + [pl.BlockSpec(memory_space=HBM)] * 4
        + [pl.BlockSpec(memory_space=pltpu.VMEM)] * 2,
        out_specs=[pl.BlockSpec(memory_space=HBM)] * 4,
        out_shape=[jax.ShapeDtypeStruct(b.shape, bf16) for b in buffers],
        input_output_aliases={1: 0, 2: 1, 3: 2, 4: 3},
        scratch_shapes=[
            pltpu.VMEM((4, quarter, width), bf16),
            pltpu.SemaphoreType.DMA((8,)),
        ],
        compiler_params=pltpu.CompilerParams(vmem_limit_bytes=24 * 2**20),
        name="early_sum",
    )(where, *buffers, *arriving)
    return [outs[0], outs[2], sends[2]], [outs[1], outs[3], keeps[2]]


def second_sum(where, keeps, arriving, early_width, widths):
    quarter = keeps[0].shape[0]
    pair = quarter // 2
    starts = [early_width, early_width + 2 * widths[0]] + [0] * 4
    starts[2:4] = [early_width, early_width + 2 * widths[2]]
    starts[4:] = [0, 2 * widths[4]]
    rounds = [(0, (0, 5)), (0, (2, 4)), (2 * early_width, (1, 3))]

    def kernel(where_ref, *refs):
        keep_refs, arriving_refs = refs[:3], refs[3:6]
        sends, kept = refs[6:9], refs[9:]
        totals = [k[...].astype(f32) + a[...].astype(f32) for k, a in zip(keep_refs, arriving_refs)]
        for e, g in ((0, 1), (1, 0)):
            at = slice(e * early_width, (e + 1) * early_width)
            kept[2][:, at] = totals[g][:pair, :early_width]
            sends[2][:, at] = totals[g][pair:, :early_width].astype(bf16)
        for (place, group), keep, send in zip(rounds, kept, sends):
            for c in group:
                total, start, width = totals[c // 2], starts[c], widths[c]
                for k in range(2):
                    rows = slice(k * pair, (k + 1) * pair)
                    at = slice(place + k * width, place + (k + 1) * width)
                    keep[:, at] = total[rows, start : start + width]
                    send[:, at] = total[rows, start + width : start + 2 * width].astype(bf16)
                place += 2 * width

    shapes = [(pair, place + 2 * sum(widths[c] for c in group)) for place, group in rounds]
    outs = local_call(
        kernel,
        where,
        [],
        [*keeps, *arriving],
        [jax.ShapeDtypeStruct(shape, bf16) for shape in shapes]
        + [jax.ShapeDtypeStruct(shape, f32) for shape in shapes],
        name="second_sum",
    )
    return outs[:3], outs[3:]


def third_sum(where, keeps, arriving, early_width, widths):
    pair = keeps[0].shape[0]
    rows = pair // 2
    place_in = {0: (0, 0), 5: (0, 2 * widths[0]), 2: (1, 0), 4: (1, 2 * widths[2])}
    place_in[1] = (2, 2 * early_width)
    place_in[3] = (2, 2 * early_width + 2 * widths[1])
    rounds = [(0, 2), (4, 1), (5, 3)]

    def kernel(where_ref, *refs):
        keep_refs, arriving_refs = refs[:3], refs[3:6]
        sends, kept = refs[6:10], refs[10:]
        totals = [k[...] + a[...].astype(f32) for k, a in zip(keep_refs, arriving_refs)]
        kept[0][...] = totals[2][:rows, : 2 * early_width]
        sends[0][...] = totals[2][rows:, : 2 * early_width].astype(bf16)
        for group, keep, send in zip(rounds, kept[1:], sends[1:]):
            place = 0
            for c in group:
                (g, start), width = place_in[c], widths[c]
                at = slice(place, place + width)
                keep[:, at] = totals[g][:, start : start + width]
                send[:, at] = totals[g][:, start + width : start + 2 * width].astype(bf16)
                place += width

    shapes = [(rows, 2 * early_width)] + [
        (pair, sum(widths[c] for c in group)) for group in rounds
    ]
    outs = local_call(
        kernel,
        where,
        [],
        [*keeps, *arriving],
        [jax.ShapeDtypeStruct(shape, bf16) for shape in shapes]
        + [jax.ShapeDtypeStruct(shape, f32) for shape in shapes],
        name="third_sum",
    )
    return outs[:4], outs[4:]


def fourth_sum(where, keeps, arriving):
    rows = keeps[0].shape[0] // 2
    widths = [keep.shape[1] for keep in keeps]

    def kernel(where_ref, *refs):
        send, kept = refs[6:]
        place = 0
        for keep, arrived, width in zip(refs[:3], refs[3:6], widths):
            total = keep[...] + arrived[...].astype(f32)
            kept[:, place : place + width] = total[:rows]
            send[:, place : place + width] = total[rows:].astype(bf16)
            place += width

    return local_call(
        kernel,
        where,
        [],
        [*keeps, *arriving],
        [
            jax.ShapeDtypeStruct((rows, sum(widths)), bf16),
            jax.ShapeDtypeStruct((rows, sum(widths)), f32),
        ],
        name="fourth_sum",
    )


def last_sum(where, early, early_arriving, kept, arriving, ff_local, half_width, patches):
    rows = kept.shape[0]
    early_width = early.shape[1] // 2
    rest = ff_local - early_width

    def kernel(
        where_ref, early_ref, early_arriving_ref, kept_ref, arriving_ref, up_out, down_out, in_out,
        out_out, pos_out, one_out, two_out,
    ):
        first = early_ref[...] + early_arriving_ref[...].astype(f32)
        total = kept_ref[...] + arriving_ref[...].astype(f32)
        up_out[:, :early_width] = first[:, :early_width]
        down_out[:, :early_width] = first[:, early_width:]
        up_out[:, early_width:] = total[:, :rest]
        down_out[:, early_width:] = total[:, rest : 2 * rest]
        at = 2 * rest
        in_out[1, :, half_width - 256 :] = total[:, at : at + 256]
        in_out[2] = total[:, at + 256 : at + 256 + half_width]
        at += 256 + half_width
        in_out[0, :, :256] = total[:, at : at + 256]
        at += 256
        out_out[...] = total[:, at : at + half_width]
        extra = total[:, at + half_width : at + half_width + EXTRA].T
        b = at + half_width + EXTRA
        in_out[0, :, 256:] = total[:, b : b + half_width - 256]
        in_out[1, :, : half_width - 256] = total[:, b + half_width - 256 :]
        pos_out[...] = total[:, at + half_width : at + half_width + patches]
        one_out[...] = extra[patches : patches + 1]
        two_out[...] = extra[patches + 1 : patches + 2]

    def shape(*dims):
        return jax.ShapeDtypeStruct(dims, f32)

    return local_call(
        kernel,
        where,
        [],
        [early, early_arriving, kept, arriving],
        [
            shape(rows, ff_local),
            shape(rows, ff_local),
            shape(3, rows, half_width),
            shape(rows, half_width),
            shape(rows, patches),
            shape(1, rows),
            shape(1, rows),
        ],
        name="last_sum",
    )


def in_hbm(arrays):
    return [pltpu.with_memory_space_constraint(array, pltpu.HBM) for array in arrays]


def after(values, *others):
    return lax.optimization_barrier((values, others))[0]


def shards(
    pixels,
    band_mask,
    wave_ids,
    pos_embed,
    in_proj,
    out_proj,
    up_proj,
    down_proj,
    gain_one,
    gain_two,
    kernel_gen,
    bias_gen,
    wave_table,
    hyper_in,
    hyper_out,
    hyper_up,
    hyper_down,
    hyper_gain_one,
    hyper_gain_two,
    cotangent,
):
    band_index = lax.axis_index("band")
    head_index = lax.axis_index("head")
    count = lax.axis_size("band")
    images, slot_local, patches, pixel_count = pixels.shape
    model_width = in_proj.shape[1]
    half_width = in_proj.shape[2]
    wave_count, hyper_width = wave_table.shape
    assert images == count and slot_local == 1
    orders = gather_orders(count)
    where = jnp.stack([band_index, head_index]).astype(jnp.int32)
    pixels = pixels.reshape(images, patches, pixel_count)
    wave_ids = wave_ids.reshape(1, -1)

    gen_rows = kernel_gen.reshape(-1, half_width)
    hyper_weights = [hyper_in, hyper_out, hyper_up, hyper_down]
    hyper_gains = [hyper_gain_one[None], hyper_gain_two[None]]
    slot_piece, image_bias, mix_low, *hyper_kept = hyper_forward(
        where,
        wave_ids,
        band_mask,
        wave_table,
        hyper_weights,
        hyper_gains,
        gen_rows,
        bias_gen,
        count,
    )
    slot_piece = slot_piece.reshape(count, -1, half_width)
    kernels = lax.all_to_all(slot_piece, "band", 0, 0, tiled=True).reshape(pixel_count, half_width)

    sends = embed_part(1, orders, where, band_mask, pixels, kernels)
    arriving = [hop(send, order[-1]) for send, order in zip(sends, orders)]
    keeps = embed_part(0, orders, where, band_mask, pixels, kernels)
    embed_half = jnp.concatenate(
        [part[0] for part in scatter_sum(keeps, None, orders, arriving)], axis=1
    )
    embed_low = (embed_half + image_bias).astype(bf16)
    gain_one = gain_one[None]
    gain_two = gain_two[None]
    tokens, normed_low, query, key, value, probs, attended, attn_part = attention_forward(
        where,
        embed_low,
        swap(embed_low),
        pltpu.with_memory_space_constraint(pos_embed, pltpu.HBM),
        gain_one,
        in_proj,
        out_proj,
    )
    grad_low = cotangent[0]
    mid_stream, second_low, active_low, grad_hidden, ff_parts = feed_forward(
        where,
        tokens,
        attn_part,
        swap(attn_part),
        gain_two,
        up_proj,
        pltpu.with_memory_space_constraint(down_proj, pltpu.HBM),
        grad_low,
    )
    ff_other = swap(ff_parts)

    ff_local = up_proj.shape[1]
    staged = count == 16
    if staged:
        early_width = EARLY
        ff_early = [[(0, 0, 0, early_width)], [(1, 1, 0, early_width)]]
        early_sends = early_products(
            where, [second_low, grad_low], [grad_hidden, active_low], ff_early, [XY, YX]
        )
        early_sends, ff_other = lax.optimization_barrier((early_sends, ff_other))
        early_arriving = [hop(send, step) for send, step in zip(early_sends, STEPS)]

    layer_out, gain_two_grad, grad_mid, grad_mid_low, *grad_projected, normed_part = (
        attention_backward(
            where,
            mid_stream,
            ff_parts,
            ff_other,
            grad_low,
            gain_two,
            in_proj,
            out_proj,
            query,
            key,
            value,
            probs,
        )
    )
    grad_embed_half, small = token_grad(
        where, tokens, grad_mid, normed_part, swap(normed_part), gain_one, gain_two_grad
    )

    first = hop(grad_embed_half, orders[0][0])
    lefts = [second_low, grad_low, normed_low, grad_mid_low, small]
    rights = [grad_hidden, active_low, *grad_projected, attended, jnp.eye(EXTRA, dtype=bf16)]
    side = EXTRA // 2
    if staged:
        portions = [
            [(0, 0, early_width, ff_local - early_width)],
            [(2, 2, 0, 256)],
            [(1, 1, early_width, ff_local - early_width)],
            [(2, 2, 256, half_width - 256), (2, 3, 0, half_width - 256)],
            [(2, 3, half_width - 256, 256), (2, 4, 0, half_width)],
            [(3, 5, 0, half_width), (4, 6, 0, EXTRA)],
        ]
        widths = [sum(piece[3] for piece in portion) for portion in portions]
        sends, keeps = round_products(
            where, lefts, rights, ff_early, [XY, YX], portions, [XY, XZ, YX, YZ, ZX, ZY]
        )
        first = after(first, (sends, early_arriving))
    else:
        portions = [
            [(0, 0, 0, ff_local), (4, 6, 0, side)],
            [(1, 1, 0, ff_local), (4, 6, side, side)],
            [(2, 2 + k, 0, half_width) for k in range(3)] + [(3, 5, 0, half_width)],
        ]
        keeps, sends = row_products(orders, count, where, lefts, rights, portions, "weight_grads")
        first = after(first, sends)
    early, late = [], []
    for c, order in enumerate(orders):
        block = jnp.stack([grad_embed_half[:, span(c)], first[:, span(c)]])
        for step in order[1:-1]:
            block = jnp.concatenate([block, hop(block, step)], axis=0)
        early.append(block)
        late.append(hop(block, order[-1]))
    total, bias = kernel_grad(0, orders, where, band_mask, pixels, early, None, None)
    if staged:
        sends, keeps = early_sum(where, sends, keeps, after(early_arriving, early))
    sends, late, total = lax.optimization_barrier((sends, late, total))
    if staged:
        arriving = [hop(send, step) for send, step in zip(sends, STEPS)]
    else:
        arriving = [hop(send, order[-1]) for send, order in zip(sends, orders)]
    own_pixels, other_pixels = pixel_grad(orders, where, band_mask, early, late, kernels)
    blocks = kernel_grad(1, orders, where, band_mask, pixels, late, total, bias)
    blocks = after(blocks, own_pixels)
    spread_blocks = lax.all_to_all(blocks, "band", 0, 0, tiled=True)
    grad_pixels = (own_pixels.astype(f32) + swap(other_pixels).astype(f32)).astype(bf16)
    grad_pixels = grad_pixels[:, None]
    steps = len(orders[0])
    mixing = count // 2
    arriving = after(arriving, (spread_blocks, own_pixels))
    for t in range(steps - 1):
        last = t == steps - 2
        if not staged:
            sends, keeps = half_sum(where, keeps, arriving, last)
            if last:
                arriving = hop(sends[0], orders[0][0])
            else:
                arriving = [hop(send, order[-2 - t]) for send, order in zip(sends, orders)]
        elif t == 0:
            sends, keeps = second_sum(where, in_hbm(keeps), arriving, early_width, widths)
            arriving = [hop(send, step) for send, step in zip(sends, (2, 1, 4))]
        elif t == 1:
            sends, keeps = third_sum(where, keeps, arriving, early_width, widths)
            early_last, *arriving = [hop(send, step) for send, step in zip(sends, (8, 4, 2, 1))]
            early_kept, *keeps = keeps
        else:
            sends, keeps = fourth_sum(where, keeps, arriving)
            arriving = hop(sends, 8)
        if t == 0:
            grad_mix, wave_kernels, wave_biases = mix_grad(
                where, wave_ids, after(spread_blocks, sends), gen_rows, bias_gen, wave_count, count
            )
            grad_mix = grad_mix + swap(grad_mix)
        else:
            grad_mix = after(grad_mix, sends)
        while mixing and (t >= 2 or mixing > count // 8):
            grad_mix = grad_mix + hop(grad_mix, mixing)
            mixing //= 2
        if not last:
            arriving = after(arriving, grad_mix)
    hyper_grads = hyper_backward(
        where, grad_mix, wave_table, hyper_weights, hyper_gains, hyper_kept
    )
    grad_kernel_gen, grad_bias_gen = generator_grads(where, mix_low, wave_kernels, wave_biases)
    if staged:
        sums = last_sum(
            where, early_kept, early_last, keeps, arriving, ff_local, half_width, patches
        )
    else:
        sums = final_sum(where, keeps[0], arriving, ff_local, half_width, patches)
    grad_up, grad_down, grad_in_proj, grad_out_proj, grad_pos, *grad_gains = sums
    return (
        layer_out[None],
        grad_pixels,
        grad_pos.T,
        grad_in_proj,
        grad_out_proj.T,
        grad_up,
        grad_down.T,
        grad_gains[0][0],
        grad_gains[1][0],
        grad_kernel_gen.reshape(kernel_gen.shape),
        grad_bias_gen,
        *hyper_grads[:5],
        hyper_grads[5][0],
        hyper_grads[6][0],
    )


def solution(mesh):
    in_specs = (
        P(None, "band", None, None),
        P(),
        P(),
        P(),
        P(None, None, "head"),
        P("head", None),
        P(None, "head"),
        P("head", None),
        P(),
        P(),
        P(None, "band", "head"),
        P(None, "head"),
        P(),
        P(),
        P(),
        P(),
        P(),
        P(),
        P(),
        P("band", None, None),
    )
    out_specs = (
        P("band", None, None),
        P("head", "band", None, None),
        P(None, "band"),
        P(None, "band", "head"),
        P("head", "band"),
        P("band", "head"),
        P("head", "band"),
        P("band"),
        P("band"),
        P(None, "band", "head"),
        P(None, "head"),
        P(),
        P(),
        P(),
        P(),
        P(),
        P(),
        P(),
    )
    return jax.shard_map(shards, mesh=mesh, in_specs=in_specs, out_specs=out_specs, check_vma=False)
```

```python
import jax
import jax.numpy as jnp
import numpy as np
from jax import lax
from jax.experimental import pallas as pl
from jax.experimental.pallas import tpu as pltpu
from jax.sharding import PartitionSpec as P

HS = 64
HHEADS = 4
LANES = 128
EXTRA = 256
EARLY = 896
HBM = pltpu.HBM
PART = 208

highest = lax.Precision.HIGHEST
norm_epsilon = 1e-06
score_scale = 0.125
root_half = 0.7071067811865476
density_scale = 0.3989422804014327
f32 = jnp.float32
bf16 = jnp.bfloat16


def norm_parts(values):
    centered = values - jnp.mean(values, axis=-1, keepdims=True)
    variance = jnp.mean(centered * centered, axis=-1, keepdims=True)
    scale = lax.rsqrt(variance + norm_epsilon)
    return centered * scale, scale


def norm_grad(grad, normal, scale):
    inner = jnp.mean(grad, axis=-1, keepdims=True)
    along = jnp.mean(grad * normal, axis=-1, keepdims=True)
    return scale * (grad - inner - normal * along)


def gelu_parts(values):
    cumulative = 0.5 * (1.0 + lax.erf(values * root_half))
    density = jnp.exp(-0.5 * values * values) * density_scale
    return cumulative, cumulative + values * density


def contract_first(left, right):
    return lax.dot_general(left, right, (((0,), (0,)), ((), ())), preferred_element_type=f32)


def contract_last(left, right):
    return lax.dot_general(left, right, (((1,), (1,)), ((), ())), preferred_element_type=f32)


def exact(left, right, dims=((1,), (0,))):
    def product(a, b):
        return lax.dot_general(a, b, (dims, ((), ())), preferred_element_type=f32)

    left_high, right_high = left.astype(bf16), right.astype(bf16)
    left_low = (left - left_high.astype(f32)).astype(bf16)
    right_low = (right - right_high.astype(f32)).astype(bf16)
    return product(left_high, right_high) + (
        product(left_high, right_low) + product(left_low, right_high)
    )


FIRST = ((0,), (0,))
LAST = ((1,), (1,))


def low_dot(left, right):
    return jnp.dot(left, right, preferred_element_type=f32)


def equal_index(rows, columns, row_shift, column_shift, row_mask, column_mask):
    row = lax.broadcasted_iota(jnp.int32, (rows, columns), 0)
    column = lax.broadcasted_iota(jnp.int32, (rows, columns), 1)
    return ((row >> row_shift) & row_mask) == ((column >> column_shift) & column_mask)


def onehot_of(ids_ref, wave_count):
    slots = ids_ref.shape[1]
    row = lax.broadcasted_iota(jnp.int32, (slots, wave_count), 0)
    waves = jnp.zeros((slots, wave_count), jnp.int32)
    for s in range(slots):
        waves = jnp.where(row == s, ids_ref[0, s], waves)
    return waves == lax.broadcasted_iota(jnp.int32, (slots, wave_count), 1)


def spread(mix, piece):
    rows, width = mix.shape
    shift = piece.bit_length() - 1
    all_bits = 2**30 - 1
    repeat_rows = equal_index(rows * piece, rows, shift, 0, all_bits, all_bits)
    repeat_columns = equal_index(width, width * piece, 0, shift, all_bits, all_bits)
    tall = low_dot(repeat_rows.astype(bf16), mix).astype(bf16)
    return low_dot(tall, repeat_columns.astype(bf16))


def kron_identity(mix, piece):
    rows, width = mix.shape
    same = equal_index(rows * piece, width * piece, 0, 0, piece - 1, piece - 1)
    return jnp.where(same, spread(mix, piece), 0.0).astype(bf16)


def head_lanes(width, head_size, head):
    lane = lax.broadcasted_iota(jnp.int32, (1, width), 1)
    return (lane >> (head_size.bit_length() - 1)) == head


def hop(values, step):
    count = lax.axis_size("band")
    return lax.ppermute(values, "band", [(i, i ^ step) for i in range(count)])


def swap(values):
    return lax.ppermute(values, "head", [(0, 1), (1, 0)])


def head_sum(part):
    low = part.astype(bf16)
    return low.astype(f32) + swap(low).astype(f32)


def gather_orders(count):
    steps = []
    step = count // 2
    while step:
        steps.append(step)
        step //= 2
    if len(steps) < 4:
        return [tuple(steps)] * 3
    head, (c, b, a) = tuple(steps[:-3]), steps[-3:]
    return [head + (c, b, a), head + (a, c, b), head + (b, a, c)]


def relative_index(position, order):
    index = 0
    for t, step in enumerate(order):
        index = index + ((position >> t) & 1) * step
    return index


def position_of(index, order):
    position = 0
    for t, step in enumerate(order):
        position = position + (((index >> (step.bit_length() - 1)) & 1) << t)
    return position


def scatter_sum(keeps, sends, orders, arriving=None):
    if arriving is None:
        arriving = [hop(send, order[-1]) for send, order in zip(sends, orders)]
    for t in range(len(orders[0]) - 2, -1, -1):
        sends, kept = [], []
        for k, a in zip(keeps, arriving):
            half = k.shape[0] // 2
            sends.append((k[half:].astype(f32) + a[half:].astype(f32)).astype(bf16))
            kept.append(k[:half].astype(f32) + a[:half].astype(f32))
        keeps = kept
        if t == 0 and len({order[0] for order in orders}) == 1:
            merged = hop(jnp.concatenate(sends, axis=-1), orders[0][0])
            arriving, start = [], 0
            for send in sends:
                arriving.append(merged[..., start : start + send.shape[-1]])
                start += send.shape[-1]
        else:
            arriving = [hop(send, order[t]) for send, order in zip(sends, orders)]
    return [k.astype(f32) + a.astype(f32) for k, a in zip(keeps, arriving)]


def loop(count, body):
    if count <= 16:
        for q in range(count):
            body(q)
    else:

        def step(q, carry):
            body(q)
            return carry

        lax.fori_loop(0, count, step, 0)


def span(c):
    return slice(c * LANES, (c + 1) * LANES)


def local_call(
    kernel, where, tables, args, out_shape, scratch=(), name=None, flops=0, mebibytes=24,
    spaces=None,
):
    vmem = pl.BlockSpec(memory_space=pltpu.VMEM)
    smem = pl.BlockSpec(memory_space=pltpu.SMEM)
    moved = sum(x.size * x.dtype.itemsize for x in args)
    moved += sum(int(np.prod(s.shape)) * s.dtype.itemsize for s in out_shape)
    return pl.pallas_call(
        kernel,
        in_specs=[smem] * (1 + len(tables)) + [vmem] * len(args),
        out_specs=[
            pl.BlockSpec(memory_space=space or pltpu.VMEM)
            for space in spaces or [None] * len(out_shape)
        ],
        out_shape=list(out_shape),
        scratch_shapes=list(scratch),
        cost_estimate=pl.CostEstimate(flops=flops, bytes_accessed=moved, transcendentals=0),
        compiler_params=pltpu.CompilerParams(vmem_limit_bytes=mebibytes * 2**20),
        name=name,
    )(where, *tables, *args)


def hyper_forward(where, wave_ids, band_mask, table, weights, gains, gen_rows, bias_gen, count):
    slots = wave_ids.shape[1]
    wave_count, width = table.shape
    piece = gen_rows.shape[0] // width
    half_width = gen_rows.shape[1]
    inner = weights[2].shape[1]
    head_size = width // HHEADS

    def kernel(
        ids_ref, mask_ref, table_ref, in_ref, out_ref, up_ref, down_ref, one_ref,
        two_ref, gen_ref, bias_ref, piece_out, image_bias_out, mix_out, projected_out, probs_out,
        attended_out, normal_one_out, scale_one_out, hidden_out, normal_two_out, scale_two_out,
    ):
        values = table_ref[...]
        projected = exact(values, in_ref[...])
        projected_out[...] = projected
        query, key, value = (projected[:, i * width : (i + 1) * width] for i in range(3))
        attended = jnp.zeros((wave_count, width), f32)
        for head in range(HHEADS):
            lanes = head_lanes(width, head_size, head)
            scores = exact(jnp.where(lanes, query, 0.0), key, LAST) * head_size ** (-0.5)
            scores = jnp.exp(scores - jnp.max(scores, axis=-1, keepdims=True))
            probs = scores / jnp.sum(scores, axis=-1, keepdims=True)
            probs_out[head] = probs
            attended += exact(probs, jnp.where(lanes, value, 0.0))
        attended_out[...] = attended
        normal_one, scale_one = norm_parts(values + exact(attended, out_ref[...]))
        first = normal_one * one_ref[...]
        hidden = exact(first, up_ref[...])
        factor, _ = gelu_parts(hidden)
        normal_two, scale_two = norm_parts(first + exact(hidden * factor, down_ref[...]))
        mix = (normal_two * two_ref[...]).astype(bf16)
        normal_one_out[...] = normal_one
        scale_one_out[...] = scale_one
        hidden_out[...] = hidden
        normal_two_out[...] = normal_two
        scale_two_out[...] = scale_two
        mix_out[...] = mix
        onehot = onehot_of(ids_ref, wave_count)
        slot_mix = low_dot(onehot.astype(bf16), mix).astype(bf16)
        piece_out[...] = low_dot(kron_identity(slot_mix, piece), gen_ref[...]).astype(bf16)
        waves = exact(mask_ref[...].astype(f32), onehot.astype(f32))
        image_bias_out[...] = exact(waves, low_dot(mix, bias_ref[...]))

    def shape(*dims):
        return jax.ShapeDtypeStruct(dims, f32)

    return local_call(
        kernel,
        wave_ids,
        [],
        [band_mask, table, *weights, *gains, gen_rows, bias_gen],
        [
            jax.ShapeDtypeStruct((slots * piece, half_width), bf16),
            shape(band_mask.shape[0], half_width),
            jax.ShapeDtypeStruct((wave_count, width), bf16),
            shape(wave_count, 3 * width),
            shape(HHEADS, wave_count, wave_count),
            shape(wave_count, width),
            shape(wave_count, width),
            shape(wave_count, 1),
            shape(wave_count, inner),
            shape(wave_count, width),
            shape(wave_count, 1),
        ],
        name="hyper_forward",
        mebibytes=56,
        flops=8 * slots * piece * gen_rows.size,
    )


def hyper_backward(where, grad_mix, table, weights, gains, kept):
    wave_count, width = table.shape
    head_size = width // HHEADS

    def kernel(
        where_ref, grad_ref, table_ref, in_ref, out_ref, up_ref, down_ref, one_ref, two_ref,
        projected_ref, probs_ref, attended_ref, normal_one_ref, scale_one_ref, hidden_ref,
        normal_two_ref, scale_two_ref, table_out, in_out, out_out, up_out, down_out, one_out,
        two_out,
    ):
        grad = grad_ref[...]
        normal_two = normal_two_ref[...]
        two_out[...] = jnp.sum(grad * normal_two, axis=0, keepdims=True)
        grad_two = norm_grad(grad * two_ref[...], normal_two, scale_two_ref[...])
        hidden = hidden_ref[...]
        factor, slope = gelu_parts(hidden)
        normal_one = normal_one_ref[...]
        first = normal_one * one_ref[...]
        grad_hidden = exact(grad_two, down_ref[...], LAST) * slope
        down_out[...] = exact(hidden * factor, grad_two, FIRST)
        up_out[...] = exact(first, grad_hidden, FIRST)
        grad_first = grad_two + exact(grad_hidden, up_ref[...], LAST)
        one_out[...] = jnp.sum(grad_first * normal_one, axis=0, keepdims=True)
        grad_one = norm_grad(grad_first * one_ref[...], normal_one, scale_one_ref[...])
        out_out[...] = exact(attended_ref[...], grad_one, FIRST)
        grad_attended = exact(grad_one, out_ref[...], LAST)
        projected = projected_ref[...]
        query, key, value = (projected[:, i * width : (i + 1) * width] for i in range(3))
        grads = [jnp.zeros((wave_count, width), f32) for _ in range(3)]
        for head in range(HHEADS):
            lanes = head_lanes(width, head_size, head)
            own = jnp.where(lanes, grad_attended, 0.0)
            probs = probs_ref[head]
            grad_probs = exact(own, value, LAST)
            grads[2] += exact(probs, own, FIRST)
            scores = probs * (grad_probs - jnp.sum(grad_probs * probs, axis=-1, keepdims=True))
            scores = scores * head_size ** (-0.5)
            grads[0] += exact(scores, jnp.where(lanes, key, 0.0))
            grads[1] += exact(scores, jnp.where(lanes, query, 0.0), FIRST)
        grad_projected = jnp.concatenate(grads, axis=1)
        in_out[...] = exact(table_ref[...], grad_projected, FIRST)
        table_out[...] = grad_one + exact(grad_projected, in_ref[...], LAST)

    arrays = [table, *weights, *gains]
    return local_call(
        kernel,
        where,
        [],
        [grad_mix, *arrays, *kept],
        [jax.ShapeDtypeStruct(a.shape, f32) for a in arrays],
        name="hyper_backward",
        flops=80 * wave_count * weights[2].size,
    )


def attention_forward(where, own, other, pos, gain, in_proj, out_proj):
    patches, half_width = own.shape
    width = 2 * half_width
    heads = half_width // HS

    def kernel(
        where_ref, own_ref, other_ref, pos_ref, gain_ref, in_ref, out_ref, tokens_out, normed_out,
        query_out, key_out, value_out, probs_out, attended_out, part_out,
    ):
        own_half, other_half = own_ref[...].astype(f32), other_ref[...].astype(f32)
        first = where_ref[1] == 0
        embed = jnp.concatenate(
            [jnp.where(first, own_half, other_half), jnp.where(first, other_half, own_half)], axis=1
        )
        tokens = embed + pos_ref[...].astype(f32)
        tokens_out[...] = tokens
        normal, _ = norm_parts(tokens)
        normed = (normal * gain_ref[...].astype(f32)).astype(bf16)
        normed_out[...] = normed
        projected = [low_dot(normed, in_ref[j]).astype(bf16) for j in range(3)]
        query_out[...], key_out[...], value_out[...] = projected
        for pair in range(heads // 2):
            lanes = slice(pair * 2 * HS, (pair + 1) * 2 * HS)
            query, key, value = (p[:, lanes] for p in projected)
            total = None
            for side in range(2):
                mine = head_lanes(2 * HS, HS, side)
                scores = contract_last(jnp.where(mine, query, 0), key) * score_scale
                scores = jnp.exp(scores - jnp.max(scores, axis=-1, keepdims=True))
                probs = scores / jnp.sum(scores, axis=-1, keepdims=True)
                probs_out[2 * pair + side] = probs
                part = low_dot(probs.astype(bf16), jnp.where(mine, value, 0))
                total = part if total is None else total + part
            attended_out[:, lanes] = total.astype(bf16)
        part_out[...] = low_dot(attended_out[...], out_ref[...]).astype(bf16)

    def low(*dims):
        return jax.ShapeDtypeStruct(dims, bf16)

    return local_call(
        kernel,
        where,
        [],
        [own, other, pos, gain, in_proj, out_proj],
        [
            jax.ShapeDtypeStruct((patches, width), f32),
            low(patches, width),
            low(patches, half_width),
            low(patches, half_width),
            low(patches, half_width),
            jax.ShapeDtypeStruct((heads, patches, patches), f32),
            low(patches, half_width),
            low(patches, width),
        ],
        name="attention_forward",
        flops=2 * patches * (in_proj.size + out_proj.size + 4 * patches * half_width),
    )


def feed_forward(where, tokens, own, other, gain, up, down, cotangent):
    patches, width = tokens.shape
    local = up.shape[1]
    tile = local // 3

    def kernel(
        where_ref, tokens_ref, own_ref, other_ref, gain_ref, up_ref, down_ref, cotangent_ref,
        mid_out, second_out, active_out, grad_hidden_out, parts_out,
    ):
        mid = tokens_ref[...] + (own_ref[...].astype(f32) + other_ref[...].astype(f32))
        mid_out[...] = mid
        normal, _ = norm_parts(mid)
        second = (normal * gain_ref[...].astype(f32)).astype(bf16)
        second_out[...] = second
        for t in range(3):
            columns = slice(t * tile, (t + 1) * tile)
            hidden = low_dot(second, up_ref[:, columns])
            factor, slope = gelu_parts(hidden)
            active_out[:, columns] = (hidden * factor).astype(bf16)
            grad_active = contract_last(cotangent_ref[...], down_ref[columns, :])
            grad_hidden_out[:, columns] = (grad_active * slope).astype(bf16)
        parts_out[:patches, :] = low_dot(active_out[...], down_ref[...]).astype(bf16)
        parts_out[PART : PART + patches, :] = contract_last(
            grad_hidden_out[...], up_ref[...]
        ).astype(bf16)

    return local_call(
        kernel,
        where,
        [],
        [tokens, own, other, gain, up, down, cotangent],
        [
            jax.ShapeDtypeStruct((patches, width), f32),
            jax.ShapeDtypeStruct((patches, width), bf16),
            jax.ShapeDtypeStruct((patches, local), bf16),
            jax.ShapeDtypeStruct((patches, local), bf16),
            jax.ShapeDtypeStruct((PART + patches, width), bf16),
        ],
        name="feed_forward",
        flops=8 * patches * up.size,
    )


def attention_backward(
    where, mid, own, other, cotangent, gain, in_proj, out_proj, query, key, value, probs
):
    patches, width = mid.shape
    half_width = width // 2
    heads = half_width // HS

    def kernel(
        where_ref, mid_ref, own_ref, other_ref, cotangent_ref, gain_ref, in_ref, out_ref,
        query_ref, key_ref, value_ref, probs_ref, layer_out, gain_out, grad_mid_out, low_out,
        query_out, key_out, value_out, part_out,
    ):
        mid_values = mid_ref[...]
        down = own_ref[:patches, :].astype(f32) + other_ref[:patches, :].astype(f32)
        layer_out[...] = (mid_values + down).astype(bf16)
        back = slice(PART, PART + patches)
        grad_second = own_ref[back, :].astype(f32) + other_ref[back, :].astype(f32)
        normal, scale = norm_parts(mid_values)
        gain_out[...] = jnp.sum(grad_second * normal, axis=0, keepdims=True)
        grad_mid = cotangent_ref[...].astype(f32) + norm_grad(
            grad_second * gain_ref[...].astype(f32), normal, scale
        )
        grad_mid_out[...] = grad_mid
        grad_low = grad_mid.astype(bf16)
        low_out[...] = grad_low
        grad_attended = contract_last(grad_low, out_ref[...]).astype(bf16)
        for pair in range(heads // 2):
            lanes = slice(pair * 2 * HS, (pair + 1) * 2 * HS)
            query, key, value = query_ref[:, lanes], key_ref[:, lanes], value_ref[:, lanes]
            totals = [None] * 3
            for side in range(2):
                mine = head_lanes(2 * HS, HS, side)
                own_grad = jnp.where(mine, grad_attended[:, lanes], 0)
                probs = probs_ref[2 * pair + side]
                grad_probs = contract_last(own_grad, value)
                inner = jnp.sum(grad_probs * probs, axis=-1, keepdims=True)
                scores = (probs * (grad_probs - inner)).astype(bf16)
                parts = (
                    low_dot(scores, jnp.where(mine, key, 0)),
                    contract_first(scores, jnp.where(mine, query, 0)),
                    contract_first(probs.astype(bf16), own_grad),
                )
                totals = [p if t is None else t + p for t, p in zip(totals, parts)]
            query_out[:, lanes] = (totals[0] * score_scale).astype(bf16)
            key_out[:, lanes] = (totals[1] * score_scale).astype(bf16)
            value_out[:, lanes] = totals[2].astype(bf16)
        part = contract_last(query_out[...], in_ref[0])
        part += contract_last(key_out[...], in_ref[1])
        part += contract_last(value_out[...], in_ref[2])
        part_out[...] = part.astype(bf16)

    def low(*dims):
        return jax.ShapeDtypeStruct(dims, bf16)

    return local_call(
        kernel,
        where,
        [],
        [mid, own, other, cotangent, gain, in_proj, out_proj, query, key, value, probs],
        [
            low(patches, width),
            jax.ShapeDtypeStruct((1, width), f32),
            jax.ShapeDtypeStruct((patches, width), f32),
            low(patches, width),
            low(patches, half_width),
            low(patches, half_width),
            low(patches, half_width),
            low(patches, width),
        ],
        name="attention_backward",
        flops=2 * patches * (in_proj.size + out_proj.size + 8 * patches * half_width),
    )


def token_grad(where, tokens, grad_mid, own, other, gain, gain_two_grad):
    patches, width = tokens.shape
    half_width = width // 2

    def kernel(
        where_ref, tokens_ref, grad_mid_ref, own_ref, other_ref, gain_ref, two_ref, half_out,
        small_out,
    ):
        grad_normed = own_ref[...].astype(f32) + other_ref[...].astype(f32)
        normal, scale = norm_parts(tokens_ref[...])
        grad_one = jnp.sum(grad_normed * normal, axis=0, keepdims=True)
        grad = grad_mid_ref[...] + norm_grad(
            grad_normed * gain_ref[...].astype(f32), normal, scale
        )
        low = grad.astype(bf16)
        half_out[...] = jnp.where(where_ref[1] == 0, low[:, :half_width], low[:, half_width:])
        small_out[...] = jnp.zeros_like(small_out)
        small_out[:patches, :] = low
        small_out[patches : patches + 1, :] = grad_one.astype(bf16)
        small_out[patches + 1 : patches + 2, :] = two_ref[...].astype(bf16)

    return local_call(
        kernel,
        where,
        [],
        [tokens, grad_mid, own, other, gain, gain_two_grad],
        [
            jax.ShapeDtypeStruct((patches, half_width), bf16),
            jax.ShapeDtypeStruct((EXTRA, width), bf16),
        ],
        name="token_grad",
    )


def wave_grads(ids_ref, blocks_ref, rows_ref, wave_count, piece):
    slots = ids_ref.shape[1]
    for s in range(slots):
        rows_ref[s * piece : (s + 1) * piece, :] = blocks_ref[s, :piece, :]
    onehot = onehot_of(ids_ref, wave_count)
    bits = 2**30 - 1
    shift = piece.bit_length() - 1
    tall = low_dot(
        equal_index(slots * piece, slots, shift, 0, bits, bits).astype(bf16), onehot.astype(bf16)
    ).astype(bf16)
    wide = low_dot(
        tall, equal_index(wave_count, wave_count * piece, 0, shift, bits, bits).astype(bf16)
    )
    same = equal_index(slots * piece, wave_count * piece, 0, 0, piece - 1, piece - 1)
    select = jnp.where(same, wide, 0.0).astype(bf16)
    kernels = contract_first(select, rows_ref[...]).astype(bf16)
    biases = jnp.concatenate(
        [
            blocks_ref[s, piece : piece + 1, :].astype(f32)
            + blocks_ref[s, piece + 1 : piece + 2, :].astype(f32)
            for s in range(slots)
        ],
        axis=0,
    )
    return kernels, exact(onehot.astype(f32), biases, FIRST)


def mix_grad(where, wave_ids, blocks, gen_rows, bias_gen, wave_count, count):
    width, half_width = bias_gen.shape
    piece = gen_rows.shape[0] // width

    def kernel(
        where_ref, ids_ref, blocks_ref, gen_ref, bias_ref, mix_out, kernels_out, biases_out, rows_ref
    ):
        kernels, biases = wave_grads(ids_ref, blocks_ref, rows_ref, wave_count, piece)
        kernels_out[...] = kernels
        biases_out[...] = biases
        products = contract_last(kernels, gen_ref[...])
        same = equal_index(*products.shape, 0, 0, piece - 1, piece - 1)
        products = jnp.where(same, products, 0.0)
        rows = jnp.sum(products.reshape(wave_count, piece, -1), axis=1)
        bits = 2**30 - 1
        gather = equal_index(
            width * piece, width, piece.bit_length() - 1, 0, bits, bits
        ).astype(f32)
        mix = exact(rows, gather)
        mix_out[...] = mix + exact(biases, bias_ref[...].astype(f32), LAST) * (1.0 / count)

    return local_call(
        kernel,
        where,
        [wave_ids],
        [blocks, gen_rows, bias_gen],
        [
            jax.ShapeDtypeStruct((wave_count, width), f32),
            jax.ShapeDtypeStruct((wave_count * piece, half_width), bf16),
            jax.ShapeDtypeStruct((wave_count, half_width), f32),
        ],
        scratch=[pltpu.VMEM((wave_ids.shape[1] * piece, half_width), bf16)],
        name="mix_grad",
        flops=2 * wave_count * piece * gen_rows.size,
    )


def generator_grads(where, mix_low, kernels, biases):
    wave_count, width = mix_low.shape
    piece = kernels.shape[0] // wave_count
    half_width = kernels.shape[1]

    def kernel(where_ref, mix_ref, kernels_ref, biases_ref, gen_out, bias_out):
        mix = mix_ref[...]
        gen_out[...] = contract_first(kron_identity(mix, piece), kernels_ref[...])
        bias_out[...] = exact(mix.astype(f32), biases_ref[...], FIRST)

    return local_call(
        kernel,
        where,
        [],
        [mix_low, kernels, biases],
        [
            jax.ShapeDtypeStruct((width * piece, half_width), f32),
            jax.ShapeDtypeStruct((width, half_width), f32),
        ],
        name="generator_grads",
        flops=2 * wave_count * piece * width * piece * half_width,
    )


def embed_part(upper, orders, where, mask, pixels, kernels):
    images, patches, pixel_count = pixels.shape
    half = images // 2

    def kernel(where_ref, mask_ref, pixel_ref, kernel_ref, *outs):
        band = where_ref[0]

        def body(q):
            for c, order in enumerate(orders):
                image = band ^ relative_index(q + half * upper, order)
                scale = mask_ref[image, band].astype(f32)
                product = jnp.dot(
                    pixel_ref[image], kernel_ref[:, span(c)], preferred_element_type=f32
                )
                outs[c][q] = (product * scale).astype(bf16)

        loop(half, body)

    return local_call(
        kernel,
        where,
        [mask],
        [pixels, kernels],
        [jax.ShapeDtypeStruct((half, patches, LANES), bf16)] * 3,
        name="embed_part",
        flops=images * patches * pixel_count * 3 * LANES,
    )


def kernel_grad(upper, orders, where, mask, pixels, grads, total, bias):
    images, patches, pixel_count = pixels.shape
    half = images // 2
    piece = pixel_count // images
    width = 3 * LANES

    def kernel(where_ref, mask_ref, pixel_ref, *refs):
        band = where_ref[0]
        grad_refs = refs[:3]
        if upper:
            old_total, old_bias, out_ref, total_ref, bias_ref = refs[3:]
            total_ref[...] = old_total[...]
            bias_ref[...] = old_bias[...]
        else:
            total_ref, bias_ref = refs[3:]
            total_ref[...] = jnp.zeros_like(total_ref)
            bias_ref[...] = jnp.zeros_like(bias_ref)

        def body(q):
            for c, order in enumerate(orders):
                image = band ^ relative_index(q + half * upper, order)

                @pl.when(mask_ref[image, band] != 0)
                def _(c=c, image=image):
                    grad = grad_refs[c][q]
                    total_ref[span(c), :] += contract_first(grad, pixel_ref[image])
                    bias_ref[:, span(c)] += jnp.sum(grad.astype(f32), axis=0, keepdims=True)

        loop(half, body)
        if upper:
            high = bias_ref[...].astype(bf16)
            low = (bias_ref[...] - high.astype(f32)).astype(bf16)
            whole = total_ref[...].T.astype(bf16)
            for k in range(images):
                out_ref[k, :piece, :] = whole[k * piece : (k + 1) * piece]
                out_ref[k, piece : piece + 1, :] = high
                out_ref[k, piece + 1 : piece + 2, :] = low

    accumulators = [
        jax.ShapeDtypeStruct((width, pixel_count), f32),
        jax.ShapeDtypeStruct((1, width), f32),
    ]
    flops = images * patches * pixel_count * width
    if not upper:
        return local_call(
            kernel, where, [mask], [pixels, *grads], accumulators, name="kernel_grad", flops=flops
        )
    return local_call(
        kernel,
        where,
        [mask],
        [pixels, *grads, total, bias],
        [jax.ShapeDtypeStruct((images, piece + 2, width), bf16)],
        scratch=[pltpu.VMEM(s.shape, f32) for s in accumulators],
        name="kernel_grad_end",
        flops=flops,
    )[0]


def pixel_grad(orders, where, mask, early, late, kernels):
    half, patches, _ = early[0].shape
    pixel_count = kernels.shape[0]

    def kernel(where_ref, mask_ref, *refs):
        early_refs, late_refs, kernel_ref, outs = refs[:3], refs[3:6], refs[6], refs[7:]
        band, head = where_ref[0], where_ref[1]

        def body(q):
            for side in range(2):
                first = head if side == 0 else 1 - head
                image = first * half + q
                parts = []
                for c, order in enumerate(orders):
                    position = position_of(image ^ band, order)
                    low = jnp.minimum(position, half - 1)
                    high = jnp.maximum(position - half, 0)
                    parts.append(
                        jnp.where(position < half, early_refs[c][low], late_refs[c][high])
                    )
                total = contract_last(jnp.concatenate(parts, axis=1), kernel_ref[...])
                outs[side][q] = (total * mask_ref[image, band].astype(f32)).astype(bf16)

        loop(half, body)

    return local_call(
        kernel,
        where,
        [mask],
        [*early, *late, kernels],
        [jax.ShapeDtypeStruct((half, patches, pixel_count), bf16)] * 2,
        name="pixel_grad",
        flops=4 * half * patches * pixel_count * 3 * LANES,
    )


def row_products(orders, count, where, lefts, rights, portions, name):
    rows = lefts[0].shape[1] // count
    half = count // 2 * rows
    widths = [sum(piece[3] for piece in portion) for portion in portions]
    if rows % 16:
        keeps, sends = [], []
        for portion, order in zip(portions, orders):
            places = jnp.asarray([relative_index(p, order) for p in range(count)], jnp.int32)
            columns = ((where[0] ^ places) * rows)[:, None] + jnp.arange(rows, dtype=jnp.int32)
            select = jnp.arange(count * rows, dtype=jnp.int32)[:, None] == columns.reshape(1, -1)
            turned = [jnp.dot(left, select.astype(bf16)) for left in lefts]
            whole = jnp.concatenate(
                [contract_first(turned[i], rights[j][:, s : s + w]) for i, j, s, w in portion],
                axis=1,
            ).astype(bf16)
            keeps.append(whole[:half])
            sends.append(whole[half:])
        return keeps, sends
    uses = sorted({(piece[0], c) for c, portion in enumerate(portions) for piece in portion})

    def kernel(where_ref, *refs):
        left_refs = refs[: len(lefts)]
        right_refs = refs[len(lefts) : len(lefts) + len(rights)]
        outs = refs[len(lefts) + len(rights) : len(lefts) + len(rights) + 6]
        turned_refs = refs[len(lefts) + len(rights) + 6 : -len(uses) - 7]
        ordered = dict(zip(uses, refs[-len(uses) - 7 : -7]))
        made, sems = refs[-7:-1], refs[-1]
        band = where_ref[0]
        for left_ref, turned_ref in zip(left_refs, turned_refs):
            turned_ref[...] = left_ref[...].T
        for (i, c), ordered_ref in ordered.items():
            for p in range(count):
                block = (band ^ relative_index(p, orders[c])) * rows
                ordered_ref[p * rows : (p + 1) * rows, :] = turned_refs[i][
                    pl.ds(pl.multiple_of(block, 16), rows), :
                ]
        copies = []
        for side in (1, 0):
            for c, portion in enumerate(portions):
                place = 0
                slot = 3 - 3 * side + c
                for i, j, start, width in portion:
                    left = ordered[i, c][side * half : (side + 1) * half, :]
                    for column in range(0, width, 256):
                        wide = min(256, width - column)
                        made[slot][:, place : place + wide] = jnp.dot(
                            left,
                            right_refs[j][:, start + column : start + column + wide],
                            preferred_element_type=f32,
                        ).astype(bf16)
                        place += wide
                copies.append(pltpu.make_async_copy(made[slot], outs[slot], sems.at[slot]))
                copies[-1].start()
        for copy in copies:
            copy.wait()

    shapes = [jax.ShapeDtypeStruct((half, width), bf16) for width in widths] * 2
    turned = [pltpu.VMEM((left.shape[1], left.shape[0]), bf16) for left in lefts]
    ordered = [pltpu.VMEM((lefts[i].shape[1], lefts[i].shape[0]), bf16) for i, _ in uses]
    outs = local_call(
        kernel,
        where,
        [],
        [*lefts, *rights],
        shapes,
        scratch=turned
        + ordered
        + [pltpu.VMEM(shape.shape, bf16) for shape in shapes]
        + [pltpu.SemaphoreType.DMA((6,))],
        spaces=[HBM] * 6,
        name=name,
        flops=2 * lefts[0].size * sum(widths),
        mebibytes=32,
    )
    return outs[3:], outs[:3]


def half_sum(where, keeps, arriving, last):
    half = keeps[0].shape[0] // 2
    widths = [keep.shape[1] for keep in keeps]

    def kernel(where_ref, *refs):
        keep_refs, arriving_refs = refs[:3], refs[3:6]
        sends, kept = (refs[6:7], refs[7:8]) if last else (refs[6:9], refs[9:12])
        place = 0
        for c in range(3):
            total = keep_refs[c][...].astype(f32) + arriving_refs[c][...].astype(f32)
            at = slice(place, place + widths[c]) if last else slice(None)
            out = 0 if last else c
            kept[out][:, at] = total[:half]
            sends[out][:, at] = total[half:].astype(bf16)
            place += widths[c]

    shapes = [(half, sum(widths))] if last else [(half, width) for width in widths]
    outs = local_call(
        kernel,
        where,
        [],
        [*keeps, *arriving],
        [jax.ShapeDtypeStruct(shape, bf16) for shape in shapes]
        + [jax.ShapeDtypeStruct(shape, f32) for shape in shapes],
        name="half_sum",
    )
    return outs[: len(shapes)], outs[len(shapes) :]


def final_sum(where, kept, arriving, ff_local, half_width, patches):
    rows = kept.shape[0]

    def kernel(
        where_ref, kept_ref, arriving_ref, up_out, down_out, in_out, out_out, pos_out, one_out,
        two_out,
    ):
        total = kept_ref[...] + arriving_ref[...].astype(f32)
        side = ff_local + EXTRA // 2
        up_out[...] = total[:, :ff_local]
        down_out[...] = total[:, side : side + ff_local]
        for k in range(3):
            in_out[k] = total[:, 2 * side + k * half_width : 2 * side + (k + 1) * half_width]
        out_out[...] = total[:, 2 * side + 3 * half_width :]
        extra = jnp.concatenate(
            [total[:, ff_local:side], total[:, side + ff_local : 2 * side]], axis=1
        )
        pos_out[...] = extra[:, :patches]
        extra = extra.T
        one_out[...] = extra[patches : patches + 1]
        two_out[...] = extra[patches + 1 : patches + 2]

    def shape(*dims):
        return jax.ShapeDtypeStruct(dims, f32)

    return local_call(
        kernel,
        where,
        [],
        [kept, arriving],
        [
            shape(rows, ff_local),
            shape(rows, ff_local),
            shape(3, rows, half_width),
            shape(rows, half_width),
            shape(rows, patches),
            shape(1, rows),
            shape(1, rows),
        ],
        name="final_sum",
    )


STEPS = (1, 2, 4, 8)
XY, YX, ZX, ZY = (8, 4, 2, 1), (8, 4, 1, 2), (8, 2, 1, 4), (8, 1, 2, 4)
XZ, YZ = (8, 2, 4, 1), (8, 1, 4, 2)


def product_scratch(lefts, uses):
    return [pltpu.VMEM((left.shape[1], left.shape[0]), bf16) for left in lefts] + [
        pltpu.VMEM((lefts[i].shape[1], lefts[i].shape[0]), bf16) for i, _ in uses
    ]


def order_rows(band, left_refs, turned_refs, ordered, positions):
    rows = left_refs[0].shape[1] // 16
    for left_ref, turned_ref in zip(left_refs, turned_refs):
        turned_ref[...] = left_ref[...].T
    for (i, order), ordered_ref in ordered.items():
        for p in positions:
            block = (band ^ relative_index(p, order)) * rows
            ordered_ref[p * rows : (p + 1) * rows, :] = turned_refs[i][
                pl.ds(pl.multiple_of(block, 16), rows), :
            ]


def product_tiles(left, right_refs, portion, ordered, order, rows):
    place = 0
    for i, j, start, width in portion:
        for column in range(0, width, 256):
            wide = min(256, width - column)
            yield (
                place,
                wide,
                jnp.dot(
                    ordered[i, order][rows, :],
                    right_refs[j][:, start + column : start + column + wide],
                    preferred_element_type=f32,
                ).astype(bf16),
            )
            place += wide


def early_products(where, lefts, rights, portions, orders):
    uses = sorted({(piece[0], order) for portion, order in zip(portions, orders) for piece in portion})
    half = lefts[0].shape[1] // 2
    widths = [sum(piece[3] for piece in portion) for portion in portions]
    n = len(lefts) + len(rights)

    def kernel(where_ref, *refs):
        left_refs, right_refs = refs[: len(lefts)], refs[len(lefts) : n]
        outs, scratch = refs[n : n + len(portions)], refs[n + len(portions) :]
        ordered = dict(zip(uses, scratch[len(lefts) :]))
        order_rows(where_ref[0], left_refs, scratch[: len(lefts)], ordered, range(8, 16))
        for out, portion, order in zip(outs, portions, orders):
            tiles = product_tiles(
                None, right_refs, portion, ordered, order, slice(half, 2 * half)
            )
            for place, wide, product in tiles:
                out[:, place : place + wide] = product

    return local_call(
        kernel,
        where,
        [],
        [*lefts, *rights],
        [jax.ShapeDtypeStruct((half, width), bf16) for width in widths],
        scratch=product_scratch(lefts, uses),
        name="early_products",
        flops=lefts[0].size * sum(widths),
    )


def round_products(where, lefts, rights, early, early_orders, portions, orders):
    early_of = {0: 1, 1: 0}
    groups = [(0, 1), (2, 3), (4, 5)]
    uses = sorted(
        {
            (piece[0], order)
            for portion, order in zip([*early, *portions], [*early_orders, *orders])
            for piece in portion
        }
    )
    quarter = lefts[0].shape[1] // 4
    early_width = sum(piece[3] for piece in early[0])
    widths = [sum(piece[3] for piece in portion) for portion in portions]
    shapes = []
    for g, group in enumerate(groups):
        width = 2 * sum(widths[c] for c in group) + (early_width if g in early_of else 0)
        shapes.append(jax.ShapeDtypeStruct((quarter, width), bf16))
    n = len(lefts) + len(rights)

    def kernel(where_ref, *refs):
        left_refs, right_refs = refs[: len(lefts)], refs[len(lefts) : n]
        outs, made, sems = refs[n : n + 6], refs[-7:-1], refs[-1]
        scratch = refs[n + 6 : -7]
        ordered = dict(zip(uses, scratch[len(lefts) :]))
        order_rows(where_ref[0], left_refs, scratch[: len(lefts)], ordered, range(16))
        copies = []
        for side in (1, 0):
            for g, group in enumerate(groups):
                slot = 3 * (1 - side) + g
                base = 0
                if g in early_of:
                    e = early_of[g]
                    rows = slice(side * quarter, (side + 1) * quarter)
                    tiles = product_tiles(
                        None, right_refs, early[e], ordered, early_orders[e], rows
                    )
                    for place, wide, product in tiles:
                        made[slot][:, place : place + wide] = product
                    base = early_width
                for c in group:
                    rows = slice(side * 2 * quarter, (side + 1) * 2 * quarter)
                    tiles = product_tiles(None, right_refs, portions[c], ordered, orders[c], rows)
                    for place, wide, product in tiles:
                        for k in range(2):
                            at = base + k * widths[c] + place
                            made[slot][:, at : at + wide] = product[k * quarter : (k + 1) * quarter]
                    base += 2 * widths[c]
                copies.append(pltpu.make_async_copy(made[slot], outs[slot], sems.at[slot]))
                copies[-1].start()
        for copy in copies:
            copy.wait()

    outs = local_call(
        kernel,
        where,
        [],
        [*lefts, *rights],
        shapes * 2,
        scratch=product_scratch(lefts, uses)
        + [pltpu.VMEM(shape.shape, bf16) for shape in shapes * 2]
        + [pltpu.SemaphoreType.DMA((6,))],
        spaces=[HBM] * 6,
        name="round_products",
        flops=2 * lefts[0].size * sum(widths) + lefts[0].size * early_width,
        mebibytes=32,
    )
    return outs[:3], outs[3:]


def early_sum(where, sends, keeps, arriving):
    quarter = sends[0].shape[0]
    width = arriving[0].shape[1]
    buffers = [sends[0], keeps[0], sends[1], keeps[1]]

    def kernel(where_ref, *refs):
        arriving_refs, outs, parts, sems = refs[4:6], refs[6:10], refs[10], refs[11]
        loads = []
        for k in range(4):
            loads.append(
                pltpu.make_async_copy(refs[k].at[:, pl.ds(0, width)], parts.at[k], sems.at[k])
            )
            loads[-1].start()
        stores = []
        for k in range(4):
            loads[k].wait()
            rows = slice(quarter, 2 * quarter) if k % 2 == 0 else slice(0, quarter)
            added = arriving_refs[1 - k // 2][rows, :].astype(f32)
            parts[k] = (parts[k].astype(f32) + added).astype(bf16)
            stores.append(
                pltpu.make_async_copy(parts.at[k], outs[k].at[:, pl.ds(0, width)], sems.at[4 + k])
            )
            stores[-1].start()
        for store in stores:
            store.wait()

    smem = pl.BlockSpec(memory_space=pltpu.SMEM)
    outs = pl.pallas_call(
        kernel,
        in_specs=[smem]
        + [pl.BlockSpec(memory_space=HBM)] * 4
        + [pl.BlockSpec(memory_space=pltpu.VMEM)] * 2,
        out_specs=[pl.BlockSpec(memory_space=HBM)] * 4,
        out_shape=[jax.ShapeDtypeStruct(b.shape, bf16) for b in buffers],
        input_output_aliases={1: 0, 2: 1, 3: 2, 4: 3},
        scratch_shapes=[
            pltpu.VMEM((4, quarter, width), bf16),
            pltpu.SemaphoreType.DMA((8,)),
        ],
        compiler_params=pltpu.CompilerParams(vmem_limit_bytes=24 * 2**20),
        name="early_sum",
    )(where, *buffers, *arriving)
    return [outs[0], outs[2], sends[2]], [outs[1], outs[3], keeps[2]]


def second_sum(where, keeps, arriving, early_width, widths):
    quarter = keeps[0].shape[0]
    pair = quarter // 2
    starts = [early_width, early_width + 2 * widths[0]] + [0] * 4
    starts[2:4] = [early_width, early_width + 2 * widths[2]]
    starts[4:] = [0, 2 * widths[4]]
    rounds = [(0, (0, 5)), (0, (2, 4)), (2 * early_width, (1, 3))]

    def kernel(where_ref, *refs):
        keep_refs, arriving_refs = refs[:3], refs[3:6]
        sends, kept = refs[6:9], refs[9:]
        totals = [k[...].astype(f32) + a[...].astype(f32) for k, a in zip(keep_refs, arriving_refs)]
        for e, g in ((0, 1), (1, 0)):
            at = slice(e * early_width, (e + 1) * early_width)
            kept[2][:, at] = totals[g][:pair, :early_width]
            sends[2][:, at] = totals[g][pair:, :early_width].astype(bf16)
        for (place, group), keep, send in zip(rounds, kept, sends):
            for c in group:
                total, start, width = totals[c // 2], starts[c], widths[c]
                for k in range(2):
                    rows = slice(k * pair, (k + 1) * pair)
                    at = slice(place + k * width, place + (k + 1) * width)
                    keep[:, at] = total[rows, start : start + width]
                    send[:, at] = total[rows, start + width : start + 2 * width].astype(bf16)
                place += 2 * width

    shapes = [(pair, place + 2 * sum(widths[c] for c in group)) for place, group in rounds]
    outs = local_call(
        kernel,
        where,
        [],
        [*keeps, *arriving],
        [jax.ShapeDtypeStruct(shape, bf16) for shape in shapes]
        + [jax.ShapeDtypeStruct(shape, f32) for shape in shapes],
        name="second_sum",
    )
    return outs[:3], outs[3:]


def third_sum(where, keeps, arriving, early_width, widths):
    pair = keeps[0].shape[0]
    rows = pair // 2
    place_in = {0: (0, 0), 5: (0, 2 * widths[0]), 2: (1, 0), 4: (1, 2 * widths[2])}
    place_in[1] = (2, 2 * early_width)
    place_in[3] = (2, 2 * early_width + 2 * widths[1])
    rounds = [(0, 2), (4, 1), (5, 3)]

    def kernel(where_ref, *refs):
        keep_refs, arriving_refs = refs[:3], refs[3:6]
        sends, kept = refs[6:10], refs[10:]
        totals = [k[...] + a[...].astype(f32) for k, a in zip(keep_refs, arriving_refs)]
        kept[0][...] = totals[2][:rows, : 2 * early_width]
        sends[0][...] = totals[2][rows:, : 2 * early_width].astype(bf16)
        for group, keep, send in zip(rounds, kept[1:], sends[1:]):
            place = 0
            for c in group:
                (g, start), width = place_in[c], widths[c]
                at = slice(place, place + width)
                keep[:, at] = totals[g][:, start : start + width]
                send[:, at] = totals[g][:, start + width : start + 2 * width].astype(bf16)
                place += width

    shapes = [(rows, 2 * early_width)] + [
        (pair, sum(widths[c] for c in group)) for group in rounds
    ]
    outs = local_call(
        kernel,
        where,
        [],
        [*keeps, *arriving],
        [jax.ShapeDtypeStruct(shape, bf16) for shape in shapes]
        + [jax.ShapeDtypeStruct(shape, f32) for shape in shapes],
        name="third_sum",
    )
    return outs[:4], outs[4:]


def fourth_sum(where, keeps, arriving):
    rows = keeps[0].shape[0] // 2
    widths = [keep.shape[1] for keep in keeps]

    def kernel(where_ref, *refs):
        send, kept = refs[6:]
        place = 0
        for keep, arrived, width in zip(refs[:3], refs[3:6], widths):
            total = keep[...] + arrived[...].astype(f32)
            kept[:, place : place + width] = total[:rows]
            send[:, place : place + width] = total[rows:].astype(bf16)
            place += width

    return local_call(
        kernel,
        where,
        [],
        [*keeps, *arriving],
        [
            jax.ShapeDtypeStruct((rows, sum(widths)), bf16),
            jax.ShapeDtypeStruct((rows, sum(widths)), f32),
        ],
        name="fourth_sum",
    )


def last_sum(where, early, early_arriving, kept, arriving, ff_local, half_width, patches):
    rows = kept.shape[0]
    early_width = early.shape[1] // 2
    rest = ff_local - early_width

    def kernel(
        where_ref, early_ref, early_arriving_ref, kept_ref, arriving_ref, up_out, down_out, in_out,
        out_out, pos_out, one_out, two_out,
    ):
        first = early_ref[...] + early_arriving_ref[...].astype(f32)
        total = kept_ref[...] + arriving_ref[...].astype(f32)
        up_out[:, :early_width] = first[:, :early_width]
        down_out[:, :early_width] = first[:, early_width:]
        up_out[:, early_width:] = total[:, :rest]
        down_out[:, early_width:] = total[:, rest : 2 * rest]
        at = 2 * rest
        in_out[1, :, half_width - 256 :] = total[:, at : at + 256]
        in_out[2] = total[:, at + 256 : at + 256 + half_width]
        at += 256 + half_width
        in_out[0, :, :256] = total[:, at : at + 256]
        at += 256
        out_out[...] = total[:, at : at + half_width]
        extra = total[:, at + half_width : at + half_width + EXTRA].T
        b = at + half_width + EXTRA
        in_out[0, :, 256:] = total[:, b : b + half_width - 256]
        in_out[1, :, : half_width - 256] = total[:, b + half_width - 256 :]
        pos_out[...] = total[:, at + half_width : at + half_width + patches]
        one_out[...] = extra[patches : patches + 1]
        two_out[...] = extra[patches + 1 : patches + 2]

    def shape(*dims):
        return jax.ShapeDtypeStruct(dims, f32)

    return local_call(
        kernel,
        where,
        [],
        [early, early_arriving, kept, arriving],
        [
            shape(rows, ff_local),
            shape(rows, ff_local),
            shape(3, rows, half_width),
            shape(rows, half_width),
            shape(rows, patches),
            shape(1, rows),
            shape(1, rows),
        ],
        name="last_sum",
    )


def in_hbm(arrays):
    return [pltpu.with_memory_space_constraint(array, pltpu.HBM) for array in arrays]


def after(values, *others):
    return lax.optimization_barrier((values, others))[0]


def shards(
    pixels,
    band_mask,
    wave_ids,
    pos_embed,
    in_proj,
    out_proj,
    up_proj,
    down_proj,
    gain_one,
    gain_two,
    kernel_gen,
    bias_gen,
    wave_table,
    hyper_in,
    hyper_out,
    hyper_up,
    hyper_down,
    hyper_gain_one,
    hyper_gain_two,
    cotangent,
):
    band_index = lax.axis_index("band")
    head_index = lax.axis_index("head")
    count = lax.axis_size("band")
    images, slot_local, patches, pixel_count = pixels.shape
    model_width = in_proj.shape[1]
    half_width = in_proj.shape[2]
    wave_count, hyper_width = wave_table.shape
    assert images == count and slot_local == 1
    orders = gather_orders(count)
    where = jnp.stack([band_index, head_index]).astype(jnp.int32)
    pixels = pixels.reshape(images, patches, pixel_count)
    wave_ids = wave_ids.reshape(1, -1)

    gen_rows = kernel_gen.reshape(-1, half_width)
    hyper_weights = [hyper_in, hyper_out, hyper_up, hyper_down]
    hyper_gains = [hyper_gain_one[None], hyper_gain_two[None]]
    slot_piece, image_bias, mix_low, *hyper_kept = hyper_forward(
        where,
        wave_ids,
        band_mask,
        wave_table,
        hyper_weights,
        hyper_gains,
        gen_rows,
        bias_gen,
        count,
    )
    slot_piece = slot_piece.reshape(count, -1, half_width)
    kernels = lax.all_to_all(slot_piece, "band", 0, 0, tiled=True).reshape(pixel_count, half_width)

    sends = embed_part(1, orders, where, band_mask, pixels, kernels)
    arriving = [hop(send, order[-1]) for send, order in zip(sends, orders)]
    keeps = embed_part(0, orders, where, band_mask, pixels, kernels)
    embed_half = jnp.concatenate(
        [part[0] for part in scatter_sum(keeps, None, orders, arriving)], axis=1
    )
    own_bias = lax.dynamic_slice_in_dim(image_bias, band_index, 1, 0)
    embed_low = (embed_half + own_bias).astype(bf16)
    gain_one = gain_one[None]
    gain_two = gain_two[None]
    tokens, normed_low, query, key, value, probs, attended, attn_part = attention_forward(
        where,
        embed_low,
        swap(embed_low),
        pltpu.with_memory_space_constraint(pos_embed, pltpu.HBM),
        gain_one,
        in_proj,
        out_proj,
    )
    grad_low = cotangent[0]
    mid_stream, second_low, active_low, grad_hidden, ff_parts = feed_forward(
        where,
        tokens,
        attn_part,
        swap(attn_part),
        gain_two,
        up_proj,
        pltpu.with_memory_space_constraint(down_proj, pltpu.HBM),
        grad_low,
    )
    ff_other = swap(ff_parts)

    ff_local = up_proj.shape[1]
    staged = count == 16
    if staged:
        early_width = EARLY
        ff_early = [[(0, 0, 0, early_width)], [(1, 1, 0, early_width)]]
        early_sends = early_products(
            where, [second_low, grad_low], [grad_hidden, active_low], ff_early, [XY, YX]
        )
        early_sends, ff_other = lax.optimization_barrier((early_sends, ff_other))
        early_arriving = [hop(send, step) for send, step in zip(early_sends, STEPS)]

    layer_out, gain_two_grad, grad_mid, grad_mid_low, *grad_projected, normed_part = (
        attention_backward(
            where,
            mid_stream,
            ff_parts,
            ff_other,
            grad_low,
            gain_two,
            in_proj,
            out_proj,
            query,
            key,
            value,
            probs,
        )
    )
    grad_embed_half, small = token_grad(
        where, tokens, grad_mid, normed_part, swap(normed_part), gain_one, gain_two_grad
    )

    first = hop(grad_embed_half, orders[0][0])
    lefts = [second_low, grad_low, normed_low, grad_mid_low, small]
    rights = [grad_hidden, active_low, *grad_projected, attended, jnp.eye(EXTRA, dtype=bf16)]
    side = EXTRA // 2
    if staged:
        portions = [
            [(0, 0, early_width, ff_local - early_width)],
            [(2, 2, 0, 256)],
            [(1, 1, early_width, ff_local - early_width)],
            [(2, 2, 256, half_width - 256), (2, 3, 0, half_width - 256)],
            [(2, 3, half_width - 256, 256), (2, 4, 0, half_width)],
            [(3, 5, 0, half_width), (4, 6, 0, EXTRA)],
        ]
        widths = [sum(piece[3] for piece in portion) for portion in portions]
        sends, keeps = round_products(
            where, lefts, rights, ff_early, [XY, YX], portions, [XY, XZ, YX, YZ, ZX, ZY]
        )
        first = after(first, (sends, early_arriving))
    else:
        portions = [
            [(0, 0, 0, ff_local), (4, 6, 0, side)],
            [(1, 1, 0, ff_local), (4, 6, side, side)],
            [(2, 2 + k, 0, half_width) for k in range(3)] + [(3, 5, 0, half_width)],
        ]
        keeps, sends = row_products(orders, count, where, lefts, rights, portions, "weight_grads")
        first = after(first, sends)
    early, late = [], []
    for c, order in enumerate(orders):
        block = jnp.stack([grad_embed_half[:, span(c)], first[:, span(c)]])
        for step in order[1:-1]:
            block = jnp.concatenate([block, hop(block, step)], axis=0)
        early.append(block)
        late.append(hop(block, order[-1]))
    total, bias = kernel_grad(0, orders, where, band_mask, pixels, early, None, None)
    if staged:
        sends, keeps = early_sum(where, sends, keeps, after(early_arriving, early))
    sends, late, total = lax.optimization_barrier((sends, late, total))
    if staged:
        arriving = [hop(send, step) for send, step in zip(sends, STEPS)]
    else:
        arriving = [hop(send, order[-1]) for send, order in zip(sends, orders)]
    own_pixels, other_pixels = pixel_grad(orders, where, band_mask, early, late, kernels)
    blocks = kernel_grad(1, orders, where, band_mask, pixels, late, total, bias)
    blocks = after(blocks, own_pixels)
    spread_blocks = lax.all_to_all(blocks, "band", 0, 0, tiled=True)
    grad_pixels = (own_pixels.astype(f32) + swap(other_pixels).astype(f32)).astype(bf16)
    grad_pixels = grad_pixels[:, None]
    steps = len(orders[0])
    mixing = count // 2
    arriving = after(arriving, (spread_blocks, own_pixels))
    for t in range(steps - 1):
        last = t == steps - 2
        if not staged:
            sends, keeps = half_sum(where, keeps, arriving, last)
            if last:
                arriving = hop(sends[0], orders[0][0])
            else:
                arriving = [hop(send, order[-2 - t]) for send, order in zip(sends, orders)]
        elif t == 0:
            sends, keeps = second_sum(where, in_hbm(keeps), arriving, early_width, widths)
            arriving = [hop(send, step) for send, step in zip(sends, (2, 1, 4))]
        elif t == 1:
            sends, keeps = third_sum(where, keeps, arriving, early_width, widths)
            early_last, *arriving = [hop(send, step) for send, step in zip(sends, (8, 4, 2, 1))]
            early_kept, *keeps = keeps
        else:
            sends, keeps = fourth_sum(where, keeps, arriving)
            arriving = hop(sends, 8)
        if t == 0:
            grad_mix, wave_kernels, wave_biases = mix_grad(
                where, wave_ids, after(spread_blocks, sends), gen_rows, bias_gen, wave_count, count
            )
            grad_mix = grad_mix + swap(grad_mix)
        else:
            grad_mix = after(grad_mix, sends)
        while mixing and (t >= 2 or mixing > count // 8):
            grad_mix = grad_mix + hop(grad_mix, mixing)
            mixing //= 2
        if not last:
            arriving = after(arriving, grad_mix)
    hyper_grads = hyper_backward(
        where, grad_mix, wave_table, hyper_weights, hyper_gains, hyper_kept
    )
    grad_kernel_gen, grad_bias_gen = generator_grads(where, mix_low, wave_kernels, wave_biases)
    if staged:
        sums = last_sum(
            where, early_kept, early_last, keeps, arriving, ff_local, half_width, patches
        )
    else:
        sums = final_sum(where, keeps[0], arriving, ff_local, half_width, patches)
    grad_up, grad_down, grad_in_proj, grad_out_proj, grad_pos, *grad_gains = sums
    return (
        layer_out[None],
        grad_pixels,
        grad_pos.T,
        grad_in_proj,
        grad_out_proj.T,
        grad_up,
        grad_down.T,
        grad_gains[0][0],
        grad_gains[1][0],
        grad_kernel_gen.reshape(kernel_gen.shape),
        grad_bias_gen,
        *hyper_grads[:5],
        hyper_grads[5][0],
        hyper_grads[6][0],
    )


def solution(mesh):
    in_specs = (
        P(None, "band", None, None),
        P(),
        P(),
        P(),
        P(None, None, "head"),
        P("head", None),
        P(None, "head"),
        P("head", None),
        P(),
        P(),
        P(None, "band", "head"),
        P(None, "head"),
        P(),
        P(),
        P(),
        P(),
        P(),
        P(),
        P(),
        P("band", None, None),
    )
    out_specs = (
        P("band", None, None),
        P("head", "band", None, None),
        P(None, "band"),
        P(None, "band", "head"),
        P("head", "band"),
        P("band", "head"),
        P("head", "band"),
        P("band"),
        P("band"),
        P(None, "band", "head"),
        P(None, "head"),
        P(),
        P(),
        P(),
        P(),
        P(),
        P(),
        P(),
    )
    return jax.shard_map(shards, mesh=mesh, in_specs=in_specs, out_specs=out_specs, check_vma=False)
```
